32 devices in a mesh: row: 4 (over x, core), tile: 8 (over z, y).
Axes of the slice: x: 2, y: 2, z: 4, core: 2. Of those that a mesh axis runs over, the one named last changes fastest.
Arguments:
- currents: bfloat16 [2, 4, 2, 128, 8192], P(None, None, None, ('row', 'tile')), may hold values from -6 to 6
- row_angles: int32 [2048], replicated, may hold values from 0 to 32767
- column_angles: int32 [2048], replicated, may hold values from 0 to 32767
- target: float32 [2, 2048, 2048], P(None, 'tile', 'row'), may hold values from 2 to 14
- weight: float32 [2, 2048, 2048], P(None, 'tile', 'row'), may hold values from 0.01 to 0.1
- tile_owner: int32 [8192, 1], P(('row', 'tile')), may hold values from 0 to 31; in each aligned block of 256 rows (0 to 255, 256 to 511, ...) at most 16 rows name the same one
- face_slot: int32 [8192], P(('row', 'tile')), may hold values from 0 to 255
Outputs:
- intensity: float32 [2, 2048, 2048], P(None, 'tile', 'row')
- faces: float32 [2, 4, 2, 8192, 128], P(None, None, None, ('row', 'tile'))
The draws below stay inside these ranges and needn't reach their ends.
Inputs may be any that keep to these rules, and one draw needn't show every extreme that they name: `tile_owner`: among the 256 segments of one device no owner is named more than 16 times, a bound that some block reaches.
All inputs are finite; a program needn't handle non-finite values.
Results may differ from the reference program's by a relative error of at most 0.0085.
Values may be sent and summed in bfloat16 or wider, within the bound.
No kernel may reach another device: no remote copies, remote signals or barrier semaphores. Data moves between devices by JAX's collectives and lax.ppermute only.
A program may use at most 128 MiB of HBM per device.

```python
import math
import jax
import jax.numpy as jnp
import numpy as np
from jax import lax

NY = 8192
U = 2048
V = 2048
NF = 2
SEG = 128
PX = 128
SEGS_DEV = 256
SEGS = 8192
FACES_DEV = 256
CAP = 16
N_ROW = 4
N_TILE = 8


def plant(drawn, key, least, high):
    shape = drawn.shape
    index_at = [jax.random.randint(jax.random.fold_in(key, axis), (), 0, shape[axis]) for axis in range(len(shape))]
    drawn = drawn.at[tuple(index_at)].set(least)
    longest = shape.index(max(shape))
    index_at[longest] = (index_at[longest] + 1) % shape[longest]
    return drawn.at[tuple(index_at)].set(high)


def level_of(stream_key, shape, pieces, low, high):
    loudness, own = 1.0, jax.random.fold_in(stream_key, 6)
    for dim, parts in pieces:
        draws = jnp.exp(jax.random.uniform(jax.random.fold_in(own, dim), (parts,), jnp.float32, low / len(pieces), high / len(pieces)))
        loudness = loudness * jnp.repeat(draws, shape[dim] // parts).reshape([-1 if axis == dim else 1 for axis in range(len(shape))])
    return loudness


def routed_block(stream_key, own, number, rows, amount, top, most, slope):
    order = jax.random.permutation(stream_key, amount)
    crowded, usual = load_shares(amount, rows * top, most, slope, True), load_shares(amount, rows * top, most, slope, False)
    places = jnp.arange(amount)

    def named(sizes, offset_by):
        used = int((sizes > 0).sum())
        fixed = max(1, used // 4)
        shifted = fixed + (places - fixed + offset_by * (used - fixed)) % max(1, amount - fixed)
        return jnp.zeros((amount,), jnp.int32).at[order[jnp.where(places < fixed, places, shifted)]].set(jnp.asarray(sizes, jnp.int32))

    sizes = jnp.where(number % 4 == 0, named(crowded, number // 4), named(usual, number - number // 4 - 1))
    mixed = jax.random.permutation(jax.random.fold_in(own, 3), amount)
    source_of, sink = mixed[0:amount // 2 * 2:2], mixed[1:amount // 2 * 2:2]
    room = jnp.minimum(sizes[source_of] - 1, most - sizes[sink]) // 2
    room = jnp.where((source_of == order[0]) | (sink == order[0]) | (sizes[sink] == 0), 0, jnp.maximum(room, 0))
    shifted = jax.random.randint(jax.random.fold_in(own, 4), (amount // 2,), 0, 1 << 20) % (room + 1)
    sizes = sizes.at[source_of].add(-shifted).at[sink].add(shifted)
    items = jnp.searchsorted(jnp.cumsum(sizes), jnp.arange(rows * top), side="right").astype(jnp.int32)
    listing = items.reshape(top, rows).T
    listing = listing[jax.random.permutation(jax.random.fold_in(own, 1), rows)]
    offset_by = jax.random.randint(jax.random.fold_in(own, 2), (rows, 1), 0, top)
    return jnp.take_along_axis(listing, (jnp.arange(top)[None, :] + offset_by) % top, axis=1)


def load_shares(count, total, limit, lean, full):
    weights = [(1 << 20) // math.isqrt(grade ** lean) + 1 for grade in range(1, count + 1)]
    largest = limit if full else min(limit, max(-(-total // count), total * weights[0] // sum(weights)))
    least = 1 if total - largest >= count - 1 else 0
    counts, surplus = [largest] + [least] * (count - 1), total - largest - least * (count - 1)
    while surplus > 0:
        free = [i for i in range(1, count) if counts[i] < largest] or [i for i in range(1, count) if counts[i] < limit]
        whole, left = sum([weights[i] for i in free]), surplus
        for i in free:
            addition = min(limit - counts[i], max(1, left * weights[i] // whole), surplus)
            counts[i] = counts[i] + addition
            surplus = surplus - addition
    return np.array(counts)


def normal_values(rng, extent, spread, reach, shards=(), kind=jnp.bfloat16):
    level = level_of(rng, extent, shards, -0.22, 0.18) if shards else 1.0
    array = jax.random.normal(rng, extent, jnp.float32) * spread * level
    return jnp.minimum(jnp.maximum(array, -reach), reach).astype(kind)


def setup_inputs(seed: int = 0) -> dict:
    key_of = jax.random.split(jax.random.key(seed), 8)
    currents = normal_values(key_of[0], (NF, 4, 2, PX, NY), 1.0, 6.0, ((3, 32),))
    row_angles = plant(jax.random.randint(key_of[1], (U,), 0, 4 * NY), jax.random.fold_in(key_of[1], 1), 0, (4 * NY) - 1).astype(jnp.int32)
    column_angles = plant(jax.random.randint(key_of[2], (V,), 0, 4 * NY), jax.random.fold_in(key_of[2], 1), 0, (4 * NY) - 1).astype(jnp.int32)
    target = jnp.clip(2.0 + 12.0 * jax.random.uniform(key_of[3], (NF, V, U), jnp.float32) ** level_of(key_of[3], (NF, V, U), ((1, 8), (2, 4)), -0.2, 0.2), 2.0, 14.0)
    weight = jnp.clip(jnp.exp(math.log(0.1) - 2.3025851 * jax.random.uniform(key_of[4], (NF, V, U), jnp.float32) ** level_of(key_of[4], (NF, V, U), ((1, 8), (2, 4)), -0.2, 0.2)), 0.01, 0.1)
    tile_owner_keys = jax.random.split(jax.random.fold_in(key_of[5], 1), SEGS // SEGS_DEV)
    tile_owner_turns = jax.random.permutation(jax.random.fold_in(key_of[5], 3), SEGS // SEGS_DEV)
    tile_owner = jax.vmap(lambda own, number: routed_block(jax.random.fold_in(key_of[5], 2), own, number, SEGS_DEV, N_ROW * N_TILE, 1, CAP, 2))(tile_owner_keys, tile_owner_turns).reshape((SEGS, 1))
    face_slot = plant(jax.random.randint(key_of[6], (SEGS,), 0, FACES_DEV), jax.random.fold_in(key_of[6], 1), 0, FACES_DEV - 1).astype(jnp.int32)
    return {"currents": currents, "row_angles": row_angles, "column_angles": column_angles, "target": target, "weight": weight, "tile_owner": tile_owner, "face_slot": face_slot}


def phase_pair(position, angles, modulus, scale):
    turns = position[:, None] * angles[None, :] % modulus
    angle = turns.astype(jnp.float32) * (2.0 * math.pi / modulus)
    return (jnp.cos(angle) * scale, jnp.sin(angle) * scale)

def rounded(value):
    return lax.optimization_barrier(value.astype(jnp.bfloat16)).astype(jnp.float32)

def spread_back(half):
    return jnp.stack([half[:, 0], half[:, 1], -half[:, 1], half[:, 0]], axis=1)

def reference(currents, row_angles, column_angles, target, weight, tile_owner, face_slot):
    freq_count, comp_count, part_count, plane_rows, columns = currents.shape
    modulus = 4 * columns
    column_index = jnp.arange(columns, dtype=jnp.int32)
    row_index = jnp.arange(plane_rows, dtype=jnp.int32)
    col_cos, col_sin = phase_pair(column_index, column_angles, modulus, 1.0 / math.sqrt(columns))
    col_cos = rounded(col_cos)
    col_sin = rounded(col_sin)
    row_cos, row_sin = phase_pair(row_index, row_angles, modulus, 1.0 / math.sqrt(plane_rows))
    row_cos = rounded(row_cos)
    row_sin = rounded(row_sin)
    real_in = currents[:, :, 0].astype(jnp.float32).reshape(freq_count * comp_count, plane_rows, columns)
    imag_in = currents[:, :, 1].astype(jnp.float32).reshape(freq_count * comp_count, plane_rows, columns)
    cols_re = rounded(jnp.einsum('qxy,yv->qxv', real_in, col_cos) + jnp.einsum('qxy,yv->qxv', imag_in, col_sin))
    cols_im = rounded(jnp.einsum('qxy,yv->qxv', imag_in, col_cos) - jnp.einsum('qxy,yv->qxv', real_in, col_sin))
    field_re = jnp.einsum('qxv,xu->qvu', cols_re, row_cos) + jnp.einsum('qxv,xu->qvu', cols_im, row_sin)
    field_im = jnp.einsum('qxv,xu->qvu', cols_im, row_cos) - jnp.einsum('qxv,xu->qvu', cols_re, row_sin)
    field_re = field_re.reshape(freq_count, comp_count, field_re.shape[1], field_re.shape[2])
    field_im = field_im.reshape(freq_count, comp_count, field_im.shape[1], field_im.shape[2])
    mixed_re = jnp.stack([field_re[:, 0] + field_re[:, 3], field_re[:, 1] - field_re[:, 2]], axis=1)
    mixed_im = jnp.stack([field_im[:, 0] + field_im[:, 3], field_im[:, 1] - field_im[:, 2]], axis=1)
    intensity = lax.optimization_barrier(jnp.sum(mixed_re * mixed_re + mixed_im * mixed_im, axis=1))
    factor = 4.0 * weight * (intensity - target)
    grad_re = rounded(factor[:, None] * mixed_re)
    grad_im = rounded(factor[:, None] * mixed_im)
    back_re = jnp.einsum('fpvu,xu->fpxv', grad_re, row_cos) - jnp.einsum('fpvu,xu->fpxv', grad_im, row_sin)
    back_im = jnp.einsum('fpvu,xu->fpxv', grad_re, row_sin) + jnp.einsum('fpvu,xu->fpxv', grad_im, row_cos)
    plane_re = rounded(spread_back(back_re)).reshape(freq_count * comp_count, plane_rows, -1)
    plane_im = rounded(spread_back(back_im)).reshape(freq_count * comp_count, plane_rows, -1)
    adjoint_re = jnp.einsum('qxv,yv->qxy', plane_re, col_cos) - jnp.einsum('qxv,yv->qxy', plane_im, col_sin)
    adjoint_im = jnp.einsum('qxv,yv->qxy', plane_re, col_sin) + jnp.einsum('qxv,yv->qxy', plane_im, col_cos)
    adjoint = rounded(jnp.stack([adjoint_re, adjoint_im], axis=1))
    segments = adjoint.reshape(freq_count * comp_count * part_count, plane_rows * columns // SEG, SEG)
    target_index = (tile_owner[:, 0] * FACES_DEV + face_slot).astype(jnp.int32)
    faces = jnp.zeros((freq_count * comp_count * part_count, N_ROW * N_TILE * FACES_DEV, SEG), jnp.float32)
    faces = faces.at[:, target_index].add(segments)
    return (intensity, faces.reshape(freq_count, comp_count, part_count, N_ROW * N_TILE * FACES_DEV, SEG))
```

```python
import functools
import math

import jax
import jax.numpy as jnp
from jax import lax
from jax.experimental import pallas as pl
from jax.experimental.pallas import tpu as pltpu
from jax.sharding import PartitionSpec as P

SEG = 128
CHUNK = 256
BF = jnp.bfloat16
F32 = jnp.float32


def cos_sin(turns, quarter, scale):
    bits = int(math.log2(quarter))
    turns = turns & (4 * quarter - 1)
    octant = (turns + quarter // 2) >> bits
    angle = (turns - (octant << bits)).astype(F32) * (math.pi / (2 * quarter))
    square = angle * angle
    sin_part = angle * scale + (angle * scale) * square * (
        -1.6666654611e-1 + square * (8.3321608736e-3 - square * 1.9515295891e-4)
    )
    cos_part = scale - square * (0.5 * scale) + (square * scale) * square * (
        4.166664568298827e-2 + square * (-1.388731625493765e-3 + square * 2.443315711809948e-5)
    )
    swap = (octant & 1) == 1
    cos_out = jnp.where(swap, sin_part, cos_part)
    sin_out = jnp.where(swap, cos_part, sin_part)
    cos_out = jnp.where(((octant + 1) & 2) == 2, -cos_out, cos_out)
    sin_out = jnp.where((octant & 2) == 2, -sin_out, sin_out)
    return cos_out, sin_out


def iota(shape, dim):
    return lax.broadcasted_iota(jnp.int32, shape, dim)


def forward_kernel(quarter, rows_dev, angle_ref, cur_ref, f_ref, w_ref, t_ref, lhs):
    columns = quarter
    points = rows_dev * columns // SEG
    width = angle_ref.shape[-1]

    @pl.when(pl.program_id(0) == 0)
    def _():
        for f in range(2):
            for p in range(2):
                rows = pl.ds((2 * f + p) * points, points)
                for c in range(2):
                    first, second = (0, 3) if p == 0 else (1, 2)
                    lhs[rows, c * SEG:(c + 1) * SEG] = cur_ref[f, first, c]
                    other = cur_ref[f, second, c]
                    if p == 1:
                        other = (-other.astype(F32)).astype(BF)
                    lhs[rows, (2 + c) * SEG:(3 + c) * SEG] = other

    angles = angle_ref[0]
    cos_b, sin_b = cos_sin(iota((SEG, width), 0) * angles, quarter, 1.0 / math.sqrt(columns))
    cos_b, sin_b = cos_b.astype(BF), sin_b.astype(BF)
    table = jnp.concatenate(
        [
            jnp.concatenate([cos_b, -sin_b], axis=1),
            jnp.concatenate([sin_b, cos_b], axis=1),
        ],
        axis=0,
    )
    w_ref[0] = table
    coarse = (iota((points, width), 0) // rows_dev) * SEG
    cos_a, sin_a = cos_sin(coarse * angles, quarter, 1.0)
    t_ref[0, 0] = cos_a
    t_ref[0, 1] = sin_a
    both = jnp.concatenate([table, table], axis=0)
    low = iota((8, width), 0) < 4
    for fp in range(4):
        grid_sum = jnp.dot(
            lhs[pl.ds(fp * points, points), :], both, preferred_element_type=F32
        )
        real, imag = grid_sum[:, :width], grid_sum[:, width:]
        out_re = jnp.sum((real * cos_a + imag * sin_a).reshape(points // 8, 8, width), axis=0)
        out_im = jnp.sum((imag * cos_a - real * sin_a).reshape(points // 8, 8, width), axis=0)
        out_re = out_re + pltpu.roll(out_re, 4, 0)
        out_im = out_im + pltpu.roll(out_im, 4, 0)
        out = jnp.where(low, out_re, out_im).astype(BF)
        for copy in range(f_ref.shape[0]):
            f_ref[copy, 0, fp] = out


def middle_kernel(quarter, rows_dev, angle_ref, got_ref, target_ref, weight_ref, int_ref, back_ref, table):
    devices = got_ref.shape[0]
    share_v = got_ref.shape[-1]
    share_u = angle_ref.shape[-1]
    depth = devices * 2 * rows_dev

    @pl.when(pl.program_id(0) == 0)
    def _():
        row = iota((depth, share_u), 0)
        x = (row // (2 * rows_dev)) * rows_dev + (row & (rows_dev - 1))
        is_imag = (row & rows_dev) == rows_dev
        scale = 1.0 / math.sqrt(rows_dev * devices)
        cos_x, sin_x = cos_sin(x * angle_ref[...], quarter, scale)
        table[:, :share_u] = jnp.where(is_imag, sin_x, cos_x).astype(BF)
        table[:, share_u:] = jnp.where(is_imag, cos_x, -sin_x).astype(BF)

    mixed = []
    for p in range(2):
        plane = got_ref[:, p].astype(F32).reshape(depth, share_v).astype(BF)
        mixed.append(
            lax.dot_general(plane, table[...], (((0,), (0,)), ((), ())), preferred_element_type=F32)
        )
    power = mixed[0] * mixed[0] + mixed[1] * mixed[1]
    intensity = power[:, :share_u] + power[:, share_u:]
    int_ref[0] = intensity
    factor = 4.0 * weight_ref[0] * (intensity - target_ref[0])
    factor = jnp.concatenate([factor, factor], axis=1)
    for p in range(2):
        far_grad = (factor * mixed[p]).astype(BF)
        back = lax.dot_general(
            table[...], far_grad, (((1,), (1,)), ((), ())), preferred_element_type=F32
        )
        back_ref[:, p] = back.reshape(devices, 2 * rows_dev, share_v).astype(BF)


def adjoint_kernel(devices, rows_dev, got_ref, w_ref, t_ref, owner_ref, slot_ref, out_ref, label_ref, total):
    points = t_ref.shape[2]
    width = t_ref.shape[3]
    segs = points // rows_dev
    slots = out_ref.shape[1]
    cap = slots // devices
    step = pl.program_id(0)

    @pl.when(step == 0)
    def _():
        total[...] = jnp.zeros_like(total)

    cos_a, sin_a = t_ref[0, 0], t_ref[0, 1]
    low = iota((8, width), 0) < 4
    parts = []
    for fp in range(4):
        plane = jnp.sum(got_ref[:, 0, fp].astype(F32), axis=0)
        turned = pltpu.roll(plane, 4, 0)
        real = jnp.where(low, plane, turned)
        imag = jnp.where(low, turned, plane)
        real = jnp.broadcast_to(real[None], (points // 8, 8, width)).reshape(points, width)
        imag = jnp.broadcast_to(imag[None], (points // 8, 8, width)).reshape(points, width)
        parts.append(
            jnp.concatenate(
                [
                    (cos_a * real - sin_a * imag).astype(BF),
                    (cos_a * imag + sin_a * real).astype(BF),
                ],
                axis=1,
            )
        )
    lhs = jnp.concatenate(parts, axis=0)
    total[...] += lax.dot_general(
        lhs, w_ref[0], (((1,), (1,)), ((), ())), preferred_element_type=F32
    )

    @pl.when(step == pl.num_programs(0) - 1)
    def _():
        point = iota((points, points), 1)
        point = (point & (rows_dev - 1)) * segs + (point // rows_dev)
        source = iota((points, points), 0)
        owner_col = owner_ref[...]
        owner_row = jnp.sum(jnp.where(source == point, owner_col, 0), axis=0, keepdims=True)
        same = jnp.where((source < point) & (owner_col == owner_row), 1, 0)
        place = owner_row * cap + jnp.sum(same, axis=0, keepdims=True)
        choose = jnp.where(iota((slots, points), 0) == place, 1.0, 0.0).astype(BF)
        for fp in range(4):
            block = total[fp * points:(fp + 1) * points, :].astype(BF)
            sent = jnp.dot(choose, block, preferred_element_type=F32).astype(BF)
            out_ref[2 * fp] = sent[:, :SEG]
            out_ref[2 * fp + 1] = sent[:, SEG:]
        slot_col = slot_ref[...]
        slot_row = jnp.sum(jnp.where(source == point, slot_col, 0), axis=0, keepdims=True)
        marks = jnp.where(iota((slots, points), 0) == place, slot_row + 1, 0)
        marks = jnp.sum(marks, axis=1, keepdims=True)
        label_ref[...] = marks


def faces_kernel(got_ref, label_ref, out_ref):
    faces = out_ref.shape[3]
    slots = got_ref.shape[1]
    hit = iota((faces, slots), 0) + 1 == label_ref[...]
    choose = jnp.where(hit, 1.0, 0.0).astype(BF)
    for f in range(2):
        for p in range(2):
            for c in range(2):
                found = jnp.dot(
                    choose, got_ref[4 * f + 2 * p + c], preferred_element_type=F32
                )
                if p == 0:
                    out_ref[f, 0, c] = found
                    out_ref[f, 3, c] = found
                else:
                    out_ref[f, 1, c] = found
                    out_ref[f, 2, c] = -found


def params():
    return pltpu.CompilerParams(
        dimension_semantics=("arbitrary",), vmem_limit_bytes=56 * 1024 * 1024
    )


def whole(shape):
    return pl.BlockSpec(shape, lambda i: (0,) * len(shape))


def body(currents, row_angles, column_angles, target, weight, tile_owner, face_slot):
    row_count = lax.axis_size("row")
    tile_count = lax.axis_size("tile")
    devices = row_count * tile_count
    freq_count, comp_count, part_count, rows_dev, columns = currents.shape
    far_rows = row_angles.shape[0]
    far_cols = column_angles.shape[0]
    share_v = far_cols // tile_count
    share_u = far_rows // row_count
    chunks = far_cols // CHUNK
    tiles = columns // SEG
    points = rows_dev * tiles
    both = ("row", "tile")

    cur = currents.reshape(freq_count, comp_count, part_count, rows_dev, tiles, SEG)
    cur = cur.transpose(0, 1, 2, 4, 3, 5).reshape(freq_count, comp_count, part_count, points, SEG)
    copies = row_count if share_v == CHUNK else 1
    plane, table, turn = pl.pallas_call(
        functools.partial(forward_kernel, columns, rows_dev),
        grid=(chunks,),
        in_specs=[
            pl.BlockSpec((1, 1, CHUNK), lambda i: (i, 0, 0)),
            whole(cur.shape),
        ],
        out_specs=[
            pl.BlockSpec((copies, 1, 4, 2 * rows_dev, CHUNK), lambda i: (0, i, 0, 0, 0)),
            pl.BlockSpec((1, 2 * SEG, 2 * CHUNK), lambda i: (i, 0, 0)),
            pl.BlockSpec((1, 2, points, CHUNK), lambda i: (i, 0, 0, 0)),
        ],
        out_shape=[
            jax.ShapeDtypeStruct((copies, chunks, 4, 2 * rows_dev, CHUNK), BF),
            jax.ShapeDtypeStruct((chunks, 2 * SEG, 2 * CHUNK), BF),
            jax.ShapeDtypeStruct((chunks, 2, points, CHUNK), F32),
        ],
        scratch_shapes=[pltpu.VMEM((4 * points, 4 * SEG), BF)],
        compiler_params=params(),
        name="columns",
    )(column_angles.reshape(chunks, 1, CHUNK), cur)

    if share_v != CHUNK:
        plane = plane.reshape(chunks, 4, 2 * rows_dev, CHUNK // share_v, share_v)
        plane = plane.transpose(0, 3, 1, 2, 4).reshape(1, tile_count, 4, 2 * rows_dev, share_v)
        plane = jnp.broadcast_to(plane, (row_count,) + plane.shape[1:])
    plane = plane.reshape(devices, 4, 2 * rows_dev, share_v)
    got = lax.all_to_all(plane, both, split_axis=0, concat_axis=0, tiled=True)

    own_angles = lax.dynamic_slice_in_dim(row_angles, lax.axis_index("row") * share_u, share_u)
    pair = pl.BlockSpec((devices, 2, 2 * rows_dev, share_v), lambda i: (0, i, 0, 0))
    far = pl.BlockSpec((1, share_v, share_u), lambda i: (i, 0, 0))
    intensity, back = pl.pallas_call(
        functools.partial(middle_kernel, columns, rows_dev),
        grid=(freq_count,),
        in_specs=[whole((1, share_u)), pair, far, far],
        out_specs=[far, pair],
        out_shape=[
            jax.ShapeDtypeStruct((freq_count, share_v, share_u), F32),
            jax.ShapeDtypeStruct((devices, 4, 2 * rows_dev, share_v), BF),
        ],
        scratch_shapes=[pltpu.VMEM((devices * 2 * rows_dev, 2 * share_u), BF)],
        compiler_params=params(),
        name="objective",
    )(own_angles.reshape(1, share_u), got, target, weight)

    back = lax.all_to_all(back, both, split_axis=0, concat_axis=0, tiled=True)
    back = back.reshape(row_count, tile_count, 4, 2 * rows_dev, share_v)
    if share_v != CHUNK:
        back = back.reshape(row_count, chunks, CHUNK // share_v, 4, 2 * rows_dev, share_v)
        back = back.transpose(0, 1, 3, 4, 2, 5).reshape(row_count, chunks, 4, 2 * rows_dev, CHUNK)

    seg_count = rows_dev * tiles
    slots = 2 * seg_count
    cap = slots // devices
    outgoing, labels = pl.pallas_call(
        functools.partial(adjoint_kernel, devices, rows_dev),
        grid=(chunks,),
        in_specs=[
            pl.BlockSpec((row_count, 1, 4, 2 * rows_dev, CHUNK), lambda i: (0, i, 0, 0, 0)),
            pl.BlockSpec((1, 2 * SEG, 2 * CHUNK), lambda i: (i, 0, 0)),
            pl.BlockSpec((1, 2, points, CHUNK), lambda i: (i, 0, 0, 0)),
            whole((seg_count, 1)),
            whole((seg_count, 1)),
        ],
        out_specs=[whole((8, slots, SEG)), whole((slots, 1))],
        out_shape=[
            jax.ShapeDtypeStruct((8, slots, SEG), BF),
            jax.ShapeDtypeStruct((slots, 1), jnp.int32),
        ],
        scratch_shapes=[pltpu.VMEM((4 * points, 2 * SEG), F32)],
        compiler_params=params(),
        name="adjoint",
    )(back, table, turn, tile_owner, face_slot.reshape(seg_count, 1))

    arrived = lax.all_to_all(
        outgoing.reshape(8, devices, cap, SEG), both, split_axis=1, concat_axis=1, tiled=True
    )
    marks = lax.all_to_all(
        labels.reshape(devices, cap), both, split_axis=0, concat_axis=0, tiled=True
    )
    out_shape = (freq_count, comp_count, part_count, seg_count, SEG)
    faces = pl.pallas_call(
        faces_kernel,
        grid=(1,),
        in_specs=[whole((8, slots, SEG)), whole((1, slots))],
        out_specs=whole(out_shape),
        out_shape=jax.ShapeDtypeStruct(out_shape, F32),
        compiler_params=params(),
        name="faces",
    )(arrived.reshape(8, slots, SEG), marks.reshape(1, slots))
    return (intensity, faces)


def solution(mesh):
    in_specs = (
        P(None, None, None, ("row", "tile"), None),
        P(),
        P(),
        P(None, "tile", "row"),
        P(None, "tile", "row"),
        P(("row", "tile"), None),
        P(("row", "tile")),
    )
    out_specs = (P(None, "tile", "row"), P(None, None, None, ("row", "tile"), None))
    return jax.shard_map(body, mesh=mesh, in_specs=in_specs, out_specs=out_specs, check_vma=False)
```

```python
import functools
import math

import jax
import jax.numpy as jnp
from jax import lax
from jax.experimental import pallas as pl
from jax.experimental.pallas import tpu as pltpu
from jax.sharding import PartitionSpec as P

SEG = 128
CHUNK = 256
PACK = 16
BF = jnp.bfloat16
F32 = jnp.float32


def cos_sin(turns, quarter, scale):
    bits = int(math.log2(quarter))
    turns = turns & (4 * quarter - 1)
    octant = (turns + quarter // 2) >> bits
    angle = (turns - (octant << bits)).astype(F32) * (math.pi / (2 * quarter))
    square = angle * angle
    sin_part = angle * scale + (angle * scale) * square * (
        -1.6666654611e-1 + square * (8.3321608736e-3 - square * 1.9515295891e-4)
    )
    cos_part = scale - square * (0.5 * scale) + (square * scale) * square * (
        4.166664568298827e-2 + square * (-1.388731625493765e-3 + square * 2.443315711809948e-5)
    )
    swap = (octant & 1) == 1
    cos_out = jnp.where(swap, sin_part, cos_part)
    sin_out = jnp.where(swap, cos_part, sin_part)
    cos_out = jnp.where(((octant + 1) & 2) == 2, -cos_out, cos_out)
    sin_out = jnp.where((octant & 2) == 2, -sin_out, sin_out)
    return cos_out, sin_out


def iota(shape, dim):
    return lax.broadcasted_iota(jnp.int32, shape, dim)


def turned(cos_0, sin_0, cos_1, sin_1):
    rows, width = cos_0.shape
    cos_out, sin_out = [], []
    for j in range(cos_1.shape[0]):
        cos_j = jnp.broadcast_to(cos_1[j:j + 1], (rows, width))
        sin_j = jnp.broadcast_to(sin_1[j:j + 1], (rows, width))
        cos_out.append(cos_0 * cos_j - sin_0 * sin_j)
        sin_out.append(sin_0 * cos_j + cos_0 * sin_j)
    return jnp.concatenate(cos_out, axis=0), jnp.concatenate(sin_out, axis=0)


def fine_table(quarter, angles):
    width = angles.shape[-1]
    steps = SEG // 8
    step = iota((2 * steps, width), 0)
    start = (step // steps) * (quarter // 2) + (step & (steps - 1)) * 8
    cos_0, sin_0 = cos_sin(iota((8, width), 0) * angles, quarter, 1.0 / math.sqrt(quarter))
    cos_1, sin_1 = cos_sin(start * angles, quarter, 1.0)
    return turned(cos_0, sin_0, cos_1, sin_1)


def coarse_table(quarter, rows_dev, angles):
    width = angles.shape[-1]
    tiles = quarter // SEG // 2
    group = 8 // rows_dev
    cos_0, sin_0 = cos_sin((iota((8, width), 0) // rows_dev) * SEG * angles, quarter, 1.0)
    start = iota((tiles // group, width), 0) * (group * SEG)
    cos_1, sin_1 = cos_sin(start * angles, quarter, 1.0)
    return turned(cos_0, sin_0, cos_1, sin_1)


def rotation(cos_part, sin_part):
    cos_part, sin_part = cos_part.astype(BF), sin_part.astype(BF)
    return jnp.concatenate(
        [
            jnp.concatenate([cos_part, -sin_part], axis=1),
            jnp.concatenate([sin_part, cos_part], axis=1),
        ],
        axis=0,
    )


def forward_kernel(quarter, rows_dev, angle_ref, cur_ref, f_ref, lhs):
    points = rows_dev * quarter // SEG // 2
    width = angle_ref.shape[-1]

    @pl.when(pl.program_id(0) == 0)
    def _():
        for f in range(2):
            for c in range(2):
                for half in range(2):
                    part = pl.ds(half * points, points)
                    spot = (2 * c + half) * SEG
                    j = [cur_ref[f, k, c, part, :].astype(F32) for k in range(4)]
                    lhs[2 * f * points:(2 * f + 1) * points, spot:spot + SEG] = (j[0] + j[3]).astype(BF)
                    lhs[(2 * f + 1) * points:(2 * f + 2) * points, spot:spot + SEG] = (j[1] - j[2]).astype(BF)

    angles = angle_ref[0]
    table = rotation(*fine_table(quarter, angles))
    cos_a, sin_a = coarse_table(quarter, rows_dev, angles)
    low = iota((8, width), 0) < 4
    for fp in range(4):
        grid_sum = jnp.dot(
            lhs[pl.ds(fp * points, points), :], table, preferred_element_type=F32
        )
        real, imag = grid_sum[:, :width], grid_sum[:, width:]
        out_re = jnp.sum((real * cos_a + imag * sin_a).reshape(points // 8, 8, width), axis=0)
        out_im = jnp.sum((imag * cos_a - real * sin_a).reshape(points // 8, 8, width), axis=0)
        out_re = out_re + pltpu.roll(out_re, 4, 0)
        out_im = out_im + pltpu.roll(out_im, 4, 0)
        out = jnp.where(low, out_re, out_im).astype(BF)
        for copy in range(f_ref.shape[0]):
            f_ref[copy, 0, fp] = out


def prepare_kernel(
    quarter, rows_dev, devices, angle_ref, row_ref, owner_ref, slot_ref,
    w_ref, t_ref, r_ref, choose_ref, mark_ref,
):
    points = owner_ref.shape[0]
    slots, units = choose_ref.shape[0], mark_ref.shape[0]
    depth, share_u = r_ref.shape[0], row_ref.shape[1]
    angles = angle_ref[0]
    w_ref[0] = rotation(*fine_table(quarter, angles))
    t_ref[0, 0], t_ref[0, 1] = coarse_table(quarter, rows_dev, angles)

    @pl.when(pl.program_id(0) == 0)
    def _():
        row = iota((depth, share_u), 0)
        x = (row // (2 * rows_dev)) * rows_dev + (row & (rows_dev - 1))
        is_imag = (row & rows_dev) == rows_dev
        scale = 1.0 / math.sqrt(rows_dev * devices)
        cos_x, sin_x = cos_sin(x * row_ref[...], quarter, scale)
        r_ref[:, :share_u] = jnp.where(is_imag, sin_x, cos_x).astype(BF)
        r_ref[:, share_u:] = jnp.where(is_imag, cos_x, -sin_x).astype(BF)

    @pl.when(pl.program_id(0) == 1)
    def _():
        segs = points // rows_dev
        cap = slots // devices
        point = iota((points, points), 1)
        point = (point & (rows_dev - 1)) * segs + (point // rows_dev)
        source = iota((points, points), 0)
        owner_col = owner_ref[...]
        owner_row = jnp.sum(jnp.where(source == point, owner_col, 0), axis=0, keepdims=True)
        same = jnp.where((source < point) & (owner_col == owner_row), 1, 0)
        place = owner_row * cap + jnp.sum(same, axis=0, keepdims=True)
        hit = iota((slots, points), 0) == place
        choose_ref[...] = jnp.where(hit, 1.0, 0.0).astype(BF)
        slot_col = slot_ref[...]
        slot_row = jnp.sum(jnp.where(source == point, slot_col, 0), axis=0, keepdims=True)
        marks = jnp.sum(jnp.where(hit, slot_row + 1, 0), axis=1, keepdims=True)
        marks = jnp.broadcast_to(marks, (slots, SEG)).reshape(units, 2, PACK // 2, SEG)
        marks = jnp.where(iota((PACK // 2, SEG), 1) < SEG // 2, marks[:, 0], marks[:, 1])
        mark_ref[...] = marks.astype(F32).astype(BF)


def middle_kernel(table, got_ref, target_ref, weight_ref, int_ref, back_ref):
    devices, pairs, rows, share_v = got_ref.shape
    depth = devices * rows
    share_u = table.shape[1] // 2

    mixed = []
    for p in range(2):
        plane = got_ref[:, p].astype(F32).reshape(depth, share_v).astype(BF)
        mixed.append(
            lax.dot_general(plane, table[...], (((0,), (0,)), ((), ())), preferred_element_type=F32)
        )
    power = mixed[0] * mixed[0] + mixed[1] * mixed[1]
    intensity = power[:, :share_u] + power[:, share_u:]
    int_ref[0] = intensity
    factor = 4.0 * weight_ref[0] * (intensity - target_ref[0])
    factor = jnp.concatenate([factor, factor], axis=1)
    for p in range(2):
        far_grad = (factor * mixed[p]).astype(BF)
        back = lax.dot_general(
            table[...], far_grad, (((1,), (1,)), ((), ())), preferred_element_type=F32
        )
        back_ref[:, p] = back.reshape(devices, rows, share_v).astype(BF)


def adjoint_kernel(got_ref, w_ref, t_ref, choose_ref, mark_ref, out_ref, total):
    points, width = t_ref.shape[2], t_ref.shape[3]
    units = out_ref.shape[0]
    step = pl.program_id(0)

    @pl.when(step == 0)
    def _():
        total[...] = jnp.zeros_like(total)

    cos_a, sin_a = t_ref[0, 0], t_ref[0, 1]
    low = iota((8, width), 0) < 4
    parts = []
    for fp in range(4):
        plane = jnp.sum(got_ref[:, 0, fp].astype(F32), axis=0)
        other = pltpu.roll(plane, 4, 0)
        real = jnp.where(low, plane, other)
        imag = jnp.where(low, other, plane)
        real = jnp.broadcast_to(real[None], (points // 8, 8, width)).reshape(points, width)
        imag = jnp.broadcast_to(imag[None], (points // 8, 8, width)).reshape(points, width)
        parts.append(
            jnp.concatenate(
                [
                    (cos_a * real - sin_a * imag).astype(BF),
                    (cos_a * imag + sin_a * real).astype(BF),
                ],
                axis=1,
            )
        )
    lhs = jnp.concatenate(parts, axis=0)
    total[...] += lax.dot_general(
        lhs, w_ref[0], (((1,), (1,)), ((), ())), preferred_element_type=F32
    )

    @pl.when(step == pl.num_programs(0) - 1)
    def _():
        for fp in range(4):
            block = total[fp * points:(fp + 1) * points, :].astype(BF)
            halves = []
            for half in range(2):
                spots = [(2 * c + half) * SEG for c in range(2)]
                halves.append(jnp.concatenate([block[:, i:i + SEG] for i in spots], axis=1))
            block = jnp.concatenate(halves, axis=0)
            sent = jnp.dot(choose_ref[...], block, preferred_element_type=F32).astype(BF)
            sent = sent.reshape(units, PACK, 2 * SEG)
            for c in range(2):
                rows = pl.ds((2 * fp + c) * PACK, PACK)
                out_ref[:, rows, :] = sent[:, :, c * SEG:(c + 1) * SEG]
        out_ref[:, 8 * PACK:, :] = mark_ref[...]


def faces_kernel(got_ref, out_ref):
    faces = out_ref.shape[3]
    units = got_ref.shape[0]
    slots = units * PACK
    marks = got_ref[:, 8 * PACK:, :].astype(F32)
    marks = jnp.concatenate([marks[:, :, :1], marks[:, :, SEG // 2:SEG // 2 + 1]], axis=1)
    marks = jnp.broadcast_to(marks.reshape(slots, 1), (slots, faces))
    hit = iota((slots, faces), 1) + 1 == marks.astype(jnp.int32)
    choose = jnp.where(hit, 1.0, 0.0).astype(BF)
    for f in range(2):
        for p in range(2):
            for c in range(2):
                rows = pl.ds((4 * f + 2 * p + c) * PACK, PACK)
                block = got_ref[:, rows, :].reshape(slots, SEG)
                found = lax.dot_general(
                    choose, block, (((0,), (0,)), ((), ())), preferred_element_type=F32
                )
                if p == 0:
                    out_ref[f, 0, c] = found
                    out_ref[f, 3, c] = found
                else:
                    out_ref[f, 1, c] = found
                    out_ref[f, 2, c] = -found


def exchange_small(outgoing, axes, devices, cap):
    units = outgoing.shape[0]
    rows = outgoing[:, :8 * PACK].reshape(units, 8, PACK, SEG).transpose(1, 0, 2, 3)
    rows = rows.reshape(8, devices, cap, SEG)
    marks = outgoing[:, 8 * PACK:, ::SEG // 2].transpose(0, 2, 1).reshape(devices, cap)
    rows = lax.all_to_all(rows, axes, split_axis=1, concat_axis=1, tiled=True)
    marks = lax.all_to_all(marks, axes, split_axis=0, concat_axis=0, tiled=True)
    rows = rows.reshape(8, units, PACK, SEG).transpose(1, 0, 2, 3).reshape(units, 8 * PACK, SEG)
    marks = marks.reshape(units, 2, PACK // 2).transpose(0, 2, 1)
    marks = jnp.repeat(marks, SEG // 2, axis=2)
    return jnp.concatenate([rows, marks], axis=1)


def params():
    return pltpu.CompilerParams(
        dimension_semantics=("arbitrary",), vmem_limit_bytes=24 * 1024 * 1024
    )


def cost(flops, moved):
    return pl.CostEstimate(flops=int(flops), bytes_accessed=int(moved), transcendentals=0)


def whole(shape):
    return pl.BlockSpec(shape, lambda i: (0,) * len(shape))


def body(currents, row_angles, column_angles, target, weight, tile_owner, face_slot):
    row_count = lax.axis_size("row")
    tile_count = lax.axis_size("tile")
    devices = row_count * tile_count
    freq_count, comp_count, part_count, rows_dev, columns = currents.shape
    far_rows = row_angles.shape[0]
    far_cols = column_angles.shape[0]
    share_v = far_cols // tile_count
    share_u = far_rows // row_count
    chunks = far_cols // CHUNK
    tiles = columns // SEG
    points = rows_dev * tiles
    both = ("row", "tile")

    half = points // 2
    seg_count = points
    slots = 2 * seg_count
    cap = slots // devices
    units = slots // PACK
    held = 8 * PACK + PACK // 2
    depth = devices * 2 * rows_dev
    angles = column_angles.reshape(chunks, 1, CHUNK)
    angle_spec = pl.BlockSpec((1, 1, CHUNK), lambda i: (i, 0, 0))
    table_spec = pl.BlockSpec((1, 4 * SEG, 2 * CHUNK), lambda i: (i, 0, 0))
    turn_spec = pl.BlockSpec((1, 2, half, CHUNK), lambda i: (i, 0, 0, 0))

    cur = currents.reshape(freq_count, comp_count, part_count, rows_dev, tiles, SEG)
    cur = cur.transpose(0, 1, 2, 4, 3, 5).reshape(freq_count, comp_count, part_count, points, SEG)
    copies = row_count if share_v == CHUNK else 1
    plane = pl.pallas_call(
        functools.partial(forward_kernel, columns, rows_dev),
        grid=(chunks,),
        in_specs=[angle_spec, whole(cur.shape)],
        out_specs=pl.BlockSpec((copies, 1, 4, 2 * rows_dev, CHUNK), lambda i: (0, i, 0, 0, 0)),
        out_shape=jax.ShapeDtypeStruct((copies, chunks, 4, 2 * rows_dev, CHUNK), BF),
        scratch_shapes=[pltpu.VMEM((4 * half, 4 * SEG), BF)],
        compiler_params=params(),
        cost_estimate=cost(4.3e9, 1.6e6),
        name="columns",
    )(angles, cur)

    if share_v != CHUNK:
        plane = plane.reshape(chunks, 4, 2 * rows_dev, CHUNK // share_v, share_v)
        plane = plane.transpose(0, 3, 1, 2, 4).reshape(1, tile_count, 4, 2 * rows_dev, share_v)
        plane = jnp.broadcast_to(plane, (row_count,) + plane.shape[1:])
    plane = plane.reshape(devices, 4, 2 * rows_dev, share_v)
    own_angles = lax.dynamic_slice_in_dim(row_angles, lax.axis_index("row") * share_u, share_u)
    angles, own_angles, owner, slot, plane = lax.optimization_barrier(
        (angles, own_angles, tile_owner, face_slot.reshape(seg_count, 1), plane)
    )
    table, turn, row_table, choose, mark = pl.pallas_call(
        functools.partial(prepare_kernel, columns, rows_dev, devices),
        grid=(chunks,),
        in_specs=[angle_spec, whole((1, share_u)), whole((seg_count, 1)), whole((seg_count, 1))],
        out_specs=[
            table_spec,
            turn_spec,
            whole((depth, 2 * share_u)),
            whole((slots, points)),
            whole((units, PACK // 2, SEG)),
        ],
        out_shape=[
            jax.ShapeDtypeStruct((chunks, 4 * SEG, 2 * CHUNK), BF),
            jax.ShapeDtypeStruct((chunks, 2, half, CHUNK), F32),
            jax.ShapeDtypeStruct((depth, 2 * share_u), BF),
            jax.ShapeDtypeStruct((slots, points), BF),
            jax.ShapeDtypeStruct((units, PACK // 2, SEG), BF),
        ],
        compiler_params=params(),
        cost_estimate=cost(4e9, 8e6),
        name="prepare",
    )(angles, own_angles.reshape(1, share_u), owner, slot)
    got = lax.all_to_all(plane, both, split_axis=0, concat_axis=0, tiled=True)

    pair = pl.BlockSpec((devices, 2, 2 * rows_dev, share_v), lambda i: (0, i, 0, 0))
    far = pl.BlockSpec((1, share_v, share_u), lambda i: (i, 0, 0))
    intensity, back = pl.pallas_call(
        middle_kernel,
        grid=(freq_count,),
        in_specs=[whole((depth, 2 * share_u)), pair, far, far],
        out_specs=[far, pair],
        out_shape=[
            jax.ShapeDtypeStruct((freq_count, share_v, share_u), F32),
            jax.ShapeDtypeStruct((devices, 4, 2 * rows_dev, share_v), BF),
        ],
        compiler_params=params(),
        cost_estimate=cost(1.1e9, 5e6),
        name="objective",
    )(row_table, got, target, weight)

    back = lax.all_to_all(back, both, split_axis=0, concat_axis=0, tiled=True)
    back = back.reshape(row_count, tile_count, 4, 2 * rows_dev, share_v)
    if share_v != CHUNK:
        back = back.reshape(row_count, chunks, CHUNK // share_v, 4, 2 * rows_dev, share_v)
        back = back.transpose(0, 1, 3, 4, 2, 5).reshape(row_count, chunks, 4, 2 * rows_dev, CHUNK)

    outgoing = pl.pallas_call(
        adjoint_kernel,
        grid=(chunks,),
        in_specs=[
            pl.BlockSpec((row_count, 1, 4, 2 * rows_dev, CHUNK), lambda i: (0, i, 0, 0, 0)),
            table_spec,
            turn_spec,
            whole((slots, points)),
            whole((units, PACK // 2, SEG)),
        ],
        out_specs=whole((units, held, SEG)),
        out_shape=jax.ShapeDtypeStruct((units, held, SEG), BF),
        scratch_shapes=[pltpu.VMEM((4 * half, 4 * SEG), F32)],
        compiler_params=params(),
        cost_estimate=cost(4.3e9, 8e6),
        name="adjoint",
    )(back, table, turn, choose, mark)

    if cap == PACK:
        arrived = lax.all_to_all(outgoing, both, split_axis=0, concat_axis=0, tiled=True)
    else:
        arrived = exchange_small(outgoing, both, devices, cap)
    out_shape = (freq_count, comp_count, part_count, seg_count, SEG)
    faces = pl.pallas_call(
        faces_kernel,
        grid=(1,),
        in_specs=[whole((units, held, SEG))],
        out_specs=whole(out_shape),
        out_shape=jax.ShapeDtypeStruct(out_shape, F32),
        compiler_params=params(),
        name="faces",
    )(arrived)
    return (intensity, faces)


def solution(mesh):
    in_specs = (
        P(None, None, None, ("row", "tile"), None),
        P(),
        P(),
        P(None, "tile", "row"),
        P(None, "tile", "row"),
        P(("row", "tile"), None),
        P(("row", "tile")),
    )
    out_specs = (P(None, "tile", "row"), P(None, None, None, ("row", "tile"), None))
    return jax.shard_map(body, mesh=mesh, in_specs=in_specs, out_specs=out_specs, check_vma=False)
```

```python
import functools
import math

import jax
import jax.numpy as jnp
from jax import lax
from jax.experimental import pallas as pl
from jax.experimental.pallas import tpu as pltpu
from jax.sharding import PartitionSpec as P

SEG = 128
CHUNK = 256
PACK = 16
BOTH = ("row", "tile")
BF = jnp.bfloat16
F32 = jnp.float32


def cos_sin(turns, quarter, scale):
    bits = int(math.log2(quarter))
    turns = turns & (4 * quarter - 1)
    octant = (turns + quarter // 2) >> bits
    angle = (turns - (octant << bits)).astype(F32) * (math.pi / (2 * quarter))
    square = angle * angle
    sin_part = angle * scale + (angle * scale) * square * (
        -1.6666654611e-1 + square * (8.3321608736e-3 - square * 1.9515295891e-4)
    )
    cos_part = scale - square * (0.5 * scale) + (square * scale) * square * (
        4.166664568298827e-2 + square * (-1.388731625493765e-3 + square * 2.443315711809948e-5)
    )
    swap = (octant & 1) == 1
    cos_out = jnp.where(swap, sin_part, cos_part)
    sin_out = jnp.where(swap, cos_part, sin_part)
    cos_out = jnp.where(((octant + 1) & 2) == 2, -cos_out, cos_out)
    sin_out = jnp.where((octant & 2) == 2, -sin_out, sin_out)
    return cos_out, sin_out


def iota(shape, dim):
    return lax.broadcasted_iota(jnp.int32, shape, dim)


def turned(cos_0, sin_0, cos_1, sin_1):
    rows, width = cos_0.shape
    cos_out, sin_out = [], []
    for j in range(cos_1.shape[0]):
        cos_j = jnp.broadcast_to(cos_1[j:j + 1], (rows, width))
        sin_j = jnp.broadcast_to(sin_1[j:j + 1], (rows, width))
        cos_out.append(cos_0 * cos_j - sin_0 * sin_j)
        sin_out.append(sin_0 * cos_j + cos_0 * sin_j)
    return jnp.concatenate(cos_out, axis=0), jnp.concatenate(sin_out, axis=0)


def fine_table(quarter, angles):
    width = angles.shape[-1]
    steps = SEG // 8
    step = iota((2 * steps, width), 0)
    start = (step // steps) * (quarter // 2) + (step & (steps - 1)) * 8
    cos_0, sin_0 = cos_sin(iota((8, width), 0) * angles, quarter, 1.0 / math.sqrt(quarter))
    cos_1, sin_1 = cos_sin(start * angles, quarter, 1.0)
    return turned(cos_0, sin_0, cos_1, sin_1)


def coarse_table(quarter, rows_dev, angles):
    width = angles.shape[-1]
    tiles = quarter // SEG // 2
    group = 8 // rows_dev
    cos_0, sin_0 = cos_sin((iota((8, width), 0) // rows_dev) * SEG * angles, quarter, 1.0)
    start = iota((tiles // group, width), 0) * (group * SEG)
    cos_1, sin_1 = cos_sin(start * angles, quarter, 1.0)
    return turned(cos_0, sin_0, cos_1, sin_1)


def rotation(cos_part, sin_part):
    cos_part, sin_part = cos_part.astype(BF), sin_part.astype(BF)
    return jnp.concatenate(
        [
            jnp.concatenate([cos_part, -sin_part], axis=1),
            jnp.concatenate([sin_part, cos_part], axis=1),
        ],
        axis=0,
    )


def forward_kernel(quarter, rows_dev, angle_ref, cur_hbm, f_ref, cur_ref, lhs, sem):
    points = rows_dev * quarter // SEG // 2
    width = angle_ref.shape[-1]
    load = pltpu.make_async_copy(cur_hbm, cur_ref, sem)

    @pl.when(pl.program_id(0) == 0)
    def _():
        load.start()

    angles = angle_ref[0]
    table = rotation(*fine_table(quarter, angles))
    cos_a, sin_a = coarse_table(quarter, rows_dev, angles)

    @pl.when(pl.program_id(0) == 0)
    def _():
        load.wait()
        for f in range(2):
            for c in range(2):
                for half in range(2):
                    part = pl.ds(half * points, points)
                    spot = (2 * c + half) * SEG
                    j = [cur_ref[f, k, c, part, :].astype(F32) for k in range(4)]
                    lhs[2 * f * points:(2 * f + 1) * points, spot:spot + SEG] = (j[0] + j[3]).astype(BF)
                    lhs[(2 * f + 1) * points:(2 * f + 2) * points, spot:spot + SEG] = (j[1] - j[2]).astype(BF)

    low = iota((8, width), 0) < 4
    for fp in range(4):
        grid_sum = jnp.dot(
            lhs[pl.ds(fp * points, points), :], table, preferred_element_type=F32
        )
        real, imag = grid_sum[:, :width], grid_sum[:, width:]
        out_re = jnp.sum((real * cos_a + imag * sin_a).reshape(points // 8, 8, width), axis=0)
        out_im = jnp.sum((imag * cos_a - real * sin_a).reshape(points // 8, 8, width), axis=0)
        out_re = out_re + pltpu.roll(out_re, 4, 0)
        out_im = out_im + pltpu.roll(out_im, 4, 0)
        out = jnp.where(low, out_re, out_im).astype(BF)
        for copy in range(f_ref.shape[0]):
            f_ref[copy, 0, fp] = out


def row_kernel(quarter, rows_dev, row_count, tile_count, row_ref, r_ref):
    depth, share_u = r_ref.shape[0], row_ref.shape[1]
    core = lax.axis_index("row") & 1
    row = iota((depth, share_u), 0)
    unit = row // (2 * rows_dev)
    far = unit // (depth // (4 * rows_dev))
    unit = unit - far * (depth // (4 * rows_dev))
    group = (unit // tile_count) * 2 + jnp.where(far == 1, 1 - core, core)
    x = (group * tile_count + unit % tile_count) * rows_dev + row % rows_dev
    is_imag = row % (2 * rows_dev) >= rows_dev
    scale = 1.0 / math.sqrt(rows_dev * row_count * tile_count)
    cos_x, sin_x = cos_sin(x * row_ref[...], quarter, scale)
    r_ref[:, :share_u] = jnp.where(is_imag, sin_x, cos_x).astype(BF)
    r_ref[:, share_u:] = jnp.where(is_imag, cos_x, -sin_x).astype(BF)


def prepare_kernel(quarter, rows_dev, tile_count, cap, angle_ref, code_ref, w_ref, v_ref, t_ref, choose_ref, mark_ref):
    points = code_ref.shape[0]
    slots, units = choose_ref.shape[1], mark_ref.shape[0]
    angles = angle_ref[0]
    table = rotation(*fine_table(quarter, angles))
    w_ref[0], v_ref[0] = table[:, :CHUNK], table[:, CHUNK:]
    t_ref[0, 0], t_ref[0, 1] = coarse_table(quarter, rows_dev, angles)

    @pl.when(pl.program_id(0) == 0)
    def _():
        segs = points // rows_dev
        half = tile_count // 2
        mine = lax.axis_index("tile") // half
        point = iota((points, points), 1)
        point = (point % rows_dev) * segs + (point // rows_dev)
        source = iota((points, points), 0)
        lane = iota((PACK // 2, SEG), 1) // (SEG // 4)
        marked = jnp.zeros((units, PACK // 2, SEG), jnp.int32)
        for side in range(2):
            code_col = code_ref[:, side:side + 1]
            code_row = jnp.sum(jnp.where(source == point, code_col, 0), axis=0, keepdims=True)
            owner_col, owner_row = code_col // points, code_row // points
            same = jnp.where((source < point) & (owner_col == owner_row), 1, 0)
            rank = jnp.sum(same, axis=0, keepdims=True)
            tile = owner_row % tile_count
            place = ((owner_row // tile_count) * half + tile % half) * cap + rank
            place = jnp.where(tile // half == mine, place, -1)
            hit = iota((slots, points), 0) == place
            choose_ref[side] = jnp.where(hit, 1.0, 0.0).astype(BF)
            marks = jnp.sum(jnp.where(hit, code_row % points + 1, 0), axis=1, keepdims=True)
            marks = jnp.broadcast_to(marks, (slots, SEG)).reshape(units, 2, PACK // 2, SEG)
            for part in range(2):
                marked = jnp.where(lane == 2 * side + part, marks[:, part], marked)
        mark_ref[...] = marked.astype(F32).astype(BF)


def middle_kernel(table, own_ref, far_ref, target_ref, weight_ref, int_ref, back_ref, over_ref):
    count, pairs, rows, share_v = own_ref.shape
    depth = 2 * count * rows
    share_u = table.shape[1] // 2

    mixed = []
    for p in range(2):
        plane = jnp.concatenate([own_ref[:, p], far_ref[:, p]], axis=0)
        plane = plane.astype(F32).reshape(depth, share_v).astype(BF)
        mixed.append(
            lax.dot_general(plane, table[...], (((0,), (0,)), ((), ())), preferred_element_type=F32)
        )
    power = mixed[0] * mixed[0] + mixed[1] * mixed[1]
    intensity = power[:, :share_u] + power[:, share_u:]
    int_ref[0] = intensity
    factor = 4.0 * weight_ref[0] * (intensity - target_ref[0])
    factor = jnp.concatenate([factor, factor], axis=1)
    for p in range(2):
        far_grad = (factor * mixed[p]).astype(BF)
        back = lax.dot_general(
            table[...], far_grad, (((1,), (1,)), ((), ())), preferred_element_type=F32
        )
        back = back.reshape(2 * count, rows, share_v).astype(BF)
        back_ref[:, p] = back[:count]
        over_ref[:, p] = back[count:]


def fold_kernel(own_ref, got_ref, out_ref):
    for side in range(2):
        total = own_ref[:, side].astype(F32) + got_ref[:, side].astype(F32)
        total = total.astype(BF)
        out_ref[:, side, :, 0] = total
        out_ref[:, 1 - side, :, 1] = total


def adjoint_kernel(got_ref, w_ref, v_ref, t_ref, choose_ref, mark_ref, out_ref, total):
    points, width = t_ref.shape[2], t_ref.shape[3]
    units = out_ref.shape[0]
    step = pl.program_id(0)

    @pl.when(step == 0)
    def _():
        total[...] = jnp.zeros_like(total)

    cos_a, sin_a = t_ref[0, 0], t_ref[0, 1]
    low = iota((8, width), 0) < 4
    parts = []
    for side, fp in [(i, j) for i in range(2) for j in range(4)]:
        plane = jnp.sum(got_ref[:, 0, side, fp].astype(F32), axis=0)
        other = pltpu.roll(plane, 4, 0)
        real = jnp.where(low, plane, other)
        imag = jnp.where(low, other, plane)
        real = jnp.broadcast_to(real[None], (points // 8, 8, width)).reshape(points, width)
        imag = jnp.broadcast_to(imag[None], (points // 8, 8, width)).reshape(points, width)
        parts.append(
            jnp.concatenate(
                [
                    (cos_a * real - sin_a * imag).astype(BF),
                    (cos_a * imag + sin_a * real).astype(BF),
                ],
                axis=1,
            )
        )
    lhs = jnp.concatenate(parts, axis=0)
    total[...] += lax.dot_general(
        lhs, jnp.concatenate([w_ref[0], v_ref[0]], axis=1), (((1,), (1,)), ((), ())),
        preferred_element_type=F32,
    )

    @pl.when(step == pl.num_programs(0) - 1)
    def _():
        for side, fp in [(i, j) for i in range(2) for j in range(4)]:
            start = (4 * side + fp) * points
            block = total[start:start + points, :].astype(BF)
            halves = []
            for half in range(2):
                spots = [(2 * c + half) * SEG for c in range(2)]
                halves.append(jnp.concatenate([block[:, i:i + SEG] for i in spots], axis=1))
            block = jnp.concatenate(halves, axis=0)
            sent = jnp.dot(choose_ref[side], block, preferred_element_type=F32).astype(BF)
            sent = sent.reshape(units, PACK, 2 * SEG)
            for c in range(2):
                rows = pl.ds((8 * side + 2 * fp + c) * PACK, PACK)
                out_ref[:, rows, :] = sent[:, :, c * SEG:(c + 1) * SEG]
        out_ref[:, 16 * PACK:, :] = mark_ref[...]


def faces_kernel(got_ref, out_ref):
    faces = out_ref.shape[3]
    units = got_ref.shape[0]
    slots = units * PACK
    marks = got_ref[:, 16 * PACK:, :].astype(F32)
    hits = []
    for side in range(2):
        spots = [(2 * side + part) * (SEG // 4) for part in range(2)]
        mark = jnp.concatenate([marks[:, :, i:i + 1] for i in spots], axis=1)
        mark = jnp.broadcast_to(mark.reshape(slots, 1), (slots, faces)).astype(jnp.int32)
        hits.append(jnp.where(iota((slots, faces), 1) + 1 == mark, 1.0, 0.0).astype(BF))
    choose = jnp.concatenate(hits, axis=0)
    for f in range(2):
        for p in range(2):
            for c in range(2):
                blocks = []
                for side in range(2):
                    rows = pl.ds((8 * side + 4 * f + 2 * p + c) * PACK, PACK)
                    blocks.append(got_ref[:, rows, :].reshape(slots, SEG))
                found = lax.dot_general(
                    choose, jnp.concatenate(blocks, axis=0), (((0,), (0,)), ((), ())),
                    preferred_element_type=F32,
                )
                if p == 0:
                    out_ref[f, 0, c] = found
                    out_ref[f, 3, c] = found
                else:
                    out_ref[f, 1, c] = found
                    out_ref[f, 2, c] = -found


def exchange_small(outgoing, groups, cap):
    units = outgoing.shape[0]
    peers = units * PACK // cap
    swap = functools.partial(
        lax.all_to_all, axis_name=BOTH, split_axis=1, concat_axis=1, tiled=True, axis_index_groups=groups
    )
    rows = outgoing[:, :16 * PACK].reshape(units, 16, PACK, SEG).transpose(1, 0, 2, 3)
    rows = swap(rows.reshape(16, peers, cap, SEG))
    rows = rows.reshape(16, units, PACK, SEG).transpose(1, 0, 2, 3).reshape(units, 16 * PACK, SEG)
    marks = outgoing[:, 16 * PACK:, ::SEG // 4].reshape(units, PACK // 2, 2, 2).transpose(2, 0, 3, 1)
    marks = swap(marks.reshape(2, peers, cap)).reshape(2, units, 2, PACK // 2)
    marks = marks.transpose(1, 3, 0, 2).reshape(units, PACK // 2, 4)
    return jnp.concatenate([rows, jnp.repeat(marks, SEG // 4, axis=2)], axis=1)


def params(mib=24):
    return pltpu.CompilerParams(
        dimension_semantics=("arbitrary",), vmem_limit_bytes=mib * 1024 * 1024
    )


def cost(flops, moved):
    return pl.CostEstimate(flops=int(flops), bytes_accessed=int(moved), transcendentals=0)


def whole(shape):
    return pl.BlockSpec(shape, lambda i: (0,) * len(shape))


def body(currents, row_angles, column_angles, target, weight, tile_owner, face_slot):
    row_count = lax.axis_size("row")
    tile_count = lax.axis_size("tile")
    devices = row_count * tile_count
    freq_count, comp_count, part_count, rows_dev, columns = currents.shape
    far_rows = row_angles.shape[0]
    far_cols = column_angles.shape[0]
    share_v = far_cols // tile_count
    share_u = far_rows // row_count
    chunks = far_cols // CHUNK
    tiles = columns // SEG
    points = rows_dev * tiles
    half = points // 2
    cap = 2 * points // devices
    slots = points
    units = slots // PACK
    held = 16 * PACK + PACK // 2
    pairs = row_count // 2
    peers = pairs * tile_count
    wide = 2 * rows_dev
    depth = devices * wide
    tile_half = tile_count // 2
    core_groups = [
        [(2 * x + core) * tile_count + t for x in range(pairs) for t in range(tile_count)]
        for core in range(2)
    ]
    half_groups = [
        [r * tile_count + side * tile_half + t for r in range(row_count) for t in range(tile_half)]
        for side in range(2)
    ]
    core_swap = [(i, i ^ 1) for i in range(row_count)]
    mirror = [(i, (i + tile_half) % tile_count) for i in range(tile_count)]
    angles = column_angles.reshape(chunks, 1, CHUNK)
    angle_spec = pl.BlockSpec((1, 1, CHUNK), lambda i: (i, 0, 0))
    table_spec = pl.BlockSpec((1, 4 * SEG, CHUNK), lambda i: (i, 0, 0))
    turn_spec = pl.BlockSpec((1, 2, half, CHUNK), lambda i: (i, 0, 0, 0))

    cur = currents.reshape(freq_count, comp_count, part_count, rows_dev, tiles, SEG)
    cur = cur.transpose(0, 1, 2, 4, 3, 5).reshape(freq_count, comp_count, part_count, points, SEG)
    copies = pairs if share_v == CHUNK else 1
    plane = pl.pallas_call(
        functools.partial(forward_kernel, columns, rows_dev),
        grid=(chunks,),
        in_specs=[angle_spec, pl.BlockSpec(memory_space=pltpu.HBM)],
        out_specs=pl.BlockSpec((copies, 1, 4, wide, CHUNK), lambda i: (0, i, 0, 0, 0)),
        out_shape=jax.ShapeDtypeStruct((copies, chunks, 4, wide, CHUNK), BF),
        scratch_shapes=[
            pltpu.VMEM(cur.shape, BF),
            pltpu.VMEM((4 * half, 4 * SEG), BF),
            pltpu.SemaphoreType.DMA(()),
        ],
        compiler_params=params(58),
        cost_estimate=cost(4.3e9, 1.6e6),
        name="columns",
    )(angles, cur)
    if share_v != CHUNK:
        plane = plane.reshape(chunks, 4, wide, CHUNK // share_v, share_v)
        plane = plane.transpose(0, 3, 1, 2, 4).reshape(1, tile_count, 4, wide, share_v)
        plane = jnp.broadcast_to(plane, (pairs,) + plane.shape[1:])
    plane = plane.reshape(peers, 4, wide, share_v)

    own = lax.all_to_all(plane, BOTH, 0, 0, tiled=True, axis_index_groups=core_groups)
    row_angles, owner, slot, own = lax.optimization_barrier(
        (row_angles, tile_owner, face_slot, own)
    )
    code = owner[:, 0] * points + slot
    code = jnp.stack([code, lax.ppermute(code, "tile", mirror)], axis=1)
    own_angles = lax.dynamic_slice_in_dim(row_angles, lax.axis_index("row") * share_u, share_u)
    row_table = pl.pallas_call(
        functools.partial(row_kernel, columns, rows_dev, row_count, tile_count),
        grid=(1,),
        in_specs=[whole((1, share_u))],
        out_specs=whole((depth, 2 * share_u)),
        out_shape=jax.ShapeDtypeStruct((depth, 2 * share_u), BF),
        compiler_params=params(),
        cost_estimate=cost(1e8, 5e5),
        name="rows",
    )(own_angles.reshape(1, share_u))
    other = lax.ppermute(own, "row", core_swap)

    pair = pl.BlockSpec((peers, 2, wide, share_v), lambda i: (0, i, 0, 0))
    far = pl.BlockSpec((1, share_v, share_u), lambda i: (i, 0, 0))
    back_shape = jax.ShapeDtypeStruct((peers, 4, wide, share_v), BF)
    intensity, back, over = pl.pallas_call(
        middle_kernel,
        grid=(freq_count,),
        in_specs=[whole((depth, 2 * share_u)), pair, pair, far, far],
        out_specs=[far, pair, pair],
        out_shape=[
            jax.ShapeDtypeStruct((freq_count, share_v, share_u), F32), back_shape, back_shape
        ],
        compiler_params=params(),
        cost_estimate=cost(1.1e9, 5e6),
        name="objective",
    )(row_table, own, other, target, weight)

    over = lax.ppermute(over, "row", core_swap)
    split = (pairs * 2, tile_half, 4, wide, share_v)
    part = pl.BlockSpec((1, 2, tile_half, 4, wide, share_v), lambda i: (i, 0, 0, 0, 0, 0))
    fold_out = (pairs, 2, tile_half, 2, 4, wide, share_v)
    back = pl.pallas_call(
        fold_kernel,
        grid=(pairs,),
        in_specs=[part, part],
        out_specs=pl.BlockSpec((1,) + fold_out[1:], lambda i: (i, 0, 0, 0, 0, 0, 0)),
        out_shape=jax.ShapeDtypeStruct(fold_out, BF),
        compiler_params=params(),
        cost_estimate=cost(1e6, 1e6),
        name="fold",
    )(back.reshape((pairs, 2) + split[1:]), over.reshape((pairs, 2) + split[1:]))

    angles, code, back = lax.optimization_barrier((angles, code, back))
    back = back.reshape(peers, 2, 4, wide, share_v)
    back = lax.all_to_all(back, BOTH, 0, 0, tiled=True, axis_index_groups=core_groups)
    table, table_im, turn, choose, mark = pl.pallas_call(
        functools.partial(prepare_kernel, columns, rows_dev, tile_count, cap),
        grid=(chunks,),
        in_specs=[angle_spec, whole((points, 2))],
        out_specs=[
            table_spec,
            table_spec,
            turn_spec,
            whole((2, slots, points)),
            whole((units, PACK // 2, SEG)),
        ],
        out_shape=[
            jax.ShapeDtypeStruct((chunks, 4 * SEG, CHUNK), BF),
            jax.ShapeDtypeStruct((chunks, 4 * SEG, CHUNK), BF),
            jax.ShapeDtypeStruct((chunks, 2, half, CHUNK), F32),
            jax.ShapeDtypeStruct((2, slots, points), BF),
            jax.ShapeDtypeStruct((units, PACK // 2, SEG), BF),
        ],
        compiler_params=params(),
        cost_estimate=cost(4e9, 8e6),
        name="prepare",
    )(angles, code)

    back = back.reshape(pairs, tile_count, 2, 4, wide, share_v)
    if share_v != CHUNK:
        back = back.reshape(pairs, chunks, CHUNK // share_v, 2, 4, wide, share_v)
        back = back.transpose(0, 1, 3, 4, 5, 2, 6).reshape(pairs, chunks, 2, 4, wide, CHUNK)
    outgoing = pl.pallas_call(
        adjoint_kernel,
        grid=(chunks,),
        in_specs=[
            pl.BlockSpec((pairs, 1, 2, 4, wide, CHUNK), lambda i: (0, i, 0, 0, 0, 0)),
            table_spec,
            table_spec,
            turn_spec,
            whole((2, slots, points)),
            whole((units, PACK // 2, SEG)),
        ],
        out_specs=whole((units, held, SEG)),
        out_shape=jax.ShapeDtypeStruct((units, held, SEG), BF),
        scratch_shapes=[pltpu.VMEM((8 * half, 4 * SEG), F32)],
        compiler_params=params(),
        cost_estimate=cost(8.6e9, 8e6),
        name="adjoint",
    )(back, table, table_im, turn, choose, mark)

    if cap == PACK:
        arrived = lax.all_to_all(outgoing, BOTH, 0, 0, tiled=True, axis_index_groups=half_groups)
    else:
        arrived = exchange_small(outgoing, half_groups, cap)
    out_shape = (freq_count, comp_count, part_count, points, SEG)
    faces = pl.pallas_call(
        faces_kernel,
        grid=(1,),
        in_specs=[whole((units, held, SEG))],
        out_specs=whole(out_shape),
        out_shape=jax.ShapeDtypeStruct(out_shape, F32),
        compiler_params=params(),
        name="faces",
    )(arrived)
    return (intensity, faces)


def solution(mesh):
    in_specs = (
        P(None, None, None, ("row", "tile"), None),
        P(),
        P(),
        P(None, "tile", "row"),
        P(None, "tile", "row"),
        P(("row", "tile"), None),
        P(("row", "tile")),
    )
    out_specs = (P(None, "tile", "row"), P(None, None, None, ("row", "tile"), None))
    return jax.shard_map(body, mesh=mesh, in_specs=in_specs, out_specs=out_specs, check_vma=False)
```

```python
import functools
import math

import jax
import jax.numpy as jnp
from jax import lax
from jax.experimental import pallas as pl
from jax.experimental.pallas import tpu as pltpu
from jax.sharding import PartitionSpec as P

SEG = 128
CHUNK = 256
PACK = 16
BOTH = ("row", "tile")
BF = jnp.bfloat16
F32 = jnp.float32


def cos_sin(turns, quarter, scale):
    bits = int(math.log2(quarter))
    turns = turns & (4 * quarter - 1)
    octant = (turns + quarter // 2) >> bits
    angle = (turns - (octant << bits)).astype(F32) * (math.pi / (2 * quarter))
    square = angle * angle
    sin_part = angle * scale + (angle * scale) * square * (
        -1.6666654611e-1 + square * (8.3321608736e-3 - square * 1.9515295891e-4)
    )
    cos_part = scale - square * (0.5 * scale) + (square * scale) * square * (
        4.166664568298827e-2 + square * (-1.388731625493765e-3 + square * 2.443315711809948e-5)
    )
    swap = (octant & 1) == 1
    cos_out = jnp.where(swap, sin_part, cos_part)
    sin_out = jnp.where(swap, cos_part, sin_part)
    cos_out = jnp.where(((octant + 1) & 2) == 2, -cos_out, cos_out)
    sin_out = jnp.where((octant & 2) == 2, -sin_out, sin_out)
    return cos_out, sin_out


def iota(shape, dim):
    return lax.broadcasted_iota(jnp.int32, shape, dim)


def turned(cos_0, sin_0, cos_1, sin_1):
    rows, width = cos_0.shape
    cos_out, sin_out = [], []
    for j in range(cos_1.shape[0]):
        cos_j = jnp.broadcast_to(cos_1[j:j + 1], (rows, width))
        sin_j = jnp.broadcast_to(sin_1[j:j + 1], (rows, width))
        cos_out.append(cos_0 * cos_j - sin_0 * sin_j)
        sin_out.append(sin_0 * cos_j + cos_0 * sin_j)
    return jnp.concatenate(cos_out, axis=0), jnp.concatenate(sin_out, axis=0)


def fine_table(quarter, angles):
    width = angles.shape[-1]
    steps = SEG // 8
    step = iota((2 * steps, width), 0)
    start = (step // steps) * (quarter // 2) + (step & (steps - 1)) * 8
    cos_0, sin_0 = cos_sin(iota((8, width), 0) * angles, quarter, 1.0 / math.sqrt(quarter))
    cos_1, sin_1 = cos_sin(start * angles, quarter, 1.0)
    return turned(cos_0, sin_0, cos_1, sin_1)


def coarse_table(quarter, rows_dev, angles):
    width = angles.shape[-1]
    tiles = quarter // SEG // 2
    group = 8 // rows_dev
    cos_0, sin_0 = cos_sin((iota((8, width), 0) // rows_dev) * SEG * angles, quarter, 1.0)
    start = iota((tiles // group, width), 0) * (group * SEG)
    cos_1, sin_1 = cos_sin(start * angles, quarter, 1.0)
    return turned(cos_0, sin_0, cos_1, sin_1)


def rotation(cos_part, sin_part):
    cos_part, sin_part = cos_part.astype(BF), sin_part.astype(BF)
    return jnp.concatenate(
        [
            jnp.concatenate([cos_part, -sin_part], axis=1),
            jnp.concatenate([sin_part, cos_part], axis=1),
        ],
        axis=0,
    )


def forward_kernel(quarter, rows_dev, angle_ref, cur_hbm, f_ref, cur_ref, lhs, sem):
    points = rows_dev * quarter // SEG // 2
    width = angle_ref.shape[-1]
    load = pltpu.make_async_copy(cur_hbm, cur_ref, sem)

    @pl.when(pl.program_id(0) == 0)
    def _():
        load.start()

    angles = angle_ref[0]
    table = rotation(*fine_table(quarter, angles))
    cos_a, sin_a = coarse_table(quarter, rows_dev, angles)

    @pl.when(pl.program_id(0) == 0)
    def _():
        load.wait()
        for f in range(2):
            for c in range(2):
                for half in range(2):
                    part = pl.ds(half * points, points)
                    spot = (2 * c + half) * SEG
                    j = [cur_ref[f, k, c, part, :].astype(F32) for k in range(4)]
                    lhs[2 * f * points:(2 * f + 1) * points, spot:spot + SEG] = (j[0] + j[3]).astype(BF)
                    lhs[(2 * f + 1) * points:(2 * f + 2) * points, spot:spot + SEG] = (j[1] - j[2]).astype(BF)

    low = iota((8, width), 0) < 4
    grid_sum = jnp.dot(lhs[...], table, preferred_element_type=F32)
    for f, p in [(i, j) for i in range(2) for j in range(2)]:
        start = (2 * f + p) * points
        real = grid_sum[start:start + points, :width]
        imag = grid_sum[start:start + points, width:]
        out_re = jnp.sum((real * cos_a + imag * sin_a).reshape(points // 8, 8, width), axis=0)
        out_im = jnp.sum((imag * cos_a - real * sin_a).reshape(points // 8, 8, width), axis=0)
        out_re = out_re + pltpu.roll(out_re, 4, 0)
        out_im = out_im + pltpu.roll(out_im, 4, 0)
        out = jnp.where(low, out_re, out_im).astype(BF)
        for copy in range(f_ref.shape[0]):
            f_ref[copy, f, 0, p] = out


def row_kernel(quarter, rows_dev, row_ref, r_ref):
    sides, depth = r_ref.shape[:2]
    share_u = row_ref.shape[-1]
    row = iota((depth, share_u), 0)
    x = (row // (2 * rows_dev)) * rows_dev + row % rows_dev
    is_imag = row % (2 * rows_dev) >= rows_dev
    scale = 1.0 / math.sqrt(depth // 2)
    for side in range(sides):
        cos_x, sin_x = cos_sin(x * row_ref[side:side + 1], quarter, scale)
        r_ref[side, :, :share_u] = jnp.where(is_imag, sin_x, cos_x).astype(BF)
        r_ref[side, :, share_u:] = jnp.where(is_imag, cos_x, -sin_x).astype(BF)


def prepare_kernel(quarter, rows_dev, tile_count, cap, angle_ref, code_ref, w_ref, t_ref, choose_ref, mark_ref):
    points = code_ref.shape[0]
    slots, units = choose_ref.shape[1], mark_ref.shape[0]
    angles = angle_ref[0]
    w_ref[0] = rotation(*fine_table(quarter, angles))
    t_ref[0, 0], t_ref[0, 1] = coarse_table(quarter, rows_dev, angles)

    @pl.when(pl.program_id(0) == 0)
    def _():
        segs = points // rows_dev
        half = tile_count // 2
        mine = lax.axis_index("tile") // half
        point = iota((points, points), 1)
        point = (point % rows_dev) * segs + (point // rows_dev)
        source = iota((points, points), 0)
        lane = iota((PACK // 2, SEG), 1) // (SEG // 4)
        marked = jnp.zeros((units, PACK // 2, SEG), jnp.int32)
        for side in range(2):
            code_col = code_ref[:, side:side + 1]
            code_row = jnp.sum(jnp.where(source == point, code_col, 0), axis=0, keepdims=True)
            owner_col, owner_row = code_col // points, code_row // points
            same = jnp.where((source < point) & (owner_col == owner_row), 1, 0)
            rank = jnp.sum(same, axis=0, keepdims=True)
            tile = owner_row % tile_count
            place = ((owner_row // tile_count) * half + tile % half) * cap + rank
            place = jnp.where(tile // half == mine, place, -1)
            hit = iota((slots, points), 0) == place
            choose_ref[side] = jnp.where(hit, 1.0, 0.0).astype(BF)
            marks = jnp.sum(jnp.where(hit, code_row % points + 1, 0), axis=1, keepdims=True)
            marks = jnp.broadcast_to(marks, (slots, SEG)).reshape(units, 2, PACK // 2, SEG)
            for part in range(2):
                marked = jnp.where(lane == 2 * side + part, marks[:, part], marked)
        mark_ref[...] = marked.astype(F32).astype(BF)


def middle_kernel(
    table, got_ref, target_ref, far_target_ref, weight_ref, far_weight_ref, int_ref, far_int_ref, back_ref
):
    devices, pols, rows, share_v = got_ref.shape
    depth = devices * rows
    share_u = table.shape[2] // 2
    planes = [
        got_ref[:, p].astype(F32).reshape(depth, share_v).astype(BF) for p in range(pols)
    ]
    sums = [None, None]
    sides = [
        (target_ref, weight_ref, int_ref), (far_target_ref, far_weight_ref, far_int_ref)
    ]
    for side, (goal_ref, gain_ref, power_ref) in enumerate(sides):
        mixed = [
            lax.dot_general(
                plane, table[side], (((0,), (0,)), ((), ())), preferred_element_type=F32
            )
            for plane in planes
        ]
        power = mixed[0] * mixed[0] + mixed[1] * mixed[1]
        intensity = power[:, :share_u] + power[:, share_u:]
        power_ref[...] = intensity
        factor = 4.0 * gain_ref[...] * (intensity - goal_ref[...])
        factor = jnp.concatenate([factor, factor], axis=1)
        for p in range(pols):
            far_grad = (factor * mixed[p]).astype(BF)
            back = lax.dot_general(
                table[side], far_grad, (((1,), (1,)), ((), ())), preferred_element_type=F32
            )
            sums[p] = back if side == 0 else sums[p] + back
    groups, halves, count = back_ref.shape[:3]
    for p in range(pols):
        total = sums[p].reshape(groups, halves, count, rows, share_v).astype(BF)
        for half in range(halves):
            back_ref[:, half, :, 0, p] = total[:, half]
            back_ref[:, 1 - half, :, 1, p] = total[:, half]


def adjoint_kernel(got_ref, w_ref, t_ref, choose_ref, mark_ref, out_ref, total):
    points, width = t_ref.shape[2], t_ref.shape[3]
    units = out_ref.shape[0]
    step = pl.program_id(0)

    @pl.when(step == 0)
    def _():
        total[...] = jnp.zeros_like(total)

    cos_a, sin_a = t_ref[0, 0], t_ref[0, 1]
    low = iota((8, width), 0) < 4
    parts = []
    for side, fp in [(i, j) for i in range(2) for j in range(4)]:
        plane = jnp.sum(got_ref[:, fp // 2, 0, side, fp % 2].astype(F32), axis=0)
        other = pltpu.roll(plane, 4, 0)
        real = jnp.where(low, plane, other)
        imag = jnp.where(low, other, plane)
        real = jnp.broadcast_to(real[None], (points // 8, 8, width)).reshape(points, width)
        imag = jnp.broadcast_to(imag[None], (points // 8, 8, width)).reshape(points, width)
        parts.append(
            jnp.concatenate(
                [
                    (cos_a * real - sin_a * imag).astype(BF),
                    (cos_a * imag + sin_a * real).astype(BF),
                ],
                axis=1,
            )
        )
    lhs = jnp.concatenate(parts, axis=0)
    total[...] += lax.dot_general(
        lhs, w_ref[0], (((1,), (1,)), ((), ())), preferred_element_type=F32
    )

    @pl.when(step == pl.num_programs(0) - 1)
    def _():
        for side, fp in [(i, j) for i in range(2) for j in range(4)]:
            start = (4 * side + fp) * points
            block = total[start:start + points, :].astype(BF)
            halves = []
            for half in range(2):
                spots = [(2 * c + half) * SEG for c in range(2)]
                halves.append(jnp.concatenate([block[:, i:i + SEG] for i in spots], axis=1))
            block = jnp.concatenate(halves, axis=0)
            sent = jnp.dot(choose_ref[side], block, preferred_element_type=F32).astype(BF)
            sent = sent.reshape(units, PACK, 2 * SEG)
            for c in range(2):
                rows = pl.ds((8 * side + 2 * fp + c) * PACK, PACK)
                out_ref[:, rows, :] = sent[:, :, c * SEG:(c + 1) * SEG]
        out_ref[:, 16 * PACK:, :] = mark_ref[...]


def faces_kernel(got_ref, out_ref):
    faces = out_ref.shape[3]
    units = got_ref.shape[0]
    slots = units * PACK
    marks = got_ref[:, 16 * PACK:, :].astype(F32)
    hits = []
    for side in range(2):
        spots = [(2 * side + part) * (SEG // 4) for part in range(2)]
        mark = jnp.concatenate([marks[:, :, i:i + 1] for i in spots], axis=1)
        mark = jnp.broadcast_to(mark.reshape(slots, 1), (slots, faces)).astype(jnp.int32)
        hits.append(jnp.where(iota((slots, faces), 1) + 1 == mark, 1.0, 0.0).astype(BF))
    choose = jnp.concatenate(hits, axis=0)
    for f in range(2):
        for p in range(2):
            for c in range(2):
                blocks = []
                for side in range(2):
                    rows = pl.ds((8 * side + 4 * f + 2 * p + c) * PACK, PACK)
                    blocks.append(got_ref[:, rows, :].reshape(slots, SEG))
                found = lax.dot_general(
                    choose, jnp.concatenate(blocks, axis=0), (((0,), (0,)), ((), ())),
                    preferred_element_type=F32,
                )
                if p == 0:
                    out_ref[f, 0, c] = found
                    out_ref[f, 3, c] = found
                else:
                    out_ref[f, 1, c] = found
                    out_ref[f, 2, c] = -found


def exchange_small(outgoing, groups, cap):
    units = outgoing.shape[0]
    peers = units * PACK // cap
    swap = functools.partial(
        lax.all_to_all, axis_name=BOTH, split_axis=1, concat_axis=1, tiled=True, axis_index_groups=groups
    )
    rows = outgoing[:, :16 * PACK].reshape(units, 16, PACK, SEG).transpose(1, 0, 2, 3)
    rows = swap(rows.reshape(16, peers, cap, SEG))
    rows = rows.reshape(16, units, PACK, SEG).transpose(1, 0, 2, 3).reshape(units, 16 * PACK, SEG)
    marks = outgoing[:, 16 * PACK:, ::SEG // 4].reshape(units, PACK // 2, 2, 2).transpose(2, 0, 3, 1)
    marks = swap(marks.reshape(2, peers, cap)).reshape(2, units, 2, PACK // 2)
    marks = marks.transpose(1, 3, 0, 2).reshape(units, PACK // 2, 4)
    return jnp.concatenate([rows, jnp.repeat(marks, SEG // 4, axis=2)], axis=1)


def params(mib=24):
    return pltpu.CompilerParams(
        dimension_semantics=("arbitrary",), vmem_limit_bytes=mib * 1024 * 1024
    )


def cost(flops, moved):
    return pl.CostEstimate(flops=int(flops), bytes_accessed=int(moved), transcendentals=0)


def whole(shape):
    return pl.BlockSpec(shape, lambda i: (0,) * len(shape))


def body(currents, row_angles, column_angles, target, weight, tile_owner, face_slot):
    row_count = lax.axis_size("row")
    tile_count = lax.axis_size("tile")
    devices = row_count * tile_count
    freq_count, comp_count, part_count, rows_dev, columns = currents.shape
    far_rows = row_angles.shape[0]
    far_cols = column_angles.shape[0]
    share_v = far_cols // tile_count
    share_u = far_rows // row_count
    chunks = far_cols // CHUNK
    tiles = columns // SEG
    points = rows_dev * tiles
    half = points // 2
    cap = 2 * points // devices
    slots = points
    units = slots // PACK
    held = 16 * PACK + PACK // 2
    pairs = row_count // 2
    wide = 2 * rows_dev
    depth = devices * wide
    tile_half = tile_count // 2
    half_groups = [
        [r * tile_count + side * tile_half + t for r in range(row_count) for t in range(tile_half)]
        for side in range(2)
    ]
    mirror = [(i, (i + tile_half) % tile_count) for i in range(tile_count)]
    angles = column_angles.reshape(chunks, 1, CHUNK)
    angle_spec = pl.BlockSpec((1, 1, CHUNK), lambda i: (i, 0, 0))
    table_spec = pl.BlockSpec((1, 4 * SEG, 2 * CHUNK), lambda i: (i, 0, 0))
    turn_spec = pl.BlockSpec((1, 2, half, CHUNK), lambda i: (i, 0, 0, 0))

    cur = currents.reshape(freq_count, comp_count, part_count, rows_dev, tiles, SEG)
    cur = cur.transpose(0, 1, 2, 4, 3, 5).reshape(freq_count, comp_count, part_count, points, SEG)
    copies = pairs if share_v == CHUNK else 1
    plane = pl.pallas_call(
        functools.partial(forward_kernel, columns, rows_dev),
        grid=(chunks,),
        in_specs=[angle_spec, pl.BlockSpec(memory_space=pltpu.HBM)],
        out_specs=pl.BlockSpec((copies, 2, 1, 2, wide, CHUNK), lambda i: (0, 0, i, 0, 0, 0)),
        out_shape=jax.ShapeDtypeStruct((copies, 2, chunks, 2, wide, CHUNK), BF),
        scratch_shapes=[
            pltpu.VMEM(cur.shape, BF),
            pltpu.VMEM((4 * half, 4 * SEG), BF),
            pltpu.SemaphoreType.DMA(()),
        ],
        compiler_params=params(58),
        cost_estimate=cost(4.3e9, 1.6e6),
        name="columns",
    )(angles, cur)
    if share_v != CHUNK:
        plane = plane.reshape(2, chunks, 2, wide, CHUNK // share_v, share_v)
        plane = plane.transpose(0, 1, 4, 2, 3, 5).reshape(1, 2, tile_count, 2, wide, share_v)
        plane = jnp.broadcast_to(plane, (pairs,) + plane.shape[1:])
    plane = plane.reshape(devices, 2, wide, share_v)

    row_angles, owner, slot, target, weight, plane = lax.optimization_barrier(
        (row_angles, tile_owner, face_slot, target, weight, plane)
    )
    got = lax.all_to_all(plane, BOTH, 0, 0, tiled=True)
    here = lax.axis_index("row")
    core = here % 2
    swap = [(i, i ^ 1) for i in range(row_count)]
    code = owner[:, 0] * points + slot
    code = jnp.stack([code, lax.ppermute(code, "tile", mirror)], axis=1)
    own_angles = jnp.stack(
        [lax.dynamic_slice_in_dim(row_angles, i * share_u, share_u) for i in (here, here ^ 1)]
    )
    own, far = [], []
    for array in (target, weight):
        own.append(lax.dynamic_index_in_dim(array, core, 0, keepdims=False))
        other = lax.dynamic_index_in_dim(array, 1 - core, 0, keepdims=False)
        far.append(lax.ppermute(other, "row", swap))
    row_table = pl.pallas_call(
        functools.partial(row_kernel, columns, rows_dev),
        grid=(1,),
        in_specs=[whole((2, share_u))],
        out_specs=whole((2, depth, 2 * share_u)),
        out_shape=jax.ShapeDtypeStruct((2, depth, 2 * share_u), BF),
        compiler_params=params(),
        cost_estimate=cost(1e8, 5e5),
        name="rows",
    )(own_angles)

    far_shape = (share_v, share_u)
    back_shape = (row_count, 2, tile_half, 2, 2, wide, share_v)
    power, far_power, back = pl.pallas_call(
        middle_kernel,
        grid=(1,),
        in_specs=[whole((2, depth, 2 * share_u)), whole((devices, 2, wide, share_v))]
        + [whole(far_shape)] * 4,
        out_specs=[whole(far_shape), whole(far_shape), whole(back_shape)],
        out_shape=[
            jax.ShapeDtypeStruct(far_shape, F32),
            jax.ShapeDtypeStruct(far_shape, F32),
            jax.ShapeDtypeStruct(back_shape, BF),
        ],
        compiler_params=params(),
        cost_estimate=cost(1.1e9, 5e6),
        name="objective",
    )(row_table, got, own[0], far[0], own[1], far[1])

    angles, code, back = lax.optimization_barrier((angles, code, back))
    back = back.reshape(devices, 2, 2, wide, share_v)
    back = lax.all_to_all(back, BOTH, 0, 0, tiled=True)
    far_power = lax.ppermute(far_power, "row", swap)
    intensity = jnp.where(
        core == 0, jnp.stack([power, far_power]), jnp.stack([far_power, power])
    )
    table, turn, choose, mark = pl.pallas_call(
        functools.partial(prepare_kernel, columns, rows_dev, tile_count, cap),
        grid=(chunks,),
        in_specs=[angle_spec, whole((points, 2))],
        out_specs=[
            table_spec,
            turn_spec,
            whole((2, slots, points)),
            whole((units, PACK // 2, SEG)),
        ],
        out_shape=[
            jax.ShapeDtypeStruct((8 * chunks, 4 * SEG, 2 * CHUNK), BF),
            jax.ShapeDtypeStruct((16 * chunks, 2, half, CHUNK), F32),
            jax.ShapeDtypeStruct((2, slots, points), BF),
            jax.ShapeDtypeStruct((units, PACK // 2, SEG), BF),
        ],
        compiler_params=params(40),
        cost_estimate=cost(4e9, 8e6),
        name="prepare",
    )(angles, code)
    intensity, mark = lax.optimization_barrier((intensity, mark))

    back = back.reshape(pairs, 2, tile_count, 2, 2, wide, share_v)
    if share_v != CHUNK:
        back = back.reshape(pairs, 2, chunks, CHUNK // share_v, 2, 2, wide, share_v)
        back = back.transpose(0, 1, 2, 4, 5, 6, 3, 7).reshape(pairs, 2, chunks, 2, 2, wide, CHUNK)
    outgoing = pl.pallas_call(
        adjoint_kernel,
        grid=(chunks,),
        in_specs=[
            pl.BlockSpec((pairs, 2, 1, 2, 2, wide, CHUNK), lambda i: (0, 0, i, 0, 0, 0, 0)),
            table_spec,
            turn_spec,
            whole((2, slots, points)),
            whole((units, PACK // 2, SEG)),
        ],
        out_specs=whole((units, held, SEG)),
        out_shape=jax.ShapeDtypeStruct((units, held, SEG), BF),
        scratch_shapes=[pltpu.VMEM((8 * half, 4 * SEG), F32)],
        compiler_params=params(40),
        cost_estimate=cost(8.6e9, 8e6),
        name="adjoint",
    )(back, table, turn, choose, mark)

    if cap == PACK:
        arrived = lax.all_to_all(outgoing, BOTH, 0, 0, tiled=True, axis_index_groups=half_groups)
    else:
        arrived = exchange_small(outgoing, half_groups, cap)
    out_shape = (freq_count, comp_count, part_count, points, SEG)
    faces = pl.pallas_call(
        faces_kernel,
        grid=(1,),
        in_specs=[whole((units, held, SEG))],
        out_specs=whole(out_shape),
        out_shape=jax.ShapeDtypeStruct(out_shape, F32),
        compiler_params=params(),
        name="faces",
    )(arrived)
    return (intensity, faces)


def solution(mesh):
    in_specs = (
        P(None, None, None, ("row", "tile"), None),
        P(),
        P(),
        P(None, "tile", "row"),
        P(None, "tile", "row"),
        P(("row", "tile"), None),
        P(("row", "tile")),
    )
    out_specs = (P(None, "tile", "row"), P(None, None, None, ("row", "tile"), None))
    return jax.shard_map(body, mesh=mesh, in_specs=in_specs, out_specs=out_specs, check_vma=False)
```

```python
import functools
import math

import jax
import jax.numpy as jnp
from jax import lax
from jax.experimental import pallas as pl
from jax.experimental.pallas import tpu as pltpu
from jax.sharding import PartitionSpec as P

SEG = 128
CHUNK = 256
PACK = 16
BOTH = ("row", "tile")
BF = jnp.bfloat16
F32 = jnp.float32


def cos_sin(turns, quarter, scale):
    bits = int(math.log2(quarter))
    turns = turns & (4 * quarter - 1)
    octant = (turns + quarter // 2) >> bits
    angle = (turns - (octant << bits)).astype(F32) * (math.pi / (2 * quarter))
    square = angle * angle
    sin_part = angle * scale + (angle * scale) * square * (
        -1.6666654611e-1 + square * (8.3321608736e-3 - square * 1.9515295891e-4)
    )
    cos_part = scale - square * (0.5 * scale) + (square * scale) * square * (
        4.166664568298827e-2 + square * (-1.388731625493765e-3 + square * 2.443315711809948e-5)
    )
    swap = (octant & 1) == 1
    cos_out = jnp.where(swap, sin_part, cos_part)
    sin_out = jnp.where(swap, cos_part, sin_part)
    cos_out = jnp.where(((octant + 1) & 2) == 2, -cos_out, cos_out)
    sin_out = jnp.where((octant & 2) == 2, -sin_out, sin_out)
    return cos_out, sin_out


def iota(shape, dim):
    return lax.broadcasted_iota(jnp.int32, shape, dim)


def turned(cos_0, sin_0, cos_1, sin_1):
    rows, width = cos_0.shape
    cos_out, sin_out = [], []
    for j in range(cos_1.shape[0]):
        cos_j = jnp.broadcast_to(cos_1[j:j + 1], (rows, width))
        sin_j = jnp.broadcast_to(sin_1[j:j + 1], (rows, width))
        cos_out.append(cos_0 * cos_j - sin_0 * sin_j)
        sin_out.append(sin_0 * cos_j + cos_0 * sin_j)
    return jnp.concatenate(cos_out, axis=0), jnp.concatenate(sin_out, axis=0)


def middle(quarter):
    return quarter // 2 + SEG - 1


def fine_table(quarter, angles):
    width = angles.shape[-1]
    start = quarter - middle(quarter) + iota((SEG // 8, width), 0) * 16
    cos_0, sin_0 = cos_sin(2 * iota((8, width), 0) * angles, 2 * quarter, 1.0 / math.sqrt(quarter))
    cos_1, sin_1 = cos_sin(start * angles, 2 * quarter, 1.0)
    return jnp.concatenate(turned(cos_0, sin_0, cos_1, sin_1), axis=0).astype(BF)


def coarse_table(quarter, rows_dev, angles):
    width = angles.shape[-1]
    tiles = quarter // SEG // 2
    group = 8 // rows_dev
    base = (iota((8, width), 0) // rows_dev) * (2 * SEG)
    start = iota((tiles // group, width), 0) * (2 * group * SEG) + middle(quarter)
    cos_0, sin_0 = cos_sin(base * angles, 2 * quarter, 1.0)
    cos_1, sin_1 = cos_sin(start * angles, 2 * quarter, 1.0)
    return turned(cos_0, sin_0, cos_1, sin_1)


def mirrored(block):
    flip = jnp.where(iota((SEG, SEG), 0) + iota((SEG, SEG), 1) == SEG - 1, 1.0, 0.0).astype(BF)
    return jnp.dot(block, flip, preferred_element_type=F32)


def forward_kernel(quarter, rows_dev, angle_ref, cur_hbm, f_ref, cur_ref, lhs, fine, coarse, sem):
    points = rows_dev * quarter // SEG // 2
    chunks, width = angle_ref.shape[0], angle_ref.shape[-1]
    load = pltpu.make_async_copy(cur_hbm, cur_ref, sem)
    load.start()
    for i in range(chunks):
        fine[i] = fine_table(quarter, angle_ref[i])
        coarse[i, 0], coarse[i, 1] = coarse_table(quarter, rows_dev, angle_ref[i])
    load.wait()
    low_half, high_half = pl.ds(0, points), pl.ds(points, points)
    for f in range(2):
        even, odd = [], []
        for c in range(2):
            right = [cur_ref[f, k, c, high_half, :].astype(F32) for k in range(4)]
            left = [mirrored(cur_ref[f, k, c, low_half, :]) for k in range(4)]
            right = [right[0] + right[3], right[1] - right[2]]
            left = [left[0] + left[3], left[1] - left[2]]
            even.append([i + j for i, j in zip(right, left)])
            odd.append([i - j for i, j in zip(right, left)])
        for p in range(2):
            real = pl.ds((2 * f + p) * points, points)
            imag = pl.ds((4 + 2 * f + p) * points, points)
            lhs[real, :SEG] = even[0][p].astype(BF)
            lhs[real, SEG:] = odd[1][p].astype(BF)
            lhs[imag, :SEG] = even[1][p].astype(BF)
            lhs[imag, SEG:] = (-odd[0][p]).astype(BF)
    low = iota((8, width), 0) < 4
    for i in range(chunks):
        grid_sum = jnp.dot(lhs[...], fine[i], preferred_element_type=F32)
        cos_a, sin_a = coarse[i, 0], coarse[i, 1]
        for f, p in [(i, j) for i in range(2) for j in range(2)]:
            start = (2 * f + p) * points
            real = grid_sum[start:start + points]
            imag = grid_sum[4 * points + start:5 * points + start]
            out_re = jnp.sum((real * cos_a + imag * sin_a).reshape(points // 8, 8, width), axis=0)
            out_im = jnp.sum((imag * cos_a - real * sin_a).reshape(points // 8, 8, width), axis=0)
            out_re = out_re + pltpu.roll(out_re, 4, 0)
            out_im = out_im + pltpu.roll(out_im, 4, 0)
            out = jnp.where(low, out_re, out_im).astype(BF)
            for copy in range(f_ref.shape[0]):
                f_ref[copy, f, i, p] = out


def row_kernel(quarter, rows_dev, row_ref, r_ref):
    sides, depth = r_ref.shape[:2]
    share_u = row_ref.shape[-1]
    row = iota((depth, share_u), 0)
    x = (row // (2 * rows_dev)) * rows_dev + row % rows_dev
    is_imag = row % (2 * rows_dev) >= rows_dev
    scale = 1.0 / math.sqrt(depth // 2)
    for side in range(sides):
        cos_x, sin_x = cos_sin(x * row_ref[side:side + 1], quarter, scale)
        r_ref[side, :, :share_u] = jnp.where(is_imag, sin_x, cos_x).astype(BF)
        r_ref[side, :, share_u:] = jnp.where(is_imag, cos_x, -sin_x).astype(BF)


def prepare_kernel(quarter, rows_dev, tile_count, cap, angle_ref, code_ref, w_ref, choose_ref, mark_ref):
    points = code_ref.shape[0]
    slots, units = choose_ref.shape[1], mark_ref.shape[0]
    for i in range(angle_ref.shape[0]):
        w_ref[i] = fine_table(quarter, angle_ref[i])
    segs = points // rows_dev
    half = tile_count // 2
    mine = lax.axis_index("tile") // half
    point = iota((points, points), 1)
    point = (point % rows_dev) * segs + (point // rows_dev)
    source = iota((points, points), 0)
    lane = iota((PACK // 2, SEG), 1) // (SEG // 4)
    marked = jnp.zeros((units, PACK // 2, SEG), jnp.int32)
    for side in range(2):
        code_col = code_ref[:, side:side + 1]
        code_row = jnp.sum(jnp.where(source == point, code_col, 0), axis=0, keepdims=True)
        owner_col, owner_row = code_col // points, code_row // points
        same = jnp.where((source < point) & (owner_col == owner_row), 1, 0)
        rank = jnp.sum(same, axis=0, keepdims=True)
        tile = owner_row % tile_count
        place = ((owner_row // tile_count) * half + tile % half) * cap + rank
        place = jnp.where(tile // half == mine, place, -1)
        hit = iota((slots, points), 0) == place
        choose_ref[side] = jnp.where(hit, 1.0, 0.0).astype(BF)
        marks = jnp.sum(jnp.where(hit, code_row % points + 1, 0), axis=1, keepdims=True)
        marks = jnp.broadcast_to(marks, (slots, SEG)).reshape(units, 2, PACK // 2, SEG)
        for part in range(2):
            marked = jnp.where(lane == 2 * side + part, marks[:, part], marked)
    mark_ref[...] = marked.astype(F32).astype(BF)


def middle_kernel(
    table, got_ref, target_ref, far_target_ref, weight_ref, far_weight_ref, int_ref, far_int_ref, back_ref
):
    devices, pols, rows, share_v = got_ref.shape
    depth = devices * rows
    share_u = table.shape[2] // 2
    core = lax.axis_index("row") % 2
    planes = [
        got_ref[:, p].astype(F32).reshape(depth, share_v).astype(BF) for p in range(pols)
    ]
    sums = [None, None]
    sides = [
        (target_ref, weight_ref, int_ref), (far_target_ref, far_weight_ref, far_int_ref)
    ]
    for side, (goal_ref, gain_ref, power_ref) in enumerate(sides):
        mixed = [
            lax.dot_general(
                plane, table[side], (((0,), (0,)), ((), ())), preferred_element_type=F32
            )
            for plane in planes
        ]
        power = mixed[0] * mixed[0] + mixed[1] * mixed[1]
        intensity = power[:, :share_u] + power[:, share_u:]
        power_ref[...] = intensity
        factor = 4.0 * gain_ref[core] * (intensity - goal_ref[core])
        factor = jnp.concatenate([factor, factor], axis=1)
        for p in range(pols):
            far_grad = (factor * mixed[p]).astype(BF)
            back = lax.dot_general(
                table[side], far_grad, (((1,), (1,)), ((), ())), preferred_element_type=F32
            )
            sums[p] = back if side == 0 else sums[p] + back
    groups, halves, count = back_ref.shape[:3]
    for p in range(pols):
        total = sums[p].reshape(groups, halves, count, rows, share_v).astype(BF)
        for half in range(halves):
            back_ref[:, half, :, 0, p] = total[:, half]
            back_ref[:, 1 - half, :, 1, p] = total[:, half]


def adjoint_kernel(quarter, rows_dev, got_ref, w_ref, angle_ref, choose_ref, mark_ref, out_ref, total):
    chunks, width = w_ref.shape[0], w_ref.shape[2]
    points = choose_ref.shape[2] // 2
    units = out_ref.shape[0]
    low = iota((8, width), 0) < 4
    for i in range(chunks):
        cos_a, sin_a = coarse_table(quarter, rows_dev, angle_ref[i])
        reals, imags = [], []
        for side, f, p in [(i, j, k) for i in range(2) for j in range(2) for k in range(2)]:
            plane = jnp.sum(got_ref[:, f, i, side, p].astype(F32), axis=0)
            other = pltpu.roll(plane, 4, 0)
            real = jnp.where(low, plane, other)
            imag = jnp.where(low, other, plane)
            real = jnp.broadcast_to(real[None], (points // 8, 8, width)).reshape(points, width)
            imag = jnp.broadcast_to(imag[None], (points // 8, 8, width)).reshape(points, width)
            reals.append((cos_a * real - sin_a * imag).astype(BF))
            imags.append((cos_a * imag + sin_a * real).astype(BF))
        found = lax.dot_general(
            jnp.concatenate(reals + imags, axis=0), w_ref[i], (((1,), (1,)), ((), ())),
            preferred_element_type=F32,
        )
        if i == 0:
            total[...] = found
        else:
            total[...] += found
    for side, fp in [(i, j) for i in range(2) for j in range(4)]:
        start = (4 * side + fp) * points
        real = total[start:start + points, :]
        imag = total[8 * points + start:9 * points + start, :]
        real_cos, real_sin, imag_cos, imag_sin = (
            real[:, :SEG], real[:, SEG:], imag[:, :SEG], imag[:, SEG:]
        )
        left = [
            mirrored((real_cos + imag_sin).astype(BF)).astype(BF),
            mirrored((imag_cos - real_sin).astype(BF)).astype(BF),
        ]
        right = [(real_cos - imag_sin).astype(BF), (imag_cos + real_sin).astype(BF)]
        block = jnp.concatenate(
            [jnp.concatenate(left, axis=1), jnp.concatenate(right, axis=1)], axis=0
        )
        sent = jnp.dot(choose_ref[side], block, preferred_element_type=F32).astype(BF)
        sent = sent.reshape(units, PACK, 2 * SEG)
        for c in range(2):
            rows = pl.ds((8 * side + 2 * fp + c) * PACK, PACK)
            out_ref[:, rows, :] = sent[:, :, c * SEG:(c + 1) * SEG]
    out_ref[:, 16 * PACK:, :] = mark_ref[...]


def faces_kernel(got_ref, out_ref):
    faces = out_ref.shape[3]
    units = got_ref.shape[0]
    slots = units * PACK
    marks = got_ref[:, 16 * PACK:, :].astype(F32)
    hits = []
    for side in range(2):
        spots = [(2 * side + part) * (SEG // 4) for part in range(2)]
        mark = jnp.concatenate([marks[:, :, i:i + 1] for i in spots], axis=1)
        mark = jnp.broadcast_to(mark.reshape(slots, 1), (slots, faces)).astype(jnp.int32)
        hits.append(jnp.where(iota((slots, faces), 1) + 1 == mark, 1.0, 0.0).astype(BF))
    choose = jnp.concatenate(hits, axis=0)
    for f in range(2):
        for p in range(2):
            for c in range(2):
                blocks = []
                for side in range(2):
                    rows = pl.ds((8 * side + 4 * f + 2 * p + c) * PACK, PACK)
                    blocks.append(got_ref[:, rows, :].reshape(slots, SEG))
                found = lax.dot_general(
                    choose, jnp.concatenate(blocks, axis=0), (((0,), (0,)), ((), ())),
                    preferred_element_type=F32,
                )
                if p == 0:
                    out_ref[f, 0, c] = found
                    out_ref[f, 3, c] = found
                else:
                    out_ref[f, 1, c] = found
                    out_ref[f, 2, c] = -found


def exchange_small(outgoing, groups, cap):
    units = outgoing.shape[0]
    peers = units * PACK // cap
    swap = functools.partial(
        lax.all_to_all, axis_name=BOTH, split_axis=1, concat_axis=1, tiled=True, axis_index_groups=groups
    )
    rows = outgoing[:, :16 * PACK].reshape(units, 16, PACK, SEG).transpose(1, 0, 2, 3)
    rows = swap(rows.reshape(16, peers, cap, SEG))
    rows = rows.reshape(16, units, PACK, SEG).transpose(1, 0, 2, 3).reshape(units, 16 * PACK, SEG)
    marks = outgoing[:, 16 * PACK:, ::SEG // 4].reshape(units, PACK // 2, 2, 2).transpose(2, 0, 3, 1)
    marks = swap(marks.reshape(2, peers, cap)).reshape(2, units, 2, PACK // 2)
    marks = marks.transpose(1, 3, 0, 2).reshape(units, PACK // 2, 4)
    return jnp.concatenate([rows, jnp.repeat(marks, SEG // 4, axis=2)], axis=1)


def params(mib=24):
    return pltpu.CompilerParams(
        dimension_semantics=("arbitrary",), vmem_limit_bytes=mib * 1024 * 1024
    )


def cost(flops, moved):
    return pl.CostEstimate(flops=int(flops), bytes_accessed=int(moved), transcendentals=0)


def whole(shape):
    return pl.BlockSpec(shape, lambda i: (0,) * len(shape))


def body(currents, row_angles, column_angles, target, weight, tile_owner, face_slot):
    row_count = lax.axis_size("row")
    tile_count = lax.axis_size("tile")
    devices = row_count * tile_count
    freq_count, comp_count, part_count, rows_dev, columns = currents.shape
    far_rows = row_angles.shape[0]
    far_cols = column_angles.shape[0]
    share_v = far_cols // tile_count
    share_u = far_rows // row_count
    chunks = far_cols // CHUNK
    tiles = columns // SEG
    points = rows_dev * tiles
    half = points // 2
    cap = 2 * points // devices
    slots = points
    units = slots // PACK
    held = 16 * PACK + PACK // 2
    pairs = row_count // 2
    wide = 2 * rows_dev
    depth = devices * wide
    tile_half = tile_count // 2
    half_groups = [
        [r * tile_count + side * tile_half + t for r in range(row_count) for t in range(tile_half)]
        for side in range(2)
    ]
    mirror = [(i, (i + tile_half) % tile_count) for i in range(tile_count)]
    angles = column_angles.reshape(chunks, 1, CHUNK)
    cur = currents.reshape(freq_count, comp_count, part_count, rows_dev, tiles, SEG)
    cur = cur.transpose(0, 1, 2, 4, 3, 5).reshape(freq_count, comp_count, part_count, points, SEG)
    copies = pairs if share_v == CHUNK else 1
    plane = pl.pallas_call(
        functools.partial(forward_kernel, columns, rows_dev),
        grid=(1,),
        in_specs=[whole(angles.shape), pl.BlockSpec(memory_space=pltpu.HBM)],
        out_specs=whole((copies, 2, chunks, 2, wide, CHUNK)),
        out_shape=jax.ShapeDtypeStruct((copies, 2, chunks, 2, wide, CHUNK), BF),
        scratch_shapes=[
            pltpu.VMEM(cur.shape, BF),
            pltpu.VMEM((8 * half, 2 * SEG), BF),
            pltpu.VMEM((chunks, 2 * SEG, CHUNK), BF),
            pltpu.VMEM((chunks, 2, half, CHUNK), F32),
            pltpu.SemaphoreType.DMA(()),
        ],
        compiler_params=params(58),
        cost_estimate=cost(4.3e9, 1.6e6),
        name="columns",
    )(angles, cur)
    if share_v != CHUNK:
        plane = plane.reshape(2, chunks, 2, wide, CHUNK // share_v, share_v)
        plane = plane.transpose(0, 1, 4, 2, 3, 5).reshape(1, 2, tile_count, 2, wide, share_v)
        plane = jnp.broadcast_to(plane, (pairs,) + plane.shape[1:])
    plane = plane.reshape(devices, 2, wide, share_v)

    row_angles, owner, slot, plane = lax.optimization_barrier(
        (row_angles, tile_owner, face_slot, plane)
    )
    got = lax.all_to_all(plane, BOTH, 0, 0, tiled=True)
    here = lax.axis_index("row")
    core = here % 2
    swap = [(i, i ^ 1) for i in range(row_count)]
    code = owner[:, 0] * points + slot
    code = jnp.stack([code, lax.ppermute(code, "tile", mirror)], axis=1)
    own_angles = jnp.stack(
        [lax.dynamic_slice_in_dim(row_angles, i * share_u, share_u) for i in (here, here ^ 1)]
    )
    far_target = lax.ppermute(target, "row", swap)
    far_weight = lax.ppermute(weight, "row", swap)
    row_table = pl.pallas_call(
        functools.partial(row_kernel, columns, rows_dev),
        grid=(1,),
        in_specs=[whole((2, share_u))],
        out_specs=whole((2, depth, 2 * share_u)),
        out_shape=jax.ShapeDtypeStruct((2, depth, 2 * share_u), BF),
        compiler_params=params(),
        cost_estimate=cost(1e8, 5e5),
        name="rows",
    )(own_angles)

    far_shape = (share_v, share_u)
    back_shape = (row_count, 2, tile_half, 2, 2, wide, share_v)
    power, far_power, back = pl.pallas_call(
        middle_kernel,
        grid=(1,),
        in_specs=[whole((2, depth, 2 * share_u)), whole((devices, 2, wide, share_v))]
        + [whole(target.shape)] * 4,
        out_specs=[whole(far_shape), whole(far_shape), whole(back_shape)],
        out_shape=[
            jax.ShapeDtypeStruct(far_shape, F32),
            jax.ShapeDtypeStruct(far_shape, F32),
            jax.ShapeDtypeStruct(back_shape, BF),
        ],
        compiler_params=params(),
        cost_estimate=cost(1.1e9, 5e6),
        name="objective",
    )(row_table, got, target, far_target, weight, far_weight)

    angles, code, back = lax.optimization_barrier((angles, code, back))
    back = back.reshape(devices, 2, 2, wide, share_v)
    back = lax.all_to_all(back, BOTH, 0, 0, tiled=True)
    table, choose, mark = pl.pallas_call(
        functools.partial(prepare_kernel, columns, rows_dev, tile_count, cap),
        grid=(1,),
        in_specs=[whole(angles.shape), whole((points, 2))],
        out_specs=[
            whole((chunks, 2 * SEG, CHUNK)),
            whole((2, slots, points)),
            whole((units, PACK // 2, SEG)),
        ],
        out_shape=[
            jax.ShapeDtypeStruct((chunks, 2 * SEG, CHUNK), BF),
            jax.ShapeDtypeStruct((2, slots, points), BF),
            jax.ShapeDtypeStruct((units, PACK // 2, SEG), BF),
        ],
        compiler_params=params(),
        cost_estimate=cost(1e9, 2e6),
        name="prepare",
    )(angles, code)
    far_power, mark = lax.optimization_barrier((far_power, mark))
    far_power = lax.ppermute(far_power, "row", swap)
    intensity = jnp.where(
        core == 0, jnp.stack([power, far_power]), jnp.stack([far_power, power])
    )
    intensity, mark = lax.optimization_barrier((intensity, mark))

    back = back.reshape(pairs, 2, tile_count, 2, 2, wide, share_v)
    if share_v != CHUNK:
        back = back.reshape(pairs, 2, chunks, CHUNK // share_v, 2, 2, wide, share_v)
        back = back.transpose(0, 1, 2, 4, 5, 6, 3, 7).reshape(pairs, 2, chunks, 2, 2, wide, CHUNK)
    outgoing = pl.pallas_call(
        functools.partial(adjoint_kernel, columns, rows_dev),
        grid=(1,),
        in_specs=[
            whole((pairs, 2, chunks, 2, 2, wide, CHUNK)),
            whole((chunks, 2 * SEG, CHUNK)),
            whole(angles.shape),
            whole((2, slots, points)),
            whole((units, PACK // 2, SEG)),
        ],
        out_specs=whole((units, held, SEG)),
        out_shape=jax.ShapeDtypeStruct((units, held, SEG), BF),
        scratch_shapes=[pltpu.VMEM((16 * half, 2 * SEG), F32)],
        compiler_params=params(),
        cost_estimate=cost(4.3e9, 4e6),
        name="adjoint",
    )(back, table, angles, choose, mark)

    if cap == PACK:
        arrived = lax.all_to_all(outgoing, BOTH, 0, 0, tiled=True, axis_index_groups=half_groups)
    else:
        arrived = exchange_small(outgoing, half_groups, cap)
    out_shape = (freq_count, comp_count, part_count, points, SEG)
    faces = pl.pallas_call(
        faces_kernel,
        grid=(1,),
        in_specs=[whole((units, held, SEG))],
        out_specs=whole(out_shape),
        out_shape=jax.ShapeDtypeStruct(out_shape, F32),
        compiler_params=params(),
        name="faces",
    )(arrived)
    return (intensity, faces)


def solution(mesh):
    in_specs = (
        P(None, None, None, ("row", "tile"), None),
        P(),
        P(),
        P(None, "tile", "row"),
        P(None, "tile", "row"),
        P(("row", "tile"), None),
        P(("row", "tile")),
    )
    out_specs = (P(None, "tile", "row"), P(None, None, None, ("row", "tile"), None))
    return jax.shard_map(body, mesh=mesh, in_specs=in_specs, out_specs=out_specs, check_vma=False)
```

```python
import functools
import math

import jax
import jax.numpy as jnp
from jax import lax
from jax.experimental import pallas as pl
from jax.experimental.pallas import tpu as pltpu
from jax.sharding import PartitionSpec as P

SEG = 128
CHUNK = 256
PACK = 16
BOTH = ("row", "tile")
BF = jnp.bfloat16
F32 = jnp.float32


def cos_sin(turns, quarter, scale):
    bits = int(math.log2(quarter))
    turns = turns & (4 * quarter - 1)
    octant = (turns + quarter // 2) >> bits
    angle = (turns - (octant << bits)).astype(F32) * (math.pi / (2 * quarter))
    square = angle * angle
    sin_part = angle * scale + (angle * scale) * square * (
        -1.6666654611e-1 + square * (8.3321608736e-3 - square * 1.9515295891e-4)
    )
    cos_part = scale - square * (0.5 * scale) + (square * scale) * square * (
        4.166664568298827e-2 + square * (-1.388731625493765e-3 + square * 2.443315711809948e-5)
    )
    swap = (octant & 1) == 1
    cos_out = jnp.where(swap, sin_part, cos_part)
    sin_out = jnp.where(swap, cos_part, sin_part)
    cos_out = jnp.where(((octant + 1) & 2) == 2, -cos_out, cos_out)
    sin_out = jnp.where((octant & 2) == 2, -sin_out, sin_out)
    return cos_out, sin_out


def iota(shape, dim):
    return lax.broadcasted_iota(jnp.int32, shape, dim)


def turned(cos_0, sin_0, cos_1, sin_1):
    rows, width = cos_0.shape
    cos_out, sin_out = [], []
    for j in range(cos_1.shape[0]):
        cos_j = jnp.broadcast_to(cos_1[j:j + 1], (rows, width))
        sin_j = jnp.broadcast_to(sin_1[j:j + 1], (rows, width))
        cos_out.append(cos_0 * cos_j - sin_0 * sin_j)
        sin_out.append(sin_0 * cos_j + cos_0 * sin_j)
    return jnp.concatenate(cos_out, axis=0), jnp.concatenate(sin_out, axis=0)


def middle(quarter):
    return quarter // 2 + SEG - 1


def fine_table(quarter, angles):
    width = angles.shape[-1]
    start = quarter - middle(quarter) + iota((SEG // 8, width), 0) * 16
    cos_0, sin_0 = cos_sin(2 * iota((8, width), 0) * angles, 2 * quarter, 1.0 / math.sqrt(quarter))
    cos_1, sin_1 = cos_sin(start * angles, 2 * quarter, 1.0)
    return jnp.concatenate(turned(cos_0, sin_0, cos_1, sin_1), axis=0).astype(BF)


def coarse_table(quarter, rows_dev, angles):
    width = angles.shape[-1]
    tiles = quarter // SEG // 2
    group = 8 // rows_dev
    base = (iota((8, width), 0) // rows_dev) * (2 * SEG)
    start = iota((tiles // group, width), 0) * (2 * group * SEG) + middle(quarter)
    cos_0, sin_0 = cos_sin(base * angles, 2 * quarter, 1.0)
    cos_1, sin_1 = cos_sin(start * angles, 2 * quarter, 1.0)
    return turned(cos_0, sin_0, cos_1, sin_1)


def mirrored(block):
    flip = jnp.where(iota((SEG, SEG), 0) + iota((SEG, SEG), 1) == SEG - 1, 1.0, 0.0).astype(BF)
    return jnp.dot(block, flip, preferred_element_type=F32)


def forward_kernel(quarter, rows_dev, angle_ref, cur_hbm, f_ref, cur_ref, lhs, fine, coarse, sem):
    points = rows_dev * quarter // SEG // 2
    chunks, width = angle_ref.shape[0], angle_ref.shape[-1]
    loads = [
        [pltpu.make_async_copy(cur_hbm.at[f, k], cur_ref.at[f, k], sem.at[f, k]) for k in range(4)]
        for f in range(2)
    ]
    for load in loads[0] + loads[1]:
        load.start()
    for i in range(chunks):
        fine[i] = fine_table(quarter, angle_ref[i])
        coarse[i, 0], coarse[i, 1] = coarse_table(quarter, rows_dev, angle_ref[i])
    low_half, high_half = pl.ds(0, points), pl.ds(points, points)
    for f in range(2):
        for load in loads[f]:
            load.wait()
        even, odd = [], []
        for c in range(2):
            right = [cur_ref[f, k, c, high_half, :].astype(F32) for k in range(4)]
            left = [mirrored(cur_ref[f, k, c, low_half, :]) for k in range(4)]
            right = [right[0] + right[3], right[1] - right[2]]
            left = [left[0] + left[3], left[1] - left[2]]
            even.append([i + j for i, j in zip(right, left)])
            odd.append([i - j for i, j in zip(right, left)])
        for p in range(2):
            real = pl.ds((2 * f + p) * points, points)
            imag = pl.ds((4 + 2 * f + p) * points, points)
            lhs[real, :SEG] = even[0][p].astype(BF)
            lhs[real, SEG:] = odd[1][p].astype(BF)
            lhs[imag, :SEG] = even[1][p].astype(BF)
            lhs[imag, SEG:] = (-odd[0][p]).astype(BF)
    low = iota((8, width), 0) < 4
    for i in range(chunks):
        grid_sum = jnp.dot(lhs[...], fine[i], preferred_element_type=F32)
        cos_a, sin_a = coarse[i, 0], coarse[i, 1]
        for f, p in [(i, j) for i in range(2) for j in range(2)]:
            start = (2 * f + p) * points
            real = grid_sum[start:start + points]
            imag = grid_sum[4 * points + start:5 * points + start]
            out_re = jnp.sum((real * cos_a + imag * sin_a).reshape(points // 8, 8, width), axis=0)
            out_im = jnp.sum((imag * cos_a - real * sin_a).reshape(points // 8, 8, width), axis=0)
            out_re = out_re + pltpu.roll(out_re, 4, 0)
            out_im = out_im + pltpu.roll(out_im, 4, 0)
            out = jnp.where(low, out_re, out_im).astype(BF)
            for copy in range(f_ref.shape[0]):
                f_ref[copy, f, i, p] = out


def row_kernel(quarter, rows_dev, row_ref, r_ref):
    sides, depth = r_ref.shape[:2]
    share_u = row_ref.shape[-1]
    row = iota((depth, share_u), 0)
    x = (row // (2 * rows_dev)) * rows_dev + row % rows_dev
    is_imag = row % (2 * rows_dev) >= rows_dev
    scale = 1.0 / math.sqrt(depth // 2)
    for side in range(sides):
        cos_x, sin_x = cos_sin(x * row_ref[side:side + 1], quarter, scale)
        r_ref[side, :, :share_u] = jnp.where(is_imag, sin_x, cos_x).astype(BF)
        r_ref[side, :, share_u:] = jnp.where(is_imag, cos_x, -sin_x).astype(BF)


def prepare_kernel(
    quarter, rows_dev, tile_count, cap, angle_ref, code_ref, power_ref, far_power_ref,
    w_ref, choose_ref, mark_ref, int_ref,
):
    core = lax.axis_index("row") % 2
    int_ref[core] = power_ref[0]
    int_ref[1 - core] = far_power_ref[...]
    points = code_ref.shape[0]
    slots, units = choose_ref.shape[1], mark_ref.shape[0]
    for i in range(angle_ref.shape[0]):
        w_ref[i] = fine_table(quarter, angle_ref[i])
    segs = points // rows_dev
    half = tile_count // 2
    mine = lax.axis_index("tile") // half
    point = iota((points, points), 1)
    point = (point % rows_dev) * segs + (point // rows_dev)
    source = iota((points, points), 0)
    lane = iota((PACK // 2, SEG), 1) // (SEG // 4)
    marked = jnp.zeros((units, PACK // 2, SEG), jnp.int32)
    for side in range(2):
        code_col = code_ref[:, side:side + 1]
        code_row = jnp.sum(jnp.where(source == point, code_col, 0), axis=0, keepdims=True)
        owner_col, owner_row = code_col // points, code_row // points
        same = jnp.where((source < point) & (owner_col == owner_row), 1, 0)
        rank = jnp.sum(same, axis=0, keepdims=True)
        tile = owner_row % tile_count
        place = ((owner_row // tile_count) * half + tile % half) * cap + rank
        place = jnp.where(tile // half == mine, place, -1)
        hit = iota((slots, points), 0) == place
        choose_ref[side] = jnp.where(hit, 1.0, 0.0).astype(BF)
        marks = jnp.sum(jnp.where(hit, code_row % points + 1, 0), axis=1, keepdims=True)
        marks = jnp.broadcast_to(marks, (slots, SEG)).reshape(units, 2, PACK // 2, SEG)
        for part in range(2):
            marked = jnp.where(lane == 2 * side + part, marks[:, part], marked)
    mark_ref[...] = marked.astype(F32).astype(BF)


def middle_kernel(
    table, got_ref, target_ref, far_target_ref, weight_ref, far_weight_ref,
    power_hbm, back_ref, powers, sems,
):
    devices, pols, rows, share_v = got_ref.shape
    depth = devices * rows
    share_u = table.shape[2] // 2
    core = lax.axis_index("row") % 2
    planes = [
        got_ref[:, p].astype(F32).reshape(depth, share_v).astype(BF) for p in range(pols)
    ]
    sums = [None, None]
    stores = []
    sides = [(target_ref, weight_ref), (far_target_ref, far_weight_ref)]
    for side, (goal_ref, gain_ref) in enumerate(sides):
        mixed = [
            lax.dot_general(
                plane, table[side], (((0,), (0,)), ((), ())), preferred_element_type=F32
            )
            for plane in planes
        ]
        power = mixed[0] * mixed[0] + mixed[1] * mixed[1]
        intensity = power[:, :share_u] + power[:, share_u:]
        powers[side] = intensity
        stores.append(pltpu.make_async_copy(powers.at[side], power_hbm.at[side], sems.at[side]))
        stores[-1].start()
        factor = 4.0 * gain_ref[core] * (intensity - goal_ref[core])
        factor = jnp.concatenate([factor, factor], axis=1)
        for p in range(pols):
            far_grad = (factor * mixed[p]).astype(BF)
            back = lax.dot_general(
                table[side], far_grad, (((1,), (1,)), ((), ())), preferred_element_type=F32
            )
            sums[p] = back if side == 0 else sums[p] + back
    groups, halves, count = back_ref.shape[:3]
    for p in range(pols):
        total = sums[p].reshape(groups, halves, count, rows, share_v).astype(BF)
        for half in range(halves):
            back_ref[:, half, :, 0, p] = total[:, half]
            back_ref[:, 1 - half, :, 1, p] = total[:, half]
    for store in stores:
        store.wait()


def adjoint_kernel(
    quarter, rows_dev, got_ref, w_ref, angle_ref, choose_ref, mark_ref, out_ref, total
):
    chunks, width = w_ref.shape[0], w_ref.shape[2]
    points = choose_ref.shape[2] // 2
    units = out_ref.shape[0]
    low = iota((8, width), 0) < 4
    for i in range(chunks):
        cos_a, sin_a = coarse_table(quarter, rows_dev, angle_ref[i])
        reals, imags = [], []
        for side, f, p in [(i, j, k) for i in range(2) for j in range(2) for k in range(2)]:
            plane = jnp.sum(got_ref[:, f, i, side, p].astype(F32), axis=0)
            other = pltpu.roll(plane, 4, 0)
            real = jnp.where(low, plane, other)
            imag = jnp.where(low, other, plane)
            real = jnp.broadcast_to(real[None], (points // 8, 8, width)).reshape(points, width)
            imag = jnp.broadcast_to(imag[None], (points // 8, 8, width)).reshape(points, width)
            reals.append((cos_a * real - sin_a * imag).astype(BF))
            imags.append((cos_a * imag + sin_a * real).astype(BF))
        found = lax.dot_general(
            jnp.concatenate(reals + imags, axis=0), w_ref[i], (((1,), (1,)), ((), ())),
            preferred_element_type=F32,
        )
        if i == 0:
            total[...] = found
        else:
            total[...] += found
    for side, fp in [(i, j) for i in range(2) for j in range(4)]:
        start = (4 * side + fp) * points
        real = total[start:start + points, :]
        imag = total[8 * points + start:9 * points + start, :]
        real_cos, real_sin, imag_cos, imag_sin = (
            real[:, :SEG], real[:, SEG:], imag[:, :SEG], imag[:, SEG:]
        )
        left = [
            mirrored((real_cos + imag_sin).astype(BF)).astype(BF),
            mirrored((imag_cos - real_sin).astype(BF)).astype(BF),
        ]
        right = [(real_cos - imag_sin).astype(BF), (imag_cos + real_sin).astype(BF)]
        block = jnp.concatenate(
            [jnp.concatenate(left, axis=1), jnp.concatenate(right, axis=1)], axis=0
        )
        sent = jnp.dot(choose_ref[side], block, preferred_element_type=F32).astype(BF)
        sent = sent.reshape(units, PACK, 2 * SEG)
        for c in range(2):
            rows = pl.ds((8 * side + 2 * fp + c) * PACK, PACK)
            out_ref[:, rows, :] = sent[:, :, c * SEG:(c + 1) * SEG]
    out_ref[:, 16 * PACK:, :] = mark_ref[...]


def faces_kernel(got_ref, out_hbm, out_ref, sems):
    faces = out_ref.shape[3]
    units = got_ref.shape[0]
    slots = units * PACK
    marks = got_ref[:, 16 * PACK:, :].astype(F32)
    hits = []
    for side in range(2):
        spots = [(2 * side + part) * (SEG // 4) for part in range(2)]
        mark = jnp.concatenate([marks[:, :, i:i + 1] for i in spots], axis=1)
        mark = jnp.broadcast_to(mark.reshape(slots, 1), (slots, faces)).astype(jnp.int32)
        hits.append(jnp.where(iota((slots, faces), 1) + 1 == mark, 1.0, 0.0).astype(BF))
    choose = jnp.concatenate(hits, axis=0)
    stores = []
    for f, p in [(i, j) for i in range(2) for j in range(2)]:
        for c in range(2):
            blocks = []
            for side in range(2):
                rows = pl.ds((8 * side + 4 * f + 2 * p + c) * PACK, PACK)
                blocks.append(got_ref[:, rows, :].reshape(slots, SEG))
            found = lax.dot_general(
                choose, jnp.concatenate(blocks, axis=0), (((0,), (0,)), ((), ())),
                preferred_element_type=F32,
            )
            out_ref[f, p, c] = found
            if p == 1:
                out_ref[f, 2, c] = -found
        places = [(0, 0), (0, 3)] if p == 0 else [(1, 1), (2, 2)]
        for source, k in places:
            stores.append(
                pltpu.make_async_copy(out_ref.at[f, source], out_hbm.at[f, k], sems.at[f, k])
            )
            stores[-1].start()
    for store in stores:
        store.wait()


def exchange_small(outgoing, groups, cap):
    units = outgoing.shape[0]
    peers = units * PACK // cap
    swap = functools.partial(
        lax.all_to_all, axis_name=BOTH, split_axis=1, concat_axis=1, tiled=True, axis_index_groups=groups
    )
    rows = outgoing[:, :16 * PACK].reshape(units, 16, PACK, SEG).transpose(1, 0, 2, 3)
    rows = swap(rows.reshape(16, peers, cap, SEG))
    rows = rows.reshape(16, units, PACK, SEG).transpose(1, 0, 2, 3).reshape(units, 16 * PACK, SEG)
    marks = outgoing[:, 16 * PACK:, ::SEG // 4].reshape(units, PACK // 2, 2, 2).transpose(2, 0, 3, 1)
    marks = swap(marks.reshape(2, peers, cap)).reshape(2, units, 2, PACK // 2)
    marks = marks.transpose(1, 3, 0, 2).reshape(units, PACK // 2, 4)
    return jnp.concatenate([rows, jnp.repeat(marks, SEG // 4, axis=2)], axis=1)


VM = pl.BlockSpec(memory_space=pltpu.VMEM)


def params(mib=24):
    return pltpu.CompilerParams(
        dimension_semantics=("arbitrary",), vmem_limit_bytes=mib * 1024 * 1024
    )


def cost(flops, moved):
    return pl.CostEstimate(flops=int(flops), bytes_accessed=int(moved), transcendentals=0)


def whole(shape):
    return pl.BlockSpec(shape, lambda i: (0,) * len(shape))


def body(currents, row_angles, column_angles, target, weight, tile_owner, face_slot):
    row_count = lax.axis_size("row")
    tile_count = lax.axis_size("tile")
    devices = row_count * tile_count
    freq_count, comp_count, part_count, rows_dev, columns = currents.shape
    far_rows = row_angles.shape[0]
    far_cols = column_angles.shape[0]
    share_v = far_cols // tile_count
    share_u = far_rows // row_count
    chunks = far_cols // CHUNK
    tiles = columns // SEG
    points = rows_dev * tiles
    half = points // 2
    cap = 2 * points // devices
    slots = points
    units = slots // PACK
    held = 16 * PACK + PACK // 2
    pairs = row_count // 2
    wide = 2 * rows_dev
    depth = devices * wide
    tile_half = tile_count // 2
    half_groups = [
        [r * tile_count + side * tile_half + t for r in range(row_count) for t in range(tile_half)]
        for side in range(2)
    ]
    swap = [(i, i ^ 1) for i in range(row_count)]
    mirror = [(i, (i + tile_half) % tile_count) for i in range(tile_count)]
    angles = column_angles.reshape(chunks, 1, CHUNK)
    far_target = lax.ppermute(target, "row", swap)
    far_weight = lax.ppermute(weight, "row", swap)
    far_owner = lax.ppermute(tile_owner, "tile", mirror)
    far_slot = lax.ppermute(face_slot, "tile", mirror)
    cur = currents.reshape(freq_count, comp_count, part_count, rows_dev, tiles, SEG)
    cur = cur.transpose(0, 1, 2, 4, 3, 5).reshape(freq_count, comp_count, part_count, points, SEG)
    copies = pairs if share_v == CHUNK else 1
    plane = pl.pallas_call(
        functools.partial(forward_kernel, columns, rows_dev),
        grid=(1,),
        in_specs=[VM, pl.BlockSpec(memory_space=pltpu.HBM)],
        out_specs=whole((copies, 2, chunks, 2, wide, CHUNK)),
        out_shape=jax.ShapeDtypeStruct((copies, 2, chunks, 2, wide, CHUNK), BF),
        scratch_shapes=[
            pltpu.VMEM(cur.shape, BF),
            pltpu.VMEM((8 * half, 2 * SEG), BF),
            pltpu.VMEM((chunks, 2 * SEG, CHUNK), BF),
            pltpu.VMEM((chunks, 2, half, CHUNK), F32),
            pltpu.SemaphoreType.DMA((2, 4)),
        ],
        compiler_params=params(58),
        cost_estimate=cost(4.3e9, 1.6e6),
        name="columns",
    )(angles, cur)
    if share_v != CHUNK:
        plane = plane.reshape(2, chunks, 2, wide, CHUNK // share_v, share_v)
        plane = plane.transpose(0, 1, 4, 2, 3, 5).reshape(1, 2, tile_count, 2, wide, share_v)
        plane = jnp.broadcast_to(plane, (pairs,) + plane.shape[1:])
    plane = plane.reshape(devices, 2, wide, share_v)

    row_angles, plane = lax.optimization_barrier((row_angles, plane))
    got = lax.all_to_all(plane, BOTH, 0, 0, tiled=True)
    here = lax.axis_index("row")
    own_angles = jnp.stack(
        [lax.dynamic_slice_in_dim(row_angles, i * share_u, share_u) for i in (here, here ^ 1)]
    )
    row_table = pl.pallas_call(
        functools.partial(row_kernel, columns, rows_dev),
        grid=(1,),
        in_specs=[VM],
        out_specs=whole((2, depth, 2 * share_u)),
        out_shape=jax.ShapeDtypeStruct((2, depth, 2 * share_u), BF),
        compiler_params=params(),
        cost_estimate=cost(1e8, 5e5),
        name="rows",
    )(own_angles)
    far_shape = (share_v, share_u)
    spare = (56 << 20) // (4 * share_v * share_u)
    back_shape = (row_count, 2, tile_half, 2, 2, wide, share_v)
    powers, back = pl.pallas_call(
        middle_kernel,
        grid=(1,),
        in_specs=[VM] * 6,
        out_specs=[pl.BlockSpec(memory_space=pl.ANY), whole(back_shape)],
        out_shape=[
            jax.ShapeDtypeStruct((spare,) + far_shape, F32),
            jax.ShapeDtypeStruct(back_shape, BF),
        ],
        scratch_shapes=[pltpu.VMEM((2,) + far_shape, F32), pltpu.SemaphoreType.DMA((2,))],
        compiler_params=params(),
        cost_estimate=cost(1.1e9, 5e6),
        name="objective",
    )(row_table, got, target, far_target, weight, far_weight)

    owner, slot, far_owner, far_slot, angles, powers, back = lax.optimization_barrier(
        (tile_owner, face_slot, far_owner, far_slot, angles, powers, back)
    )
    far_power = lax.ppermute(powers[1], "row", swap)
    code = jnp.stack(
        [owner[:, 0] * points + slot, far_owner[:, 0] * points + far_slot], axis=1
    )
    back = back.reshape(devices, 2, 2, wide, share_v)
    back = lax.all_to_all(back, BOTH, 0, 0, tiled=True)
    table, choose, mark, intensity = pl.pallas_call(
        functools.partial(prepare_kernel, columns, rows_dev, tile_count, cap),
        grid=(1,),
        in_specs=[VM, VM, pl.BlockSpec((1,) + far_shape, lambda i: (0, 0, 0)), VM],
        out_specs=[
            whole((chunks, 2 * SEG, CHUNK)),
            whole((2, slots, points)),
            whole((units, PACK // 2, SEG)),
            whole(target.shape),
        ],
        out_shape=[
            jax.ShapeDtypeStruct((chunks, 2 * SEG, CHUNK), BF),
            jax.ShapeDtypeStruct((2, slots, points), BF),
            jax.ShapeDtypeStruct((units, PACK // 2, SEG), BF),
            jax.ShapeDtypeStruct(target.shape, F32),
        ],
        compiler_params=params(),
        cost_estimate=cost(1e9, 2e6),
        name="prepare",
    )(angles, code, powers, far_power)

    back = back.reshape(pairs, 2, tile_count, 2, 2, wide, share_v)
    if share_v != CHUNK:
        back = back.reshape(pairs, 2, chunks, CHUNK // share_v, 2, 2, wide, share_v)
        back = back.transpose(0, 1, 2, 4, 5, 6, 3, 7).reshape(pairs, 2, chunks, 2, 2, wide, CHUNK)
    outgoing = pl.pallas_call(
        functools.partial(adjoint_kernel, columns, rows_dev),
        grid=(1,),
        in_specs=[VM] * 5,
        out_specs=whole((units, held, SEG)),
        out_shape=jax.ShapeDtypeStruct((units, held, SEG), BF),
        scratch_shapes=[pltpu.VMEM((16 * half, 2 * SEG), F32)],
        compiler_params=params(),
        cost_estimate=cost(4.3e9, 4e6),
        name="adjoint",
    )(back, table, angles, choose, mark)

    if cap == PACK:
        arrived = lax.all_to_all(outgoing, BOTH, 0, 0, tiled=True, axis_index_groups=half_groups)
    else:
        arrived = exchange_small(outgoing, half_groups, cap)
    out_shape = (freq_count, comp_count, part_count, points, SEG)
    faces = pl.pallas_call(
        faces_kernel,
        grid=(1,),
        in_specs=[VM],
        out_specs=pl.BlockSpec(memory_space=pl.ANY),
        out_shape=jax.ShapeDtypeStruct(out_shape, F32),
        scratch_shapes=[
            pltpu.VMEM((freq_count, 3, part_count, points, SEG), F32),
            pltpu.SemaphoreType.DMA((2, 4)),
        ],
        compiler_params=params(),
        name="faces",
    )(arrived)
    return (intensity, faces)


def solution(mesh):
    in_specs = (
        P(None, None, None, ("row", "tile"), None),
        P(),
        P(),
        P(None, "tile", "row"),
        P(None, "tile", "row"),
        P(("row", "tile"), None),
        P(("row", "tile")),
    )
    out_specs = (P(None, "tile", "row"), P(None, None, None, ("row", "tile"), None))
    return jax.shard_map(body, mesh=mesh, in_specs=in_specs, out_specs=out_specs, check_vma=False)
```

```python
import functools
import math

import jax
import jax.numpy as jnp
from jax import lax
from jax.experimental import pallas as pl
from jax.experimental.pallas import tpu as pltpu
from jax.sharding import PartitionSpec as P

SEG = 128
CHUNK = 256
PACK = 16
BOTH = ("row", "tile")
BF = jnp.bfloat16
F32 = jnp.float32


def cos_sin(turns, quarter, scale):
    bits = int(math.log2(quarter))
    turns = turns & (4 * quarter - 1)
    octant = (turns + quarter // 2) >> bits
    angle = (turns - (octant << bits)).astype(F32) * (math.pi / (2 * quarter))
    square = angle * angle
    sin_part = angle * scale + (angle * scale) * square * (
        -1.6666654611e-1 + square * (8.3321608736e-3 - square * 1.9515295891e-4)
    )
    cos_part = scale - square * (0.5 * scale) + (square * scale) * square * (
        4.166664568298827e-2 + square * (-1.388731625493765e-3 + square * 2.443315711809948e-5)
    )
    swap = (octant & 1) == 1
    cos_out = jnp.where(swap, sin_part, cos_part)
    sin_out = jnp.where(swap, cos_part, sin_part)
    cos_out = jnp.where(((octant + 1) & 2) == 2, -cos_out, cos_out)
    sin_out = jnp.where((octant & 2) == 2, -sin_out, sin_out)
    return cos_out, sin_out


def iota(shape, dim):
    return lax.broadcasted_iota(jnp.int32, shape, dim)


def turned(cos_0, sin_0, cos_1, sin_1):
    rows, width = cos_0.shape
    cos_out, sin_out = [], []
    for j in range(cos_1.shape[0]):
        cos_j = jnp.broadcast_to(cos_1[j:j + 1], (rows, width))
        sin_j = jnp.broadcast_to(sin_1[j:j + 1], (rows, width))
        cos_out.append(cos_0 * cos_j - sin_0 * sin_j)
        sin_out.append(sin_0 * cos_j + cos_0 * sin_j)
    return jnp.concatenate(cos_out, axis=0), jnp.concatenate(sin_out, axis=0)


def middle(quarter):
    return quarter // 2 + SEG - 1


def fine_table(quarter, angles):
    width = angles.shape[-1]
    start = quarter - middle(quarter) + iota((SEG // 8, width), 0) * 16
    cos_0, sin_0 = cos_sin(2 * iota((8, width), 0) * angles, 2 * quarter, 1.0 / math.sqrt(quarter))
    cos_1, sin_1 = cos_sin(start * angles, 2 * quarter, 1.0)
    return jnp.concatenate(turned(cos_0, sin_0, cos_1, sin_1), axis=0).astype(BF)


def coarse_table(quarter, rows_dev, angles):
    width = angles.shape[-1]
    tiles = quarter // SEG // 2
    group = 8 // rows_dev
    base = (iota((8, width), 0) // rows_dev) * (2 * SEG)
    start = iota((tiles // group, width), 0) * (2 * group * SEG) + middle(quarter)
    cos_0, sin_0 = cos_sin(base * angles, 2 * quarter, 1.0)
    cos_1, sin_1 = cos_sin(start * angles, 2 * quarter, 1.0)
    return turned(cos_0, sin_0, cos_1, sin_1)


def mirrored(block):
    flip = jnp.where(iota((SEG, SEG), 0) + iota((SEG, SEG), 1) == SEG - 1, 1.0, 0.0).astype(BF)
    return jnp.dot(block, flip, preferred_element_type=F32)


def forward_kernel(quarter, rows_dev, angle_ref, cur_hbm, f_ref, cur_ref, lhs, fine, coarse, sem):
    points = rows_dev * quarter // SEG // 2
    chunks, width = angle_ref.shape[0], angle_ref.shape[-1]
    loads = [
        [pltpu.make_async_copy(cur_hbm.at[f, k], cur_ref.at[f, k], sem.at[f, k]) for k in range(4)]
        for f in range(2)
    ]
    for load in loads[0] + loads[1]:
        load.start()
    for i in range(chunks):
        fine[i] = fine_table(quarter, angle_ref[i])
        coarse[i, 0], coarse[i, 1] = coarse_table(quarter, rows_dev, angle_ref[i])
    low_half, high_half = pl.ds(0, points), pl.ds(points, points)
    for f in range(2):
        for load in loads[f]:
            load.wait()
        even, odd = [], []
        for c in range(2):
            right = [cur_ref[f, k, c, high_half, :].astype(F32) for k in range(4)]
            left = [mirrored(cur_ref[f, k, c, low_half, :]) for k in range(4)]
            right = [right[0] + right[3], right[1] - right[2]]
            left = [left[0] + left[3], left[1] - left[2]]
            even.append([i + j for i, j in zip(right, left)])
            odd.append([i - j for i, j in zip(right, left)])
        for p in range(2):
            real = pl.ds((2 * f + p) * points, points)
            imag = pl.ds((4 + 2 * f + p) * points, points)
            lhs[real, :SEG] = even[0][p].astype(BF)
            lhs[real, SEG:] = odd[1][p].astype(BF)
            lhs[imag, :SEG] = even[1][p].astype(BF)
            lhs[imag, SEG:] = (-odd[0][p]).astype(BF)
    low = iota((8, width), 0) < 4
    for i in range(chunks):
        grid_sum = jnp.dot(lhs[...], fine[i], preferred_element_type=F32)
        cos_a, sin_a = coarse[i, 0], coarse[i, 1]
        for f, p in [(i, j) for i in range(2) for j in range(2)]:
            start = (2 * f + p) * points
            real = grid_sum[start:start + points]
            imag = grid_sum[4 * points + start:5 * points + start]
            out_re = jnp.sum((real * cos_a + imag * sin_a).reshape(points // 8, 8, width), axis=0)
            out_im = jnp.sum((imag * cos_a - real * sin_a).reshape(points // 8, 8, width), axis=0)
            out_re = out_re + pltpu.roll(out_re, 4, 0)
            out_im = out_im + pltpu.roll(out_im, 4, 0)
            out = jnp.where(low, out_re, out_im).astype(BF)
            for copy in range(f_ref.shape[0]):
                f_ref[copy, f, i, p] = out


def row_kernel(quarter, rows_dev, row_ref, r_ref):
    sides, depth = r_ref.shape[:2]
    share_u = row_ref.shape[-1]
    row = iota((depth, share_u), 0)
    x = (row // (2 * rows_dev)) * rows_dev + row % rows_dev
    is_imag = row % (2 * rows_dev) >= rows_dev
    scale = 1.0 / math.sqrt(depth // 2)
    for side in range(sides):
        cos_x, sin_x = cos_sin(x * row_ref[side:side + 1], quarter, scale)
        r_ref[side, :, :share_u] = jnp.where(is_imag, sin_x, cos_x).astype(BF)
        r_ref[side, :, share_u:] = jnp.where(is_imag, cos_x, -sin_x).astype(BF)


def prepare_kernel(
    quarter, rows_dev, tile_count, cap, angle_ref, code_ref, power_ref, far_power_ref,
    w_ref, choose_ref, mark_ref, int_ref,
):
    core = lax.axis_index("row") % 2
    int_ref[core] = power_ref[0]
    int_ref[1 - core] = far_power_ref[...]
    points = code_ref.shape[0]
    slots, units = choose_ref.shape[1], mark_ref.shape[0]
    for i in range(angle_ref.shape[0]):
        w_ref[i] = fine_table(quarter, angle_ref[i])
    segs = points // rows_dev
    half = tile_count // 2
    mine = lax.axis_index("tile") // half
    point = iota((points, points), 1)
    point = (point % rows_dev) * segs + (point // rows_dev)
    source = iota((points, points), 0)
    spot = iota((slots, SEG), 1) - iota((slots, SEG), 0) % PACK
    marked = jnp.zeros((slots, SEG), jnp.int32)
    for side in range(2):
        code_col = code_ref[:, side:side + 1]
        code_row = jnp.sum(jnp.where(source == point, code_col, 0), axis=0, keepdims=True)
        owner_col, owner_row = code_col // points, code_row // points
        same = jnp.where((source < point) & (owner_col == owner_row), 1, 0)
        rank = jnp.sum(same, axis=0, keepdims=True)
        tile = owner_row % tile_count
        place = ((owner_row // tile_count) * half + tile % half) * cap + rank
        place = jnp.where(tile // half == mine, place, -1)
        hit = iota((slots, points), 0) == place
        choose_ref[side] = jnp.where(hit, 1.0, 0.0).astype(BF)
        marks = jnp.sum(jnp.where(hit, code_row % points + 1, 0), axis=1, keepdims=True)
        marked = jnp.where(spot == side * PACK, marks, marked)
    marked = jnp.sum(marked.reshape(units, PACK, SEG), axis=1, keepdims=True)
    marked = jnp.broadcast_to(marked, mark_ref.shape)
    mark_ref[...] = marked.astype(F32).astype(BF)


def middle_kernel(
    table, got_ref, target_ref, far_target_ref, weight_ref, far_weight_ref,
    power_hbm, back_ref, powers, fars, sems,
):
    devices, pols, rows, share_v = got_ref.shape
    depth = devices * rows
    share_u = table.shape[2] // 2
    core = lax.axis_index("row") % 2
    loads = [
        pltpu.make_async_copy(array.at[core], fars.at[i], sems.at[2 + i])
        for i, array in enumerate((far_target_ref, far_weight_ref))
    ]
    for load in loads:
        load.start()
    planes = [
        got_ref[:, p].astype(F32).reshape(depth, share_v).astype(BF) for p in range(pols)
    ]
    sums = [None, None]
    stores = []
    for side in range(2):
        mixed = [
            lax.dot_general(
                plane, table[side], (((0,), (0,)), ((), ())), preferred_element_type=F32
            )
            for plane in planes
        ]
        power = mixed[0] * mixed[0] + mixed[1] * mixed[1]
        intensity = power[:, :share_u] + power[:, share_u:]
        powers[side] = intensity
        stores.append(pltpu.make_async_copy(powers.at[side], power_hbm.at[side], sems.at[side]))
        stores[-1].start()
        if side == 0:
            goal, gain = target_ref[core], weight_ref[core]
        else:
            for load in loads:
                load.wait()
            goal, gain = fars[0], fars[1]
        factor = 4.0 * gain * (intensity - goal)
        factor = jnp.concatenate([factor, factor], axis=1)
        for p in range(pols):
            far_grad = (factor * mixed[p]).astype(BF)
            back = lax.dot_general(
                table[side], far_grad, (((1,), (1,)), ((), ())), preferred_element_type=F32
            )
            sums[p] = back if side == 0 else sums[p] + back
    groups, halves, count = back_ref.shape[:3]
    for p in range(pols):
        total = sums[p].reshape(groups, halves, count, rows, share_v).astype(BF)
        for half in range(halves):
            back_ref[:, half, :, 0, p] = total[:, half]
            back_ref[:, 1 - half, :, 1, p] = total[:, half]
    for store in stores:
        store.wait()


def adjoint_kernel(
    quarter, rows_dev, got_ref, w_ref, angle_ref, choose_ref, mark_ref, out_ref, total
):
    chunks, width = w_ref.shape[0], w_ref.shape[2]
    points = choose_ref.shape[2] // 2
    units = out_ref.shape[0]
    low = iota((8, width), 0) < 4
    for i in range(chunks):
        cos_a, sin_a = coarse_table(quarter, rows_dev, angle_ref[i])
        reals, imags = [], []
        for side, f, p in [(i, j, k) for i in range(2) for j in range(2) for k in range(2)]:
            plane = jnp.sum(got_ref[:, f, i, side, p].astype(F32), axis=0)
            other = pltpu.roll(plane, 4, 0)
            real = jnp.where(low, plane, other)
            imag = jnp.where(low, other, plane)
            real = jnp.broadcast_to(real[None], (points // 8, 8, width)).reshape(points, width)
            imag = jnp.broadcast_to(imag[None], (points // 8, 8, width)).reshape(points, width)
            reals.append((cos_a * real - sin_a * imag).astype(BF))
            imags.append((cos_a * imag + sin_a * real).astype(BF))
        found = lax.dot_general(
            jnp.concatenate(reals + imags, axis=0), w_ref[i], (((1,), (1,)), ((), ())),
            preferred_element_type=F32,
        )
        if i == 0:
            total[...] = found
        else:
            total[...] += found
    for side, fp in [(i, j) for i in range(2) for j in range(4)]:
        start = (4 * side + fp) * points
        real = total[start:start + points, :]
        imag = total[8 * points + start:9 * points + start, :]
        real_cos, real_sin, imag_cos, imag_sin = (
            real[:, :SEG], real[:, SEG:], imag[:, :SEG], imag[:, SEG:]
        )
        left = [
            mirrored((real_cos + imag_sin).astype(BF)).astype(BF),
            mirrored((imag_cos - real_sin).astype(BF)).astype(BF),
        ]
        right = [(real_cos - imag_sin).astype(BF), (imag_cos + real_sin).astype(BF)]
        block = jnp.concatenate(
            [jnp.concatenate(left, axis=1), jnp.concatenate(right, axis=1)], axis=0
        )
        sent = jnp.dot(choose_ref[side], block, preferred_element_type=F32).astype(BF)
        sent = sent.reshape(units, PACK, 2 * SEG)
        for c in range(2):
            rows = pl.ds((8 * side + 2 * fp + c) * PACK, PACK)
            out_ref[:, rows, :] = sent[:, :, c * SEG:(c + 1) * SEG]
    out_ref[:, 16 * PACK:, :] = mark_ref[...]


def faces_kernel(got_ref, out_hbm, out_ref, sems):
    faces = out_ref.shape[3]
    units = got_ref.shape[0]
    slots = units * PACK
    marks = got_ref[:, 16 * PACK:, :].astype(F32)
    fit = SEG // (2 * PACK)
    rows = []
    for i in range(0, units, fit):
        row = marks[i]
        for j in range(1, fit):
            row = row + pltpu.roll(marks[i + j], 2 * PACK * j, 1)
        rows.append(row)
    label = jnp.concatenate(rows, axis=1).astype(jnp.int32)
    face = iota((PACK // 2, 2 * slots), 0) + 1
    choose = jnp.concatenate(
        [
            jnp.where(face + i == label, 1.0, 0.0) for i in range(0, faces, PACK // 2)
        ],
        axis=0,
    ).astype(BF)
    stores = []
    for f, p in [(i, j) for i in range(2) for j in range(2)]:
        for c in range(2):
            blocks = []
            for side in range(2):
                rows = pl.ds((8 * side + 4 * f + 2 * p + c) * PACK, PACK)
                blocks.append(got_ref[:, rows, :])
            block = jnp.concatenate(blocks, axis=1).reshape(2 * slots, SEG)
            found = jnp.dot(choose, block, preferred_element_type=F32)
            out_ref[f, p, c] = found
            if p == 1:
                out_ref[f, 2, c] = -found
        places = [(0, 0), (0, 3)] if p == 0 else [(1, 1), (2, 2)]
        for source, k in places:
            stores.append(
                pltpu.make_async_copy(out_ref.at[f, source], out_hbm.at[f, k], sems.at[f, k])
            )
            stores[-1].start()
    for store in stores:
        store.wait()


def exchange_small(outgoing, groups, cap):
    units = outgoing.shape[0]
    peers = units * PACK // cap
    swap = functools.partial(
        lax.all_to_all, axis_name=BOTH, split_axis=1, concat_axis=1, tiled=True, axis_index_groups=groups
    )
    rows = outgoing[:, :16 * PACK].reshape(units, 16, PACK, SEG).transpose(1, 0, 2, 3)
    rows = swap(rows.reshape(16, peers, cap, SEG))
    rows = rows.reshape(16, units, PACK, SEG).transpose(1, 0, 2, 3).reshape(units, 16 * PACK, SEG)
    marks = outgoing[:, 16 * PACK, :2 * PACK].reshape(units, 2, PACK).transpose(1, 0, 2)
    marks = swap(marks.reshape(2, peers, cap)).reshape(2, units, PACK)
    marks = marks.transpose(1, 0, 2).reshape(units, 1, 2 * PACK)
    marks = jnp.pad(marks, ((0, 0), (0, 0), (0, SEG - 2 * PACK)))
    marks = jnp.broadcast_to(marks, (units, PACK // 2, SEG))
    return jnp.concatenate([rows, marks], axis=1)


VM = pl.BlockSpec(memory_space=pltpu.VMEM)


def params(mib=24):
    return pltpu.CompilerParams(
        dimension_semantics=("arbitrary",), vmem_limit_bytes=mib * 1024 * 1024
    )


def cost(flops, moved):
    return pl.CostEstimate(flops=int(flops), bytes_accessed=int(moved), transcendentals=0)


def whole(shape):
    return pl.BlockSpec(shape, lambda i: (0,) * len(shape))


def body(currents, row_angles, column_angles, target, weight, tile_owner, face_slot):
    row_count = lax.axis_size("row")
    tile_count = lax.axis_size("tile")
    devices = row_count * tile_count
    freq_count, comp_count, part_count, rows_dev, columns = currents.shape
    far_rows = row_angles.shape[0]
    far_cols = column_angles.shape[0]
    share_v = far_cols // tile_count
    share_u = far_rows // row_count
    chunks = far_cols // CHUNK
    tiles = columns // SEG
    points = rows_dev * tiles
    half = points // 2
    cap = 2 * points // devices
    slots = points
    units = slots // PACK
    held = 16 * PACK + PACK // 2
    pairs = row_count // 2
    wide = 2 * rows_dev
    depth = devices * wide
    tile_half = tile_count // 2
    half_groups = [
        [r * tile_count + side * tile_half + t for r in range(row_count) for t in range(tile_half)]
        for side in range(2)
    ]
    swap = [(i, i ^ 1) for i in range(row_count)]
    mirror = [(i, (i + tile_half) % tile_count) for i in range(tile_count)]
    angles = column_angles.reshape(chunks, 1, CHUNK)
    far_target = lax.ppermute(target, "row", swap)
    far_weight = lax.ppermute(weight, "row", swap)
    far_owner = lax.ppermute(tile_owner, "tile", mirror)
    far_slot = lax.ppermute(face_slot, "tile", mirror)
    cur = currents.reshape(freq_count, comp_count, part_count, rows_dev, tiles, SEG)
    cur = cur.transpose(0, 1, 2, 4, 3, 5).reshape(freq_count, comp_count, part_count, points, SEG)
    copies = pairs if share_v == CHUNK else 1
    plane = pl.pallas_call(
        functools.partial(forward_kernel, columns, rows_dev),
        grid=(1,),
        in_specs=[VM, pl.BlockSpec(memory_space=pltpu.HBM)],
        out_specs=whole((copies, 2, chunks, 2, wide, CHUNK)),
        out_shape=jax.ShapeDtypeStruct((copies, 2, chunks, 2, wide, CHUNK), BF),
        scratch_shapes=[
            pltpu.VMEM(cur.shape, BF),
            pltpu.VMEM((8 * half, 2 * SEG), BF),
            pltpu.VMEM((chunks, 2 * SEG, CHUNK), BF),
            pltpu.VMEM((chunks, 2, half, CHUNK), F32),
            pltpu.SemaphoreType.DMA((2, 4)),
        ],
        compiler_params=params(58),
        cost_estimate=cost(4.3e9, 1.6e6),
        name="columns",
    )(angles, cur)
    if share_v != CHUNK:
        plane = plane.reshape(2, chunks, 2, wide, CHUNK // share_v, share_v)
        plane = plane.transpose(0, 1, 4, 2, 3, 5).reshape(1, 2, tile_count, 2, wide, share_v)
        plane = jnp.broadcast_to(plane, (pairs,) + plane.shape[1:])
    plane = plane.reshape(devices, 2, wide, share_v)

    row_angles, plane = lax.optimization_barrier((row_angles, plane))
    got = lax.all_to_all(plane, BOTH, 0, 0, tiled=True)
    here = lax.axis_index("row")
    own_angles = jnp.stack(
        [lax.dynamic_slice_in_dim(row_angles, i * share_u, share_u) for i in (here, here ^ 1)]
    )
    row_table = pl.pallas_call(
        functools.partial(row_kernel, columns, rows_dev),
        grid=(1,),
        in_specs=[VM],
        out_specs=whole((2, depth, 2 * share_u)),
        out_shape=jax.ShapeDtypeStruct((2, depth, 2 * share_u), BF),
        compiler_params=params(),
        cost_estimate=cost(1e8, 5e5),
        name="rows",
    )(own_angles)
    far_shape = (share_v, share_u)
    spare = (56 << 20) // (4 * share_v * share_u)
    back_shape = (row_count, 2, tile_half, 2, 2, wide, share_v)
    powers, back = pl.pallas_call(
        middle_kernel,
        grid=(1,),
        in_specs=[VM, VM, VM, pl.BlockSpec(memory_space=pl.ANY), VM, pl.BlockSpec(memory_space=pl.ANY)],
        out_specs=[pl.BlockSpec(memory_space=pl.ANY), whole(back_shape)],
        out_shape=[
            jax.ShapeDtypeStruct((spare,) + far_shape, F32),
            jax.ShapeDtypeStruct(back_shape, BF),
        ],
        scratch_shapes=[
            pltpu.VMEM((2,) + far_shape, F32),
            pltpu.VMEM((2,) + far_shape, F32),
            pltpu.SemaphoreType.DMA((4,)),
        ],
        compiler_params=params(),
        cost_estimate=cost(1.1e9, 5e6),
        name="objective",
    )(row_table, got, target, far_target, weight, far_weight)

    owner, slot, far_owner, far_slot, angles, powers, back = lax.optimization_barrier(
        (tile_owner, face_slot, far_owner, far_slot, angles, powers, back)
    )
    far_power = lax.ppermute(powers[1], "row", swap)
    code = jnp.stack(
        [owner[:, 0] * points + slot, far_owner[:, 0] * points + far_slot], axis=1
    )
    back = back.reshape(devices, 2, 2, wide, share_v)
    back = lax.all_to_all(back, BOTH, 0, 0, tiled=True)
    table, choose, mark, intensity = pl.pallas_call(
        functools.partial(prepare_kernel, columns, rows_dev, tile_count, cap),
        grid=(1,),
        in_specs=[VM, VM, pl.BlockSpec((1,) + far_shape, lambda i: (0, 0, 0)), VM],
        out_specs=[
            whole((chunks, 2 * SEG, CHUNK)),
            whole((2, slots, points)),
            whole((units, PACK // 2, SEG)),
            whole(target.shape),
        ],
        out_shape=[
            jax.ShapeDtypeStruct((chunks, 2 * SEG, CHUNK), BF),
            jax.ShapeDtypeStruct((2, slots, points), BF),
            jax.ShapeDtypeStruct((units, PACK // 2, SEG), BF),
            jax.ShapeDtypeStruct(target.shape, F32),
        ],
        compiler_params=params(),
        cost_estimate=cost(1e9, 2e6),
        name="prepare",
    )(angles, code, powers, far_power)

    back = back.reshape(pairs, 2, tile_count, 2, 2, wide, share_v)
    if share_v != CHUNK:
        back = back.reshape(pairs, 2, chunks, CHUNK // share_v, 2, 2, wide, share_v)
        back = back.transpose(0, 1, 2, 4, 5, 6, 3, 7).reshape(pairs, 2, chunks, 2, 2, wide, CHUNK)
    outgoing = pl.pallas_call(
        functools.partial(adjoint_kernel, columns, rows_dev),
        grid=(1,),
        in_specs=[VM] * 5,
        out_specs=whole((units, held, SEG)),
        out_shape=jax.ShapeDtypeStruct((units, held, SEG), BF),
        scratch_shapes=[pltpu.VMEM((16 * half, 2 * SEG), F32)],
        compiler_params=params(),
        cost_estimate=cost(4.3e9, 4e6),
        name="adjoint",
    )(back, table, angles, choose, mark)

    if cap == PACK:
        arrived = lax.all_to_all(outgoing, BOTH, 0, 0, tiled=True, axis_index_groups=half_groups)
    else:
        arrived = exchange_small(outgoing, half_groups, cap)
    out_shape = (freq_count, comp_count, part_count, points, SEG)
    faces = pl.pallas_call(
        faces_kernel,
        grid=(1,),
        in_specs=[VM],
        out_specs=pl.BlockSpec(memory_space=pl.ANY),
        out_shape=jax.ShapeDtypeStruct(out_shape, F32),
        scratch_shapes=[
            pltpu.VMEM((freq_count, 3, part_count, points, SEG), F32),
            pltpu.SemaphoreType.DMA((2, 4)),
        ],
        compiler_params=params(),
        name="faces",
    )(arrived)
    return (intensity, faces)


def solution(mesh):
    in_specs = (
        P(None, None, None, ("row", "tile"), None),
        P(),
        P(),
        P(None, "tile", "row"),
        P(None, "tile", "row"),
        P(("row", "tile"), None),
        P(("row", "tile")),
    )
    out_specs = (P(None, "tile", "row"), P(None, None, None, ("row", "tile"), None))
    return jax.shard_map(body, mesh=mesh, in_specs=in_specs, out_specs=out_specs, check_vma=False)
```

```python
import functools
import math

import jax
import jax.numpy as jnp
from jax import lax
from jax.experimental import pallas as pl
from jax.experimental.pallas import tpu as pltpu
from jax.sharding import PartitionSpec as P

SEG = 128
CHUNK = 256
PACK = 16
BOTH = ("row", "tile")
BF = jnp.bfloat16
F32 = jnp.float32


def cos_sin(turns, quarter, scale):
    bits = int(math.log2(quarter))
    turns = turns & (4 * quarter - 1)
    octant = (turns + quarter // 2) >> bits
    angle = (turns - (octant << bits)).astype(F32) * (math.pi / (2 * quarter))
    square = angle * angle
    sin_part = angle * scale + (angle * scale) * square * (
        -1.6666654611e-1 + square * (8.3321608736e-3 - square * 1.9515295891e-4)
    )
    cos_part = scale - square * (0.5 * scale) + (square * scale) * square * (
        4.166664568298827e-2 + square * (-1.388731625493765e-3 + square * 2.443315711809948e-5)
    )
    swap = (octant & 1) == 1
    cos_out = jnp.where(swap, sin_part, cos_part)
    sin_out = jnp.where(swap, cos_part, sin_part)
    cos_out = jnp.where(((octant + 1) & 2) == 2, -cos_out, cos_out)
    sin_out = jnp.where((octant & 2) == 2, -sin_out, sin_out)
    return cos_out, sin_out


def iota(shape, dim):
    return lax.broadcasted_iota(jnp.int32, shape, dim)


def turned(cos_0, sin_0, cos_1, sin_1):
    rows, width = cos_0.shape
    cos_out, sin_out = [], []
    for j in range(cos_1.shape[0]):
        cos_j = jnp.broadcast_to(cos_1[j:j + 1], (rows, width))
        sin_j = jnp.broadcast_to(sin_1[j:j + 1], (rows, width))
        cos_out.append(cos_0 * cos_j - sin_0 * sin_j)
        sin_out.append(sin_0 * cos_j + cos_0 * sin_j)
    return jnp.concatenate(cos_out, axis=0), jnp.concatenate(sin_out, axis=0)


def middle(quarter):
    return quarter // 2 + SEG - 1


def fine_table(quarter, angles):
    width = angles.shape[-1]
    start = quarter - middle(quarter) + iota((SEG // 8, width), 0) * 16
    cos_0, sin_0 = cos_sin(2 * iota((8, width), 0) * angles, 2 * quarter, 1.0 / math.sqrt(quarter))
    cos_1, sin_1 = cos_sin(start * angles, 2 * quarter, 1.0)
    return jnp.concatenate(turned(cos_0, sin_0, cos_1, sin_1), axis=0).astype(BF)


def coarse_table(quarter, rows_dev, angles):
    width = angles.shape[-1]
    tiles = quarter // SEG // 2
    group = 8 // rows_dev
    base = (iota((8, width), 0) // rows_dev) * (2 * SEG)
    start = iota((tiles // group, width), 0) * (2 * group * SEG) + middle(quarter)
    cos_0, sin_0 = cos_sin(base * angles, 2 * quarter, 1.0)
    cos_1, sin_1 = cos_sin(start * angles, 2 * quarter, 1.0)
    return turned(cos_0, sin_0, cos_1, sin_1)


def mirrored(block):
    flip = jnp.where(iota((SEG, SEG), 0) + iota((SEG, SEG), 1) == SEG - 1, 1.0, 0.0).astype(BF)
    return jnp.dot(block, flip, preferred_element_type=F32)


def forward_kernel(quarter, rows_dev, angle_ref, cur_hbm, f_ref, cur_ref, lhs, fine, coarse, sem):
    points = rows_dev * quarter // SEG // 2
    chunks, width = angle_ref.shape[0], angle_ref.shape[-1]
    loads = [
        [pltpu.make_async_copy(cur_hbm.at[f, k], cur_ref.at[f, k], sem.at[f, k]) for k in range(4)]
        for f in range(2)
    ]
    for load in loads[0] + loads[1]:
        load.start()
    for i in range(chunks):
        fine[i] = fine_table(quarter, angle_ref[i])
        coarse[i, 0], coarse[i, 1] = coarse_table(quarter, rows_dev, angle_ref[i])
    low_half, high_half = pl.ds(0, points), pl.ds(points, points)
    for f in range(2):
        for load in loads[f]:
            load.wait()
        even, odd = [], []
        for c in range(2):
            right = [cur_ref[f, k, c, high_half, :].astype(F32) for k in range(4)]
            left = [mirrored(cur_ref[f, k, c, low_half, :]) for k in range(4)]
            right = [right[0] + right[3], right[1] - right[2]]
            left = [left[0] + left[3], left[1] - left[2]]
            even.append([i + j for i, j in zip(right, left)])
            odd.append([i - j for i, j in zip(right, left)])
        for p in range(2):
            real = pl.ds((2 * f + p) * points, points)
            imag = pl.ds((4 + 2 * f + p) * points, points)
            lhs[real, :SEG] = even[0][p].astype(BF)
            lhs[real, SEG:] = odd[1][p].astype(BF)
            lhs[imag, :SEG] = even[1][p].astype(BF)
            lhs[imag, SEG:] = (-odd[0][p]).astype(BF)
    low = iota((8, width), 0) < 4
    for i in range(chunks):
        grid_sum = jnp.dot(lhs[...], fine[i], preferred_element_type=F32)
        cos_a, sin_a = coarse[i, 0], coarse[i, 1]
        for f, p in [(i, j) for i in range(2) for j in range(2)]:
            start = (2 * f + p) * points
            real = grid_sum[start:start + points]
            imag = grid_sum[4 * points + start:5 * points + start]
            out_re = jnp.sum((real * cos_a + imag * sin_a).reshape(points // 8, 8, width), axis=0)
            out_im = jnp.sum((imag * cos_a - real * sin_a).reshape(points // 8, 8, width), axis=0)
            out_re = out_re + pltpu.roll(out_re, 4, 0)
            out_im = out_im + pltpu.roll(out_im, 4, 0)
            out = jnp.where(low, out_re, out_im).astype(BF)
            for copy in range(f_ref.shape[0]):
                f_ref[copy, f, i, p] = out


def row_kernel(quarter, rows_dev, row_ref, r_ref):
    sides, depth = r_ref.shape[:2]
    share_u = row_ref.shape[-1]
    row = iota((depth, share_u), 0)
    x = (row // (2 * rows_dev)) * rows_dev + row % rows_dev
    is_imag = row % (2 * rows_dev) >= rows_dev
    scale = 1.0 / math.sqrt(depth // 2)
    for side in range(sides):
        cos_x, sin_x = cos_sin(x * row_ref[side:side + 1], quarter, scale)
        r_ref[side, :, :share_u] = jnp.where(is_imag, sin_x, cos_x).astype(BF)
        r_ref[side, :, share_u:] = jnp.where(is_imag, cos_x, -sin_x).astype(BF)


def prepare_kernel(
    quarter, rows_dev, tile_count, cap, angle_ref, code_ref, power_ref, far_power_ref,
    w_ref, choose_ref, mark_ref, int_ref,
):
    core = lax.axis_index("row") % 2
    int_ref[core] = power_ref[0]
    int_ref[1 - core] = far_power_ref[...]
    points = code_ref.shape[0]
    slots, units = choose_ref.shape[1], mark_ref.shape[0]
    for i in range(angle_ref.shape[0]):
        w_ref[i] = fine_table(quarter, angle_ref[i])
    segs = points // rows_dev
    half = tile_count // 2
    mine = lax.axis_index("tile") // half
    point = iota((points, points), 1)
    point = (point % rows_dev) * segs + (point // rows_dev)
    source = iota((points, points), 0)
    spot = iota((slots, SEG), 1) - iota((slots, SEG), 0) % PACK
    marked = jnp.zeros((slots, SEG), jnp.int32)
    for side in range(2):
        code_col = code_ref[:, side:side + 1]
        code_row = jnp.sum(jnp.where(source == point, code_col, 0), axis=0, keepdims=True)
        owner_col, owner_row = code_col // points, code_row // points
        same = jnp.where((source < point) & (owner_col == owner_row), 1, 0)
        rank = jnp.sum(same, axis=0, keepdims=True)
        tile = owner_row % tile_count
        place = ((owner_row // tile_count) * half + tile % half) * cap + rank
        place = jnp.where(tile // half == mine, place, -1)
        hit = iota((slots, points), 0) == place
        choose_ref[side] = jnp.where(hit, 1.0, 0.0).astype(BF)
        marks = jnp.sum(jnp.where(hit, code_row % points + 1, 0), axis=1, keepdims=True)
        marked = jnp.where(spot == side * PACK, marks, marked)
    marked = jnp.sum(marked.reshape(units, PACK, SEG), axis=1, keepdims=True)
    marked = jnp.broadcast_to(marked, mark_ref.shape)
    mark_ref[...] = marked.astype(F32).astype(BF)


def middle_kernel(
    table, got_ref, target_ref, far_target_ref, weight_ref, far_weight_ref,
    power_hbm, back_ref, powers, fars, sems,
):
    devices, pols, rows, share_v = got_ref.shape
    depth = devices * rows
    share_u = table.shape[2] // 2
    core = lax.axis_index("row") % 2
    loads = [
        pltpu.make_async_copy(array.at[core], fars.at[i], sems.at[2 + i])
        for i, array in enumerate((far_target_ref, far_weight_ref))
    ]
    for load in loads:
        load.start()
    planes = [
        got_ref[:, p].astype(F32).reshape(depth, share_v).astype(BF) for p in range(pols)
    ]
    sums = [None, None]
    stores = []
    for side in range(2):
        mixed = [
            lax.dot_general(
                plane, table[side], (((0,), (0,)), ((), ())), preferred_element_type=F32
            )
            for plane in planes
        ]
        power = mixed[0] * mixed[0] + mixed[1] * mixed[1]
        intensity = power[:, :share_u] + power[:, share_u:]
        powers[side] = intensity
        stores.append(pltpu.make_async_copy(powers.at[side], power_hbm.at[side], sems.at[side]))
        stores[-1].start()
        if side == 0:
            goal, gain = target_ref[core], weight_ref[core]
        else:
            for load in loads:
                load.wait()
            goal, gain = fars[0], fars[1]
        factor = 4.0 * gain * (intensity - goal)
        factor = jnp.concatenate([factor, factor], axis=1)
        for p in range(pols):
            far_grad = (factor * mixed[p]).astype(BF)
            back = lax.dot_general(
                table[side], far_grad, (((1,), (1,)), ((), ())), preferred_element_type=F32
            )
            sums[p] = back if side == 0 else sums[p] + back
    groups, halves, count = back_ref.shape[:3]
    for p in range(pols):
        total = sums[p].reshape(groups, halves, count, rows, share_v).astype(BF)
        for half in range(halves):
            back_ref[:, half, :, 0, p] = total[:, half]
            back_ref[:, 1 - half, :, 1, p] = total[:, half]
    for store in stores:
        store.wait()


def adjoint_kernel(
    quarter, rows_dev, got_ref, w_ref, angle_ref, choose_ref, mark_ref, out_ref, total
):
    chunks, width = w_ref.shape[0], w_ref.shape[2]
    points = choose_ref.shape[2] // 2
    units = out_ref.shape[0]
    low = iota((8, width), 0) < 4
    for i in range(chunks):
        cos_a, sin_a = coarse_table(quarter, rows_dev, angle_ref[i])
        reals, imags = [], []
        for side, f, p in [(i, j, k) for i in range(2) for j in range(2) for k in range(2)]:
            plane = jnp.sum(got_ref[:, f, i, side, p].astype(F32), axis=0)
            other = pltpu.roll(plane, 4, 0)
            real = jnp.where(low, plane, other)
            imag = jnp.where(low, other, plane)
            real = jnp.broadcast_to(real[None], (points // 8, 8, width)).reshape(points, width)
            imag = jnp.broadcast_to(imag[None], (points // 8, 8, width)).reshape(points, width)
            reals.append((cos_a * real - sin_a * imag).astype(BF))
            imags.append((cos_a * imag + sin_a * real).astype(BF))
        found = lax.dot_general(
            jnp.concatenate(reals + imags, axis=0), w_ref[i], (((1,), (1,)), ((), ())),
            preferred_element_type=F32,
        )
        if i == 0:
            total[...] = found
        else:
            total[...] += found
    for side in range(2):
        left, right = [], []
        for fp in range(4):
            start = (4 * side + fp) * points
            real = total[start:start + points, :]
            imag = total[8 * points + start:9 * points + start, :]
            real_cos, real_sin, imag_cos, imag_sin = (
                real[:, :SEG], real[:, SEG:], imag[:, :SEG], imag[:, SEG:]
            )
            left += [(real_cos + imag_sin).astype(BF), (imag_cos - real_sin).astype(BF)]
            right += [(real_cos - imag_sin).astype(BF), (imag_cos + real_sin).astype(BF)]
        left = mirrored(jnp.concatenate(left, axis=0)).astype(BF)
        left = [left[i * points:(i + 1) * points] for i in range(8)]
        block = jnp.concatenate(
            [jnp.concatenate(left, axis=1), jnp.concatenate(right, axis=1)], axis=0
        )
        sent = jnp.dot(choose_ref[side], block, preferred_element_type=F32).astype(BF)
        sent = sent.reshape(units, PACK, 8 * SEG)
        for i in range(8):
            rows = pl.ds((8 * side + i) * PACK, PACK)
            out_ref[:, rows, :] = sent[:, :, i * SEG:(i + 1) * SEG]
    out_ref[:, 16 * PACK:, :] = mark_ref[...]


def faces_kernel(got_ref, out_hbm, out_ref, sems):
    faces = out_ref.shape[3]
    units = got_ref.shape[0]
    slots = units * PACK
    marks = got_ref[:, 16 * PACK:, :].astype(F32)
    fit = SEG // (2 * PACK)
    rows = []
    for i in range(0, units, fit):
        row = marks[i]
        for j in range(1, fit):
            row = row + pltpu.roll(marks[i + j], 2 * PACK * j, 1)
        rows.append(row)
    label = jnp.concatenate(rows, axis=1).astype(jnp.int32)
    face = iota((PACK // 2, 2 * slots), 0) + 1
    choose = jnp.concatenate(
        [
            jnp.where(face + i == label, 1.0, 0.0) for i in range(0, faces, PACK // 2)
        ],
        axis=0,
    ).astype(BF)
    stores = []
    for f, p in [(i, j) for i in range(2) for j in range(2)]:
        for c in range(2):
            blocks = []
            for side in range(2):
                rows = pl.ds((8 * side + 4 * f + 2 * p + c) * PACK, PACK)
                blocks.append(got_ref[:, rows, :])
            block = jnp.concatenate(blocks, axis=1).reshape(2 * slots, SEG)
            found = jnp.dot(choose, block, preferred_element_type=F32)
            out_ref[f, p, c] = found
            if p == 1:
                out_ref[f, 2, c] = -found
        places = [(0, 0), (0, 3)] if p == 0 else [(1, 1), (2, 2)]
        for source, k in places:
            stores.append(
                pltpu.make_async_copy(out_ref.at[f, source], out_hbm.at[f, k], sems.at[f, k])
            )
            stores[-1].start()
    for store in stores:
        store.wait()


def exchange_small(outgoing, groups, cap):
    units = outgoing.shape[0]
    peers = units * PACK // cap
    swap = functools.partial(
        lax.all_to_all, axis_name=BOTH, split_axis=1, concat_axis=1, tiled=True, axis_index_groups=groups
    )
    rows = outgoing[:, :16 * PACK].reshape(units, 16, PACK, SEG).transpose(1, 0, 2, 3)
    rows = swap(rows.reshape(16, peers, cap, SEG))
    rows = rows.reshape(16, units, PACK, SEG).transpose(1, 0, 2, 3).reshape(units, 16 * PACK, SEG)
    marks = outgoing[:, 16 * PACK, :2 * PACK].reshape(units, 2, PACK).transpose(1, 0, 2)
    marks = swap(marks.reshape(2, peers, cap)).reshape(2, units, PACK)
    marks = marks.transpose(1, 0, 2).reshape(units, 1, 2 * PACK)
    marks = jnp.pad(marks, ((0, 0), (0, 0), (0, SEG - 2 * PACK)))
    marks = jnp.broadcast_to(marks, (units, PACK // 2, SEG))
    return jnp.concatenate([rows, marks], axis=1)


VM = pl.BlockSpec(memory_space=pltpu.VMEM)


def params(mib=24):
    return pltpu.CompilerParams(
        dimension_semantics=("arbitrary",), vmem_limit_bytes=mib * 1024 * 1024
    )


def cost(flops, moved):
    return pl.CostEstimate(flops=int(flops), bytes_accessed=int(moved), transcendentals=0)


def whole(shape):
    return pl.BlockSpec(shape, lambda i: (0,) * len(shape))


def body(currents, row_angles, column_angles, target, weight, tile_owner, face_slot):
    row_count = lax.axis_size("row")
    tile_count = lax.axis_size("tile")
    devices = row_count * tile_count
    freq_count, comp_count, part_count, rows_dev, columns = currents.shape
    far_rows = row_angles.shape[0]
    far_cols = column_angles.shape[0]
    share_v = far_cols // tile_count
    share_u = far_rows // row_count
    chunks = far_cols // CHUNK
    tiles = columns // SEG
    points = rows_dev * tiles
    half = points // 2
    cap = 2 * points // devices
    slots = points
    units = slots // PACK
    held = 16 * PACK + PACK // 2
    pairs = row_count // 2
    wide = 2 * rows_dev
    depth = devices * wide
    tile_half = tile_count // 2
    half_groups = [
        [r * tile_count + side * tile_half + t for r in range(row_count) for t in range(tile_half)]
        for side in range(2)
    ]
    swap = [(i, i ^ 1) for i in range(row_count)]
    mirror = [(i, (i + tile_half) % tile_count) for i in range(tile_count)]
    angles = column_angles.reshape(chunks, 1, CHUNK)
    far_owner = lax.ppermute(tile_owner, "tile", mirror)
    far_slot = lax.ppermute(face_slot, "tile", mirror)
    cur = currents.reshape(freq_count, comp_count, part_count, rows_dev, tiles, SEG)
    cur = cur.transpose(0, 1, 2, 4, 3, 5).reshape(freq_count, comp_count, part_count, points, SEG)
    copies = pairs if share_v == CHUNK else 1
    plane = pl.pallas_call(
        functools.partial(forward_kernel, columns, rows_dev),
        grid=(1,),
        in_specs=[VM, pl.BlockSpec(memory_space=pltpu.HBM)],
        out_specs=whole((copies, 2, chunks, 2, wide, CHUNK)),
        out_shape=jax.ShapeDtypeStruct((copies, 2, chunks, 2, wide, CHUNK), BF),
        scratch_shapes=[
            pltpu.VMEM(cur.shape, BF),
            pltpu.VMEM((8 * half, 2 * SEG), BF),
            pltpu.VMEM((chunks, 2 * SEG, CHUNK), BF),
            pltpu.VMEM((chunks, 2, half, CHUNK), F32),
            pltpu.SemaphoreType.DMA((2, 4)),
        ],
        compiler_params=params(58),
        cost_estimate=cost(4.3e9, 1.6e6),
        name="columns",
    )(angles, cur)
    if share_v != CHUNK:
        plane = plane.reshape(2, chunks, 2, wide, CHUNK // share_v, share_v)
        plane = plane.transpose(0, 1, 4, 2, 3, 5).reshape(1, 2, tile_count, 2, wide, share_v)
        plane = jnp.broadcast_to(plane, (pairs,) + plane.shape[1:])
    plane = plane.reshape(devices, 2, wide, share_v)

    row_angles, aim, gain, plane = lax.optimization_barrier((row_angles, target, weight, plane))
    far_target = lax.ppermute(aim, "row", swap)
    far_weight = lax.ppermute(gain, "row", swap)
    got = lax.all_to_all(plane, BOTH, 0, 0, tiled=True)
    here = lax.axis_index("row")
    own_angles = jnp.stack(
        [lax.dynamic_slice_in_dim(row_angles, i * share_u, share_u) for i in (here, here ^ 1)]
    )
    row_table = pl.pallas_call(
        functools.partial(row_kernel, columns, rows_dev),
        grid=(1,),
        in_specs=[VM],
        out_specs=whole((2, depth, 2 * share_u)),
        out_shape=jax.ShapeDtypeStruct((2, depth, 2 * share_u), BF),
        compiler_params=params(),
        cost_estimate=cost(1e8, 5e5),
        name="rows",
    )(own_angles)
    far_shape = (share_v, share_u)
    spare = (56 << 20) // (4 * share_v * share_u)
    back_shape = (row_count, 2, tile_half, 2, 2, wide, share_v)
    powers, back = pl.pallas_call(
        middle_kernel,
        grid=(1,),
        in_specs=[VM, VM, VM, pl.BlockSpec(memory_space=pl.ANY), VM, pl.BlockSpec(memory_space=pl.ANY)],
        out_specs=[pl.BlockSpec(memory_space=pl.ANY), whole(back_shape)],
        out_shape=[
            jax.ShapeDtypeStruct((spare,) + far_shape, F32),
            jax.ShapeDtypeStruct(back_shape, BF),
        ],
        scratch_shapes=[
            pltpu.VMEM((2,) + far_shape, F32),
            pltpu.VMEM((2,) + far_shape, F32),
            pltpu.SemaphoreType.DMA((4,)),
        ],
        compiler_params=params(),
        cost_estimate=cost(1.1e9, 5e6),
        name="objective",
    )(row_table, got, target, far_target, weight, far_weight)

    owner, slot, far_owner, far_slot, angles, powers, back = lax.optimization_barrier(
        (tile_owner, face_slot, far_owner, far_slot, angles, powers, back)
    )
    far_power = lax.ppermute(powers[1], "row", swap)
    code = jnp.stack(
        [owner[:, 0] * points + slot, far_owner[:, 0] * points + far_slot], axis=1
    )
    back = back.reshape(devices, 2, 2, wide, share_v)
    back = lax.all_to_all(back, BOTH, 0, 0, tiled=True)
    table, choose, mark, intensity = pl.pallas_call(
        functools.partial(prepare_kernel, columns, rows_dev, tile_count, cap),
        grid=(1,),
        in_specs=[VM, VM, pl.BlockSpec((1,) + far_shape, lambda i: (0, 0, 0)), VM],
        out_specs=[
            whole((chunks, 2 * SEG, CHUNK)),
            whole((2, slots, points)),
            whole((units, PACK // 2, SEG)),
            whole(target.shape),
        ],
        out_shape=[
            jax.ShapeDtypeStruct((chunks, 2 * SEG, CHUNK), BF),
            jax.ShapeDtypeStruct((2, slots, points), BF),
            jax.ShapeDtypeStruct((units, PACK // 2, SEG), BF),
            jax.ShapeDtypeStruct(target.shape, F32),
        ],
        compiler_params=params(),
        cost_estimate=cost(1e9, 2e6),
        name="prepare",
    )(angles, code, powers, far_power)

    back = back.reshape(pairs, 2, tile_count, 2, 2, wide, share_v)
    if share_v != CHUNK:
        back = back.reshape(pairs, 2, chunks, CHUNK // share_v, 2, 2, wide, share_v)
        back = back.transpose(0, 1, 2, 4, 5, 6, 3, 7).reshape(pairs, 2, chunks, 2, 2, wide, CHUNK)
    outgoing = pl.pallas_call(
        functools.partial(adjoint_kernel, columns, rows_dev),
        grid=(1,),
        in_specs=[VM] * 5,
        out_specs=whole((units, held, SEG)),
        out_shape=jax.ShapeDtypeStruct((units, held, SEG), BF),
        scratch_shapes=[pltpu.VMEM((16 * half, 2 * SEG), F32)],
        compiler_params=params(),
        cost_estimate=cost(4.3e9, 4e6),
        name="adjoint",
    )(back, table, angles, choose, mark)

    if cap == PACK:
        arrived = lax.all_to_all(outgoing, BOTH, 0, 0, tiled=True, axis_index_groups=half_groups)
    else:
        arrived = exchange_small(outgoing, half_groups, cap)
    out_shape = (freq_count, comp_count, part_count, points, SEG)
    faces = pl.pallas_call(
        faces_kernel,
        grid=(1,),
        in_specs=[VM],
        out_specs=pl.BlockSpec(memory_space=pl.ANY),
        out_shape=jax.ShapeDtypeStruct(out_shape, F32),
        scratch_shapes=[
            pltpu.VMEM((freq_count, 3, part_count, points, SEG), F32),
            pltpu.SemaphoreType.DMA((2, 4)),
        ],
        compiler_params=params(),
        name="faces",
    )(arrived)
    return (intensity, faces)


def solution(mesh):
    in_specs = (
        P(None, None, None, ("row", "tile"), None),
        P(),
        P(),
        P(None, "tile", "row"),
        P(None, "tile", "row"),
        P(("row", "tile"), None),
        P(("row", "tile")),
    )
    out_specs = (P(None, "tile", "row"), P(None, None, None, ("row", "tile"), None))
    return jax.shard_map(body, mesh=mesh, in_specs=in_specs, out_specs=out_specs, check_vma=False)
```

```python
import functools
import math

import jax
import jax.numpy as jnp
from jax import lax
from jax.experimental import pallas as pl
from jax.experimental.pallas import tpu as pltpu
from jax.sharding import PartitionSpec as P

SEG = 128
CHUNK = 256
PACK = 16
SPAN = 4
BOTH = ("row", "tile")
BF = jnp.bfloat16
F32 = jnp.float32


def cos_sin(turns, quarter, scale):
    bits = int(math.log2(quarter))
    turns = turns & (4 * quarter - 1)
    octant = (turns + quarter // 2) >> bits
    angle = (turns - (octant << bits)).astype(F32) * (math.pi / (2 * quarter))
    square = angle * angle
    sin_part = angle * scale + (angle * scale) * square * (
        -1.6666654611e-1 + square * (8.3321608736e-3 - square * 1.9515295891e-4)
    )
    cos_part = scale - square * (0.5 * scale) + (square * scale) * square * (
        4.166664568298827e-2 + square * (-1.388731625493765e-3 + square * 2.443315711809948e-5)
    )
    swap = (octant & 1) == 1
    cos_out = jnp.where(swap, sin_part, cos_part)
    sin_out = jnp.where(swap, cos_part, sin_part)
    cos_out = jnp.where(((octant + 1) & 2) == 2, -cos_out, cos_out)
    sin_out = jnp.where((octant & 2) == 2, -sin_out, sin_out)
    return cos_out, sin_out


def iota(shape, dim):
    return lax.broadcasted_iota(jnp.int32, shape, dim)


def turned(cos_0, sin_0, cos_1, sin_1):
    rows, width = cos_0.shape
    cos_out, sin_out = [], []
    for j in range(cos_1.shape[0]):
        cos_j = jnp.broadcast_to(cos_1[j:j + 1], (rows, width))
        sin_j = jnp.broadcast_to(sin_1[j:j + 1], (rows, width))
        cos_out.append(cos_0 * cos_j - sin_0 * sin_j)
        sin_out.append(sin_0 * cos_j + cos_0 * sin_j)
    return jnp.concatenate(cos_out, axis=0), jnp.concatenate(sin_out, axis=0)


def middle(quarter):
    return quarter // 2 + SEG - 1


def fine_table(quarter, angles):
    width = angles.shape[-1]
    start = quarter - middle(quarter) + iota((SEG // 8, width), 0) * 16
    cos_0, sin_0 = cos_sin(2 * iota((8, width), 0) * angles, 2 * quarter, 1.0 / math.sqrt(quarter))
    cos_1, sin_1 = cos_sin(start * angles, 2 * quarter, 1.0)
    return jnp.concatenate(turned(cos_0, sin_0, cos_1, sin_1), axis=0).astype(BF)


def coarse_table(quarter, rows_dev, angles):
    width = angles.shape[-1]
    tiles = quarter // SEG // 2
    group = 8 // rows_dev
    base = (iota((8, width), 0) // rows_dev) * (2 * SEG)
    start = iota((tiles // group, width), 0) * (2 * group * SEG) + middle(quarter)
    cos_0, sin_0 = cos_sin(base * angles, 2 * quarter, 1.0)
    cos_1, sin_1 = cos_sin(start * angles, 2 * quarter, 1.0)
    return turned(cos_0, sin_0, cos_1, sin_1)


def mirrored(block):
    flip = jnp.where(iota((SEG, SEG), 0) + iota((SEG, SEG), 1) == SEG - 1, 1.0, 0.0).astype(BF)
    return jnp.dot(block, flip, preferred_element_type=F32)


def forward_kernel(
    quarter, rows_dev, angle_ref, cur_hbm, f_hbm, f_ref, cur_ref, lhs, fine, coarse, sem, out_sem
):
    points = rows_dev * quarter // SEG // 2
    chunks, width = angle_ref.shape[0], angle_ref.shape[-1]
    loads = [
        [pltpu.make_async_copy(cur_hbm.at[f, k], cur_ref.at[f, k], sem.at[f, k]) for k in range(4)]
        for f in range(2)
    ]
    for load in loads[0] + loads[1]:
        load.start()
    for i in range(chunks):
        fine[i] = fine_table(quarter, angle_ref[i])
        coarse[i, 0], coarse[i, 1] = coarse_table(quarter, rows_dev, angle_ref[i])
    low_half, high_half = pl.ds(0, points), pl.ds(points, points)
    for f in range(2):
        for load in loads[f]:
            load.wait()
        even, odd = [], []
        for c in range(2):
            right = [cur_ref[f, k, c, high_half, :].astype(F32) for k in range(4)]
            left = [mirrored(cur_ref[f, k, c, low_half, :]) for k in range(4)]
            right = [right[0] + right[3], right[1] - right[2]]
            left = [left[0] + left[3], left[1] - left[2]]
            even.append([i + j for i, j in zip(right, left)])
            odd.append([i - j for i, j in zip(right, left)])
        for p in range(2):
            real = pl.ds((2 * f + p) * points, points)
            imag = pl.ds((4 + 2 * f + p) * points, points)
            lhs[real, :SEG] = even[0][p].astype(BF)
            lhs[real, SEG:] = odd[1][p].astype(BF)
            lhs[imag, :SEG] = even[1][p].astype(BF)
            lhs[imag, SEG:] = (-odd[0][p]).astype(BF)
    low = iota((8, width), 0) < 4
    stores = []
    for i in range(chunks):
        grid_sum = jnp.dot(lhs[...], fine[i], preferred_element_type=F32)
        cos_a, sin_a = coarse[i, 0], coarse[i, 1]
        for f, p in [(i, j) for i in range(2) for j in range(2)]:
            start = (2 * f + p) * points
            real = grid_sum[start:start + points]
            imag = grid_sum[4 * points + start:5 * points + start]
            out_re = jnp.sum((real * cos_a + imag * sin_a).reshape(points // 8, 8, width), axis=0)
            out_im = jnp.sum((imag * cos_a - real * sin_a).reshape(points // 8, 8, width), axis=0)
            out_re = out_re + pltpu.roll(out_re, 4, 0)
            out_im = out_im + pltpu.roll(out_im, 4, 0)
            out = jnp.where(low, out_re, out_im).astype(BF)
            for copy in range(f_ref.shape[0]):
                f_ref[copy, f, i, p] = out
        stores.append(
            pltpu.make_async_copy(f_ref.at[:, :, i], f_hbm.at[:, :, i], out_sem.at[i])
        )
        stores[-1].start()
    for store in stores:
        store.wait()


def row_kernel(quarter, rows_dev, row_ref, r_ref):
    sides, depth = r_ref.shape[:2]
    share_u = row_ref.shape[-1]
    row = iota((depth, share_u), 0)
    x = (row // (2 * rows_dev)) * rows_dev + row % rows_dev
    is_imag = row % (2 * rows_dev) >= rows_dev
    scale = 1.0 / math.sqrt(depth // 2)
    for side in range(sides):
        cos_x, sin_x = cos_sin(x * row_ref[side:side + 1], quarter, scale)
        r_ref[side, :, :share_u] = jnp.where(is_imag, sin_x, cos_x).astype(BF)
        r_ref[side, :, share_u:] = jnp.where(is_imag, cos_x, -sin_x).astype(BF)


def prepare_kernel(
    quarter, rows_dev, tile_count, cap, angle_ref, code_ref, power_ref, far_power_ref,
    w_ref, choose_ref, mark_ref, int_ref,
):
    core = lax.axis_index("row") % 2
    int_ref[core] = power_ref[0]
    int_ref[1 - core] = far_power_ref[...]
    points = code_ref.shape[0]
    slots, units = choose_ref.shape[1], mark_ref.shape[0]
    for i in range(angle_ref.shape[0]):
        w_ref[i] = fine_table(quarter, angle_ref[i])
    segs = points // rows_dev
    half = tile_count // 2
    mine = lax.axis_index("tile") // half
    point = iota((points, points), 1)
    point = (point % rows_dev) * segs + (point // rows_dev)
    source = iota((points, points), 0)
    spot = iota((slots, SEG), 1) - iota((slots, SEG), 0) % PACK
    marked = jnp.zeros((slots, SEG), jnp.int32)
    for side in range(2):
        code_col = code_ref[:, side:side + 1]
        code_row = jnp.sum(jnp.where(source == point, code_col, 0), axis=0, keepdims=True)
        owner_col, owner_row = code_col // points, code_row // points
        same = jnp.where((source < point) & (owner_col == owner_row), 1, 0)
        rank = jnp.sum(same, axis=0, keepdims=True)
        tile = owner_row % tile_count
        place = ((owner_row // tile_count) * half + tile % half) * cap + rank
        place = jnp.where(tile // half == mine, place, -1)
        hit = iota((slots, points), 0) == place
        choose_ref[side] = jnp.where(hit, 1.0, 0.0).astype(BF)
        marks = jnp.sum(jnp.where(hit, code_row % points + 1, 0), axis=1, keepdims=True)
        marked = jnp.where(spot == side * PACK, marks, marked)
    marked = jnp.sum(marked.reshape(units, PACK, SEG), axis=1, keepdims=True)
    marked = jnp.broadcast_to(marked, mark_ref.shape)
    mark_ref[...] = marked.astype(F32).astype(BF)


def middle_kernel(
    table, got_ref, target_ref, far_target_ref, weight_ref, far_weight_ref,
    power_hbm, back_ref, powers, fars, sems,
):
    devices, pols, rows, share_v = got_ref.shape
    depth = devices * rows
    share_u = table.shape[2] // 2
    core = lax.axis_index("row") % 2
    loads = [
        pltpu.make_async_copy(array.at[core], fars.at[i], sems.at[2 + i])
        for i, array in enumerate((far_target_ref, far_weight_ref))
    ]
    for load in loads:
        load.start()
    planes = [
        got_ref[:, p].astype(F32).reshape(depth, share_v).astype(BF) for p in range(pols)
    ]
    sums = [None, None]
    stores = []
    for side in range(2):
        mixed = [
            lax.dot_general(
                plane, table[side], (((0,), (0,)), ((), ())), preferred_element_type=F32
            )
            for plane in planes
        ]
        power = mixed[0] * mixed[0] + mixed[1] * mixed[1]
        intensity = power[:, :share_u] + power[:, share_u:]
        powers[side] = intensity
        stores.append(pltpu.make_async_copy(powers.at[side], power_hbm.at[side], sems.at[side]))
        stores[-1].start()
        if side == 0:
            goal, gain = target_ref[core], weight_ref[core]
        else:
            for load in loads:
                load.wait()
            goal, gain = fars[0], fars[1]
        factor = 4.0 * gain * (intensity - goal)
        factor = jnp.concatenate([factor, factor], axis=1)
        for p in range(pols):
            far_grad = (factor * mixed[p]).astype(BF)
            back = lax.dot_general(
                table[side], far_grad, (((1,), (1,)), ((), ())), preferred_element_type=F32
            )
            sums[p] = back if side == 0 else sums[p] + back
    groups, halves, count = back_ref.shape[:3]
    for p in range(pols):
        total = sums[p].reshape(groups, halves, count, rows, share_v).astype(BF)
        for half in range(halves):
            back_ref[:, half, :, 0, p] = total[:, half]
            back_ref[:, 1 - half, :, 1, p] = total[:, half]
    for store in stores:
        store.wait()


def adjoint_kernel(
    quarter, rows_dev, got_ref, w_ref, angle_ref, choose_ref, mark_ref, out_ref, total
):
    chunks, width = w_ref.shape[0], w_ref.shape[2]
    points = choose_ref.shape[2] // 2
    units = out_ref.shape[0]
    low = iota((8, width), 0) < 4
    for i in range(chunks):
        cos_a, sin_a = coarse_table(quarter, rows_dev, angle_ref[i])
        reals, imags = [], []
        for side, f, p in [(i, j, k) for i in range(2) for j in range(2) for k in range(2)]:
            plane = jnp.sum(got_ref[:, f, i, side, p].astype(F32), axis=0)
            other = pltpu.roll(plane, 4, 0)
            real = jnp.where(low, plane, other)
            imag = jnp.where(low, other, plane)
            real = jnp.broadcast_to(real[None], (points // 8, 8, width)).reshape(points, width)
            imag = jnp.broadcast_to(imag[None], (points // 8, 8, width)).reshape(points, width)
            reals.append((cos_a * real - sin_a * imag).astype(BF))
            imags.append((cos_a * imag + sin_a * real).astype(BF))
        found = lax.dot_general(
            jnp.concatenate(reals + imags, axis=0), w_ref[i], (((1,), (1,)), ((), ())),
            preferred_element_type=F32,
        )
        if i == 0:
            total[...] = found
        else:
            total[...] += found
    for side in range(2):
        left, right = [], []
        for fp in range(4):
            start = (4 * side + fp) * points
            real = total[start:start + points, :]
            imag = total[8 * points + start:9 * points + start, :]
            real_cos, real_sin, imag_cos, imag_sin = (
                real[:, :SEG], real[:, SEG:], imag[:, :SEG], imag[:, SEG:]
            )
            left += [(real_cos + imag_sin).astype(BF), (imag_cos - real_sin).astype(BF)]
            right += [(real_cos - imag_sin).astype(BF), (imag_cos + real_sin).astype(BF)]
        left = mirrored(jnp.concatenate(left, axis=0)).astype(BF)
        left = [left[i * points:(i + 1) * points] for i in range(8)]
        block = jnp.concatenate(
            [jnp.concatenate(left, axis=1), jnp.concatenate(right, axis=1)], axis=0
        )
        sent = jnp.dot(choose_ref[side], block, preferred_element_type=F32).astype(BF)
        sent = sent.reshape(units, PACK, 8 * SEG)
        for i in range(8):
            rows = pl.ds((8 * side + i) * PACK, PACK)
            out_ref[:, rows, :] = sent[:, :, i * SEG:(i + 1) * SEG]
    out_ref[:, 16 * PACK:, :] = mark_ref[...]


def faces_kernel(got_ref, out_hbm, out_ref, sems):
    faces = out_ref.shape[3]
    units = got_ref.shape[0]
    slots = units * PACK
    marks = got_ref[:, 16 * PACK:, :].astype(F32)
    fit = SEG // (2 * PACK)
    rows = []
    for i in range(0, units, fit):
        row = marks[i]
        for j in range(1, fit):
            row = row + pltpu.roll(marks[i + j], 2 * PACK * j, 1)
        rows.append(row)
    label = jnp.concatenate(rows, axis=1).astype(jnp.int32)
    face = iota((PACK // 2, 2 * slots), 0) + 1
    choose = jnp.concatenate(
        [
            jnp.where(face + i == label, 1.0, 0.0) for i in range(0, faces, PACK // 2)
        ],
        axis=0,
    ).astype(BF)
    stores = []
    for first in range(0, 8, SPAN):
        blocks = []
        for i in range(first, first + SPAN):
            pair = [got_ref[:, pl.ds((8 * side + i) * PACK, PACK), :] for side in range(2)]
            blocks.append(jnp.concatenate(pair, axis=1).reshape(2 * slots, SEG))
        found = jnp.dot(choose, jnp.concatenate(blocks, axis=1), preferred_element_type=F32)
        for i in range(first, first + SPAN):
            f, p, c = i // 4, i // 2 % 2, i % 2
            piece = found[:, (i - first) * SEG:(i - first + 1) * SEG]
            out_ref[f, p, c] = piece
            if p == 1:
                out_ref[f, 2, c] = -piece
            if c == 0:
                continue
            places = [(0, 0), (0, 3)] if p == 0 else [(1, 1), (2, 2)]
            for source, k in places:
                stores.append(
                    pltpu.make_async_copy(out_ref.at[f, source], out_hbm.at[f, k], sems.at[f, k])
                )
                stores[-1].start()
    for store in stores:
        store.wait()


def exchange_small(outgoing, groups, cap):
    units = outgoing.shape[0]
    peers = units * PACK // cap
    swap = functools.partial(
        lax.all_to_all, axis_name=BOTH, split_axis=1, concat_axis=1, tiled=True, axis_index_groups=groups
    )
    rows = outgoing[:, :16 * PACK].reshape(units, 16, PACK, SEG).transpose(1, 0, 2, 3)
    rows = swap(rows.reshape(16, peers, cap, SEG))
    rows = rows.reshape(16, units, PACK, SEG).transpose(1, 0, 2, 3).reshape(units, 16 * PACK, SEG)
    marks = outgoing[:, 16 * PACK, :2 * PACK].reshape(units, 2, PACK).transpose(1, 0, 2)
    marks = swap(marks.reshape(2, peers, cap)).reshape(2, units, PACK)
    marks = marks.transpose(1, 0, 2).reshape(units, 1, 2 * PACK)
    marks = jnp.pad(marks, ((0, 0), (0, 0), (0, SEG - 2 * PACK)))
    marks = jnp.broadcast_to(marks, (units, PACK // 2, SEG))
    return jnp.concatenate([rows, marks], axis=1)


VM = pl.BlockSpec(memory_space=pltpu.VMEM)


def params(mib=24):
    return pltpu.CompilerParams(
        dimension_semantics=("arbitrary",), vmem_limit_bytes=mib * 1024 * 1024
    )


def cost(flops, moved):
    return pl.CostEstimate(flops=int(flops), bytes_accessed=int(moved), transcendentals=0)


def whole(shape):
    return pl.BlockSpec(shape, lambda i: (0,) * len(shape))


def body(currents, row_angles, column_angles, target, weight, tile_owner, face_slot):
    row_count = lax.axis_size("row")
    tile_count = lax.axis_size("tile")
    devices = row_count * tile_count
    freq_count, comp_count, part_count, rows_dev, columns = currents.shape
    far_rows = row_angles.shape[0]
    far_cols = column_angles.shape[0]
    share_v = far_cols // tile_count
    share_u = far_rows // row_count
    chunks = far_cols // CHUNK
    tiles = columns // SEG
    points = rows_dev * tiles
    half = points // 2
    cap = 2 * points // devices
    slots = points
    units = slots // PACK
    held = 16 * PACK + PACK // 2
    pairs = row_count // 2
    wide = 2 * rows_dev
    depth = devices * wide
    tile_half = tile_count // 2
    half_groups = [
        [r * tile_count + side * tile_half + t for r in range(row_count) for t in range(tile_half)]
        for side in range(2)
    ]
    swap = [(i, i ^ 1) for i in range(row_count)]
    mirror = [(i, (i + tile_half) % tile_count) for i in range(tile_count)]
    angles = column_angles.reshape(chunks, 1, CHUNK)
    far_owner = lax.ppermute(tile_owner, "tile", mirror)
    far_slot = lax.ppermute(face_slot, "tile", mirror)
    cur = currents.reshape(freq_count, comp_count, part_count, rows_dev, tiles, SEG)
    cur = cur.transpose(0, 1, 2, 4, 3, 5).reshape(freq_count, comp_count, part_count, points, SEG)
    copies = pairs if share_v == CHUNK else 1
    plane = pl.pallas_call(
        functools.partial(forward_kernel, columns, rows_dev),
        grid=(1,),
        in_specs=[VM, pl.BlockSpec(memory_space=pltpu.HBM)],
        out_specs=pl.BlockSpec(memory_space=pl.ANY),
        out_shape=jax.ShapeDtypeStruct((copies, 2, chunks, 2, wide, CHUNK), BF),
        scratch_shapes=[
            pltpu.VMEM((copies, 2, chunks, 2, wide, CHUNK), BF),
            pltpu.VMEM(cur.shape, BF),
            pltpu.VMEM((8 * half, 2 * SEG), BF),
            pltpu.VMEM((chunks, 2 * SEG, CHUNK), BF),
            pltpu.VMEM((chunks, 2, half, CHUNK), F32),
            pltpu.SemaphoreType.DMA((2, 4)),
            pltpu.SemaphoreType.DMA((chunks,)),
        ],
        compiler_params=params(58),
        cost_estimate=cost(4.3e9, 1.6e6),
        name="columns",
    )(angles, cur)
    if share_v != CHUNK:
        plane = plane.reshape(2, chunks, 2, wide, CHUNK // share_v, share_v)
        plane = plane.transpose(0, 1, 4, 2, 3, 5).reshape(1, 2, tile_count, 2, wide, share_v)
        plane = jnp.broadcast_to(plane, (pairs,) + plane.shape[1:])
    plane = plane.reshape(devices, 2, wide, share_v)

    row_angles, aim, gain, plane = lax.optimization_barrier((row_angles, target, weight, plane))
    far_target = lax.ppermute(aim, "row", swap)
    far_weight = lax.ppermute(gain, "row", swap)
    got = lax.all_to_all(plane, BOTH, 0, 0, tiled=True)
    here = lax.axis_index("row")
    own_angles = jnp.stack(
        [lax.dynamic_slice_in_dim(row_angles, i * share_u, share_u) for i in (here, here ^ 1)]
    )
    row_table = pl.pallas_call(
        functools.partial(row_kernel, columns, rows_dev),
        grid=(1,),
        in_specs=[VM],
        out_specs=whole((2, depth, 2 * share_u)),
        out_shape=jax.ShapeDtypeStruct((2, depth, 2 * share_u), BF),
        compiler_params=params(),
        cost_estimate=cost(1e8, 5e5),
        name="rows",
    )(own_angles)
    far_shape = (share_v, share_u)
    spare = (56 << 20) // (4 * share_v * share_u)
    back_shape = (row_count, 2, tile_half, 2, 2, wide, share_v)
    powers, back = pl.pallas_call(
        middle_kernel,
        grid=(1,),
        in_specs=[VM, VM, VM, pl.BlockSpec(memory_space=pl.ANY), VM, pl.BlockSpec(memory_space=pl.ANY)],
        out_specs=[pl.BlockSpec(memory_space=pl.ANY), whole(back_shape)],
        out_shape=[
            jax.ShapeDtypeStruct((spare,) + far_shape, F32),
            jax.ShapeDtypeStruct(back_shape, BF),
        ],
        scratch_shapes=[
            pltpu.VMEM((2,) + far_shape, F32),
            pltpu.VMEM((2,) + far_shape, F32),
            pltpu.SemaphoreType.DMA((4,)),
        ],
        compiler_params=params(),
        cost_estimate=cost(1.1e9, 5e6),
        name="objective",
    )(row_table, got, target, far_target, weight, far_weight)

    owner, slot, far_owner, far_slot, angles, powers, back = lax.optimization_barrier(
        (tile_owner, face_slot, far_owner, far_slot, angles, powers, back)
    )
    far_power = lax.ppermute(powers[1], "row", swap)
    code = jnp.stack(
        [owner[:, 0] * points + slot, far_owner[:, 0] * points + far_slot], axis=1
    )
    back = back.reshape(devices, 2, 2, wide, share_v)
    back = lax.all_to_all(back, BOTH, 0, 0, tiled=True)
    table, choose, mark, intensity = pl.pallas_call(
        functools.partial(prepare_kernel, columns, rows_dev, tile_count, cap),
        grid=(1,),
        in_specs=[VM, VM, pl.BlockSpec((1,) + far_shape, lambda i: (0, 0, 0)), VM],
        out_specs=[
            whole((chunks, 2 * SEG, CHUNK)),
            whole((2, slots, points)),
            whole((units, PACK // 2, SEG)),
            whole(target.shape),
        ],
        out_shape=[
            jax.ShapeDtypeStruct((chunks, 2 * SEG, CHUNK), BF),
            jax.ShapeDtypeStruct((2, slots, points), BF),
            jax.ShapeDtypeStruct((units, PACK // 2, SEG), BF),
            jax.ShapeDtypeStruct(target.shape, F32),
        ],
        compiler_params=params(),
        cost_estimate=cost(1e9, 2e6),
        name="prepare",
    )(angles, code, powers, far_power)

    back = back.reshape(pairs, 2, tile_count, 2, 2, wide, share_v)
    if share_v != CHUNK:
        back = back.reshape(pairs, 2, chunks, CHUNK // share_v, 2, 2, wide, share_v)
        back = back.transpose(0, 1, 2, 4, 5, 6, 3, 7).reshape(pairs, 2, chunks, 2, 2, wide, CHUNK)
    outgoing = pl.pallas_call(
        functools.partial(adjoint_kernel, columns, rows_dev),
        grid=(1,),
        in_specs=[VM] * 5,
        out_specs=whole((units, held, SEG)),
        out_shape=jax.ShapeDtypeStruct((units, held, SEG), BF),
        scratch_shapes=[pltpu.VMEM((16 * half, 2 * SEG), F32)],
        compiler_params=params(),
        cost_estimate=cost(4.3e9, 4e6),
        name="adjoint",
    )(back, table, angles, choose, mark)

    if cap == PACK:
        arrived = lax.all_to_all(outgoing, BOTH, 0, 0, tiled=True, axis_index_groups=half_groups)
    else:
        arrived = exchange_small(outgoing, half_groups, cap)
    out_shape = (freq_count, comp_count, part_count, points, SEG)
    faces = pl.pallas_call(
        faces_kernel,
        grid=(1,),
        in_specs=[VM],
        out_specs=pl.BlockSpec(memory_space=pl.ANY),
        out_shape=jax.ShapeDtypeStruct(out_shape, F32),
        scratch_shapes=[
            pltpu.VMEM((freq_count, 3, part_count, points, SEG), F32),
            pltpu.SemaphoreType.DMA((2, 4)),
        ],
        compiler_params=params(),
        name="faces",
    )(arrived)
    return (intensity, faces)


def solution(mesh):
    in_specs = (
        P(None, None, None, ("row", "tile"), None),
        P(),
        P(),
        P(None, "tile", "row"),
        P(None, "tile", "row"),
        P(("row", "tile"), None),
        P(("row", "tile")),
    )
    out_specs = (P(None, "tile", "row"), P(None, None, None, ("row", "tile"), None))
    return jax.shard_map(body, mesh=mesh, in_specs=in_specs, out_specs=out_specs, check_vma=False)
```
